32 devices in a mesh: dp: 4 (over z), seq: 8 (over y, x, core).
Axes of the slice: x: 2, y: 2, z: 4, core: 2. Of those that a mesh axis runs over, the one named last changes fastest.
Arguments:
- states: bfloat16 [4, 2048, 768], P('dp', 'seq'), may hold values from -6 to 6
- segment_ids: int32 [4, 2048], P('dp', 'seq'), may hold values from 0 to 7, as said below
- project_weight: bfloat16 [2, 768, 2304], P(None, ('dp', 'seq')), may hold values from -0.3125 to 0.3125
- query_bias: bfloat16 [2, 768], P(None, ('dp', 'seq')), may hold values from -4 to 4
- value_bias: bfloat16 [2, 768], P(None, ('dp', 'seq')), may hold values from -1.5 to 1.5
- output_weight: bfloat16 [2, 768, 768], P(None, ('dp', 'seq')), may hold values from -1.75 to 1.75
- output_bias: bfloat16 [2, 768], P(None, ('dp', 'seq')), may hold values from -4 to 4
- attention_gain: bfloat16 [2, 768], P(None, ('dp', 'seq')), may hold values from 0.5 to 1.5
- attention_shift: bfloat16 [2, 768], P(None, ('dp', 'seq')), may hold values from -4 to 4
- up_weight: bfloat16 [2, 768, 3072], P(None, ('dp', 'seq')), may hold values from -0.21875 to 0.21875
- up_bias: bfloat16 [2, 3072], P(None, ('dp', 'seq')), may hold values from -6 to 6
- down_weight: bfloat16 [2, 3072, 768], P(None, ('dp', 'seq')), may hold values from -0.109375 to 0.109375
- down_bias: bfloat16 [2, 768], P(None, ('dp', 'seq')), may hold values from -4 to 4
- feed_gain: bfloat16 [2, 768], P(None, ('dp', 'seq')), may hold values from 0.5 to 1.5
- feed_shift: bfloat16 [2, 768], P(None, ('dp', 'seq')), may hold values from -4 to 4
- cotangent: bfloat16 [4, 2048, 768], P('dp', 'seq'), may hold values from -6 to 6
Outputs:
- output: bfloat16 [4, 2048, 768], P('dp', 'seq')
- input_grad: float32 [4, 2048, 768], P('dp', 'seq')
- grad_project_weight: float32 [2, 768, 2304], P(None, 'seq')
- grad_query_bias: float32 [2, 768], P(None, 'seq')
- grad_value_bias: float32 [2, 768], P(None, 'seq')
- grad_output_weight: float32 [2, 768, 768], P(None, 'seq')
- grad_output_bias: float32 [2, 768], P(None, 'seq')
- grad_attention_gain: float32 [2, 768], P(None, 'seq')
- grad_attention_shift: float32 [2, 768], P(None, 'seq')
- grad_up_weight: float32 [2, 768, 3072], P(None, 'seq')
- grad_up_bias: float32 [2, 3072], P(None, 'seq')
- grad_down_weight: float32 [2, 3072, 768], P(None, 'seq')
- grad_down_bias: float32 [2, 768], P(None, 'seq')
- grad_feed_gain: float32 [2, 768], P(None, 'seq')
- grad_feed_shift: float32 [2, 768], P(None, 'seq')
The draws below stay inside these ranges and needn't reach their ends.
Inputs may be any that keep to these rules, and one draw needn't show every extreme that they name: `segment_ids`: within each sequence the ids never fall and run over 0 .. 7; each document holds 60 to 800 tokens and one holds exactly 800.
All inputs are finite; a program needn't handle non-finite values.
Results may differ from the reference program's by a relative error of at most 0.035.
Values may be sent and summed in bfloat16 or wider, within the bound.
No kernel may reach another device: no remote copies, remote signals or barrier semaphores. Data moves between devices by JAX's collectives and lax.ppermute only.
A program may use at most 192 MiB of HBM per device.

```python
from functools import partial
import jax
import jax.numpy as jnp
from jax import lax

D = 768
HEADS = 12
HEAD_DIM = 64
FF = 3072
LAYERS = 2
LENGTH = 2048
BATCH = 4
DOC_MOST = 800
DOC_LEAST = 60
DOCS = 8


def segment_row(row_key):
    first_key, second_key = jax.random.split(row_key, 2)
    weights = jax.random.randint(first_key, (DOCS - 1,), 1, 5).astype(jnp.int32)
    extra = LENGTH - DOC_MOST - (DOCS - 1) * DOC_LEAST
    shares = extra * weights // jnp.sum(weights)
    leftover = extra - jnp.sum(shares)
    shares = jnp.concatenate([shares[:-1], shares[-1:] + leftover])
    others = DOC_LEAST + shares
    lengths = jnp.concatenate([jnp.full((1,), DOC_MOST, jnp.int32), others.astype(jnp.int32)])
    order = jax.random.permutation(second_key, DOCS)
    lengths = lengths[order]
    ends = jnp.cumsum(lengths).astype(jnp.int32)
    position = jnp.arange(LENGTH, dtype=jnp.int32)
    return jnp.sum((position[:, None] >= ends[None, :-1]).astype(jnp.int32), axis=1).astype(jnp.int32)


def draw_segment_ids(key, part):
    row_keys = jax.random.split(jax.random.fold_in(key, 17), BATCH)
    return jax.vmap(segment_row)(row_keys)


def levels(rng, dims, cuts, smallest, high):
    loudness, own = 1.0, jax.random.fold_in(rng, 6)
    for dim, parts in cuts:
        draws = jnp.exp(jax.random.uniform(jax.random.fold_in(own, dim), (parts,), jnp.float32, smallest / len(cuts), high / len(cuts)))
        loudness = loudness * jnp.repeat(draws, dims[dim] // parts).reshape([-1 if axis == dim else 1 for axis in range(len(dims))])
    return loudness


def bell_draw(own_key, extent, width, reach, pieces=(), kind=jnp.bfloat16):
    array = jax.random.normal(own_key, extent, jnp.float32) * width
    if len(pieces) > 0:
        array = levels(own_key, extent, pieces, -0.22, 0.18) * array
    return jnp.clip(array, min=-reach, max=reach).astype(kind)


def setup_inputs(seed: int = 0) -> dict:
    splits = jax.random.split(jax.random.key(seed), 17)
    return {
        "states": bell_draw(splits[0], (BATCH, LENGTH, D), 1.0, 6.0, ((0, 4), (1, 8))),
        "segment_ids": draw_segment_ids(jax.random.fold_in(splits[16], 71), 0),
        "project_weight": bell_draw(splits[2], (LAYERS, D, 3 * D), (D // 2) ** -0.5, 0.3125, ((1, 32),)),
        "query_bias": bell_draw(splits[3], (LAYERS, D), 0.3, 4.0, ((1, 32),)),
        "value_bias": bell_draw(splits[4], (LAYERS, D), 0.1, 1.5, ((1, 32),)),
        "output_weight": bell_draw(splits[5], (LAYERS, D, D), (D // 64) ** -0.5, 1.75, ((1, 32),)),
        "output_bias": bell_draw(splits[6], (LAYERS, D), 0.3, 4.0, ((1, 32),)),
        "attention_gain": jnp.clip(1.0 + 0.1 * jax.random.normal(splits[7], (LAYERS, D), jnp.float32), 0.5, 1.5).astype(jnp.bfloat16),
        "attention_shift": bell_draw(splits[8], (LAYERS, D), 0.3, 4.0, ((1, 32),)),
        "up_weight": bell_draw(splits[9], (LAYERS, D, FF), D ** -0.5, 0.21875, ((1, 32),)),
        "up_bias": bell_draw(splits[10], (LAYERS, FF), 0.5, 6.0, ((1, 32),)),
        "down_weight": bell_draw(splits[11], (LAYERS, FF, D), FF ** -0.5, 0.109375, ((1, 32),)),
        "down_bias": bell_draw(splits[12], (LAYERS, D), 0.3, 4.0, ((1, 32),)),
        "feed_gain": jnp.clip(1.0 + 0.1 * jax.random.normal(splits[13], (LAYERS, D), jnp.float32), 0.5, 1.5).astype(jnp.bfloat16),
        "feed_shift": bell_draw(splits[14], (LAYERS, D), 0.3, 4.0, ((1, 32),)),
        "cotangent": bell_draw(splits[15], (BATCH, LENGTH, D), 1.0, 6.0, ((0, 4), (1, 8))),
    }


MASKED_SCORE = -1000000000.0
EPSILON = 1e-12

@jax.custom_vjp
def low(v):
    return lax.optimization_barrier(v.astype(jnp.bfloat16)).astype(jnp.float32)

@jax.custom_vjp
def low_back(v):
    return v

def low_keep(v):
    return (low(v), None)

def low_pass(kept, grad):
    return (grad,)

def back_keep(v):
    return (v, None)

def back_low(kept, grad):
    return (low(grad),)
low.defvjp(low_keep, low_pass)
low_back.defvjp(back_keep, back_low)

def layer_norm(rows, gain, shift):
    centre = rows - lax.optimization_barrier(jnp.mean(rows, axis=-1, keepdims=True))
    spread = lax.optimization_barrier(jnp.mean(centre * centre, axis=-1, keepdims=True))
    return centre * lax.rsqrt(spread + EPSILON) * gain + shift

def gelu_exact(inner):
    return 0.5 * inner * (1.0 + lax.erf(inner * 0.7071067811865476))

def attend_block(block, keys_seq, values_seq, seg_seq):
    queries_block, seg_block = block
    scale = HEAD_DIM ** (-0.5)
    scores = jnp.einsum('rhd,khd->hrk', queries_block, keys_seq, precision=lax.Precision.HIGHEST) * scale
    allowed = (seg_block[:, None] == seg_seq[None, :])[None]
    scores = low_back(jnp.where(allowed, scores, MASKED_SCORE))
    top = lax.optimization_barrier(jnp.max(scores, axis=-1, keepdims=True))
    log_total = top + jnp.log(lax.optimization_barrier(jnp.sum(jnp.exp(scores - top), axis=-1, keepdims=True)))
    probs = low(jnp.exp(scores - log_total))
    return jnp.einsum('hrk,khd->rhd', probs, values_seq, precision=lax.Precision.HIGHEST)

def attend_sequence(items):
    queries_seq, keys_seq, values_seq, seg_seq = items
    rows = min(512, LENGTH)
    blocks = (queries_seq.reshape(LENGTH // rows, rows, HEADS, HEAD_DIM), seg_seq.reshape(LENGTH // rows, rows))
    one_block = jax.checkpoint(partial(attend_block, keys_seq=keys_seq, values_seq=values_seq, seg_seq=seg_seq))
    return lax.map(one_block, blocks).reshape(LENGTH, HEADS, HEAD_DIM)

def layer_forward(states_in, params, segment_ids):
    project_weight, query_bias, value_bias, output_weight, output_bias, attention_gain, attention_shift, up_weight, up_bias, down_weight, down_bias, feed_gain, feed_shift = params
    highest = lax.Precision.HIGHEST
    flat = states_in.reshape(-1, D)
    entered = low(flat)
    projected = jnp.dot(entered, project_weight, precision=highest)
    queries = low(low_back(projected[:, :D] + query_bias))
    keys_all = low(low_back(projected[:, D:2 * D]))
    values_all = low(low_back(projected[:, 2 * D:] + value_bias))
    shape_heads = (BATCH, LENGTH, HEADS, HEAD_DIM)
    attended = lax.map(attend_sequence, (queries.reshape(shape_heads), keys_all.reshape(shape_heads), values_all.reshape(shape_heads), segment_ids))
    context = low(low_back(attended.reshape(-1, D)))
    branch = low_back(jnp.dot(context, output_weight, precision=highest) + output_bias)
    hidden = layer_norm(flat + branch, attention_gain, attention_shift)
    inner = low_back(jnp.dot(low(hidden), up_weight, precision=highest) + up_bias)
    activated = low(gelu_exact(inner))
    outward = low_back(jnp.dot(activated, down_weight, precision=highest) + down_bias)
    return layer_norm(hidden + outward, feed_gain, feed_shift).reshape(BATCH, LENGTH, D)

def reference(states, segment_ids, project_weight, query_bias, value_bias, output_weight, output_bias, attention_gain, attention_shift, up_weight, up_bias, down_weight, down_bias, feed_gain, feed_shift, cotangent):
    params = (project_weight.astype(jnp.float32), query_bias.astype(jnp.float32), value_bias.astype(jnp.float32), output_weight.astype(jnp.float32), output_bias.astype(jnp.float32), attention_gain.astype(jnp.float32), attention_shift.astype(jnp.float32), up_weight.astype(jnp.float32), up_bias.astype(jnp.float32), down_weight.astype(jnp.float32), down_bias.astype(jnp.float32), feed_gain.astype(jnp.float32), feed_shift.astype(jnp.float32))

    def forward(first, weights):
        current = first
        for layer_index in range(LAYERS):
            current = layer_forward(current, tuple((item[layer_index] for item in weights)), segment_ids)
        return current
    result, backward = jax.vjp(forward, states.astype(jnp.float32), params)
    grad_input, grads = backward(cotangent.astype(jnp.float32))
    g_project, g_query, g_value, g_output_weight, g_output_bias, g_att_gain, g_att_shift, g_up_weight, g_up_bias, g_down_weight, g_down_bias, g_feed_gain, g_feed_shift = grads
    return (result.astype(jnp.bfloat16), grad_input, g_project, g_query, g_value, g_output_weight, g_output_bias, g_att_gain, g_att_shift, g_up_weight, g_up_bias, g_down_weight, g_down_bias, g_feed_gain, g_feed_shift)
```

```python
import functools
import math

import jax
import jax.numpy as jnp
from jax import lax
from jax.experimental import pallas as pl
from jax.experimental.pallas import tpu as pltpu
from jax.sharding import PartitionSpec as P

HEADS = 12
HEAD_DIM = 64
LAYERS = 2
EPSILON = 1e-12
MASKED = -2.0e9
LOWEST = -1.0e9
SCALE = HEAD_DIM**-0.5
BF16 = jnp.bfloat16
F32 = jnp.float32
VMEM_LIMIT = 58 * 1024 * 1024
RSQRT2 = 0.7071067811865476
PDF_SCALE = 0.3989422804014327


def nn(a, b):
    return lax.dot_general(a, b, (((1,), (0,)), ((), ())), preferred_element_type=F32)


def nt(a, b):
    return lax.dot_general(a, b, (((1,), (1,)), ((), ())), preferred_element_type=F32)


def tn(a, b):
    return lax.dot_general(a, b, (((0,), (0,)), ((), ())), preferred_element_type=F32)


def exchange(value, axis, size, mask):
    return lax.ppermute(value, axis, [(i, i ^ mask) for i in range(size)])


def resident(shape):
    return pl.BlockSpec(shape, lambda *unused: (0,) * len(shape))


def params(count=1):
    return pltpu.CompilerParams(
        dimension_semantics=("arbitrary",) * count, vmem_limit_bytes=VMEM_LIMIT
    )


SMEM_SPEC = pl.BlockSpec(memory_space=pltpu.SMEM)
ANY_SPEC = pl.BlockSpec(memory_space=pl.ANY)


def project_body(groups, span, order, x_ref, w_ref, b_ref, *rest):
    outs, flipped = rest[:groups], rest[groups]
    rows = nn(x_ref[...].astype(BF16), w_ref[...]) + b_ref[0]
    flipped[...] = rows.T.astype(BF16)
    for r in range(groups):
        start = pl.multiple_of(order[r] * span, span)
        outs[r][0] = flipped[pl.ds(start, span), :]


def project(order, rows, weight, bias, groups):
    tokens, width = rows.shape
    span = width // groups
    return pl.pallas_call(
        functools.partial(project_body, groups, span),
        out_shape=[jax.ShapeDtypeStruct((3, span, tokens), BF16)] * groups,
        grid=(3,),
        in_specs=[
            SMEM_SPEC,
            resident((tokens, width)),
            pl.BlockSpec((width, width), lambda j: (0, j)),
            pl.BlockSpec((1, 1, width), lambda j: (j, 0, 0)),
        ],
        out_specs=[pl.BlockSpec((1, span, tokens), lambda j: (j, 0, 0))] * groups,
        scratch_shapes=[pltpu.VMEM((width, tokens), BF16)],
        compiler_params=params(),
        cost_estimate=pl.CostEstimate(
            flops=6 * tokens * width * width, bytes_accessed=6 * width * width, transcendentals=0
        ),
        name="project",
    )(order, rows, weight, bias)


def load_stack(parts, stack, sems):
    copies = [pltpu.make_async_copy(part, stack.at[i], sems.at[i]) for i, part in enumerate(parts)]
    for copy in copies:
        copy.start()
    for copy in copies:
        copy.wait()


def attend_body(groups, members, heads, active, seg_row, seg_col, *rest):
    count = groups * members
    parts, rest = rest[:count], rest[count:]
    outs, rest = rest[:groups], rest[groups:]
    exact, log_total, stack, top, total, gathered, sems = rest
    load_stack(parts, stack, sems)
    tokens = stack.shape[-1]

    def one_block(r, unused):
        seg_query = seg_row[r]
        top[...] = jnp.full_like(top, LOWEST)
        total[...] = jnp.zeros_like(total)
        gathered[...] = jnp.zeros_like(gathered)

        def one_key(kb, unused):
            @pl.when(active[r, kb] != 0)
            def _():
                allowed = jnp.broadcast_to(seg_col[kb], (tokens, tokens)) == seg_query
                for h in range(heads):
                    part = pl.ds(h * HEAD_DIM, HEAD_DIM)
                    query = stack[r, 0, part, :] * SCALE
                    scores = tn(stack[kb, 1, part, :], query.astype(BF16))
                    scores = jnp.where(allowed, scores, MASKED)
                    old = top[h]
                    new = jnp.maximum(old, jnp.max(scores, axis=0, keepdims=True))
                    weights = jnp.exp(scores - new)
                    fade = jnp.exp(old - new)
                    total[h] = total[h] * fade + jnp.sum(weights, axis=0, keepdims=True)
                    top[h] = new
                    gathered[h] = gathered[h] * fade + nn(
                        stack[kb, 2, part, :], weights.astype(BF16)
                    )

            return unused

        lax.fori_loop(0, count, one_key, 0)
        for h in range(heads):
            exact[r, pl.ds(h * HEAD_DIM, HEAD_DIM), :] = gathered[h] / total[h]
            log_total[r, h] = top[h] + jnp.log(total[h])
        return unused

    lax.fori_loop(0, groups, one_block, 0)
    for r in range(groups):
        outs[r][...] = exact[r].astype(BF16)


def attend(active, seg_row, seg_col, parts, groups, members):
    unused, span, tokens = parts[0].shape
    heads = span // HEAD_DIM
    count = groups * members
    return pl.pallas_call(
        functools.partial(attend_body, groups, members, heads),
        out_shape=[jax.ShapeDtypeStruct((span, tokens), BF16)] * groups
        + [
            jax.ShapeDtypeStruct((groups, span, tokens), F32),
            jax.ShapeDtypeStruct((groups, heads, 1, tokens), F32),
        ],
        in_specs=[SMEM_SPEC, resident(seg_row.shape), resident(seg_col.shape)]
        + [ANY_SPEC] * count,
        out_specs=[resident((span, tokens))] * groups
        + [resident((groups, span, tokens)), resident((groups, heads, 1, tokens))],
        grid=(1,),
        scratch_shapes=[
            pltpu.VMEM((count, 3, span, tokens), BF16),
            pltpu.VMEM((heads, 1, tokens), F32),
            pltpu.VMEM((heads, 1, tokens), F32),
            pltpu.VMEM((heads, HEAD_DIM, tokens), F32),
            pltpu.SemaphoreType.DMA((count,)),
        ],
        compiler_params=params(),
        cost_estimate=pl.CostEstimate(
            flops=2 * span * groups * count * tokens * tokens,
            bytes_accessed=10 * span * tokens * count,
            transcendentals=heads * groups * count * tokens * tokens // 2,
        ),
        name="attend",
    )(active, seg_row, seg_col, *parts)


def attend_back_body(groups, members, heads, active, seg_row, seg_col, *rest):
    count = groups * members
    parts, rest = rest[:count], rest[count:]
    grads, rest = rest[:groups], rest[groups:]
    exact, log_total, rest = rest[0], rest[1], rest[2:]
    out_query, out_own, rest = rest[0], rest[1], rest[2:]
    out_send, rest = rest[: members - 1], rest[members - 1 :]
    stack, grad_stack, delta, grad_query, grad_kv, sems = rest
    load_stack(parts, stack, sems)
    tokens = stack.shape[-1]
    for r in range(groups):
        grad_stack[r] = grads[r][...]
    grad_kv[...] = jnp.zeros_like(grad_kv)

    def one_block(r, unused):
        seg_query = seg_row[r]
        grad_query[...] = jnp.zeros_like(grad_query)
        for h in range(heads):
            part = pl.ds(h * HEAD_DIM, HEAD_DIM)
            delta[h] = jnp.sum(
                grad_stack[r, part, :].astype(F32) * exact[r, part, :], axis=0, keepdims=True
            )

        def one_key(kb, unused):
            @pl.when(active[r, kb] != 0)
            def _():
                allowed = jnp.broadcast_to(seg_col[kb], (tokens, tokens)) == seg_query
                for h in range(heads):
                    part = pl.ds(h * HEAD_DIM, HEAD_DIM)
                    query = (stack[r, 0, part, :] * SCALE).astype(BF16)
                    grad = grad_stack[r, part, :]
                    keys = stack[kb, 1, part, :]
                    scores = jnp.where(allowed, tn(keys, query), MASKED)
                    weights = jnp.exp(scores - log_total[r, h])
                    grad_kv[kb, 1, part, :] += nt(grad, weights.astype(BF16))
                    grad_weights = tn(stack[kb, 2, part, :], grad)
                    grad_scores = (weights * (grad_weights - delta[h])).astype(BF16)
                    grad_kv[kb, 0, part, :] += nt(query, grad_scores)
                    grad_query[part, :] += nn(keys, grad_scores)

            return unused

        lax.fori_loop(0, count, one_key, 0)
        out_query[r] = (grad_query[...] * SCALE).astype(BF16)
        return unused

    lax.fori_loop(0, groups, one_block, 0)
    out_own[...] = grad_kv[:groups]
    for j in range(1, members):
        out_send[j - 1][...] = grad_kv[j * groups : (j + 1) * groups].astype(BF16)


def attend_back(active, seg_row, seg_col, parts, grads, exact, log_total, groups, members):
    unused, span, tokens = parts[0].shape
    heads = span // HEAD_DIM
    count = groups * members
    kv_shape = (groups, 2, span, tokens)
    return pl.pallas_call(
        functools.partial(attend_back_body, groups, members, heads),
        out_shape=[
            jax.ShapeDtypeStruct((groups, span, tokens), BF16),
            jax.ShapeDtypeStruct(kv_shape, F32),
        ]
        + [jax.ShapeDtypeStruct(kv_shape, BF16)] * (members - 1),
        in_specs=[SMEM_SPEC, resident(seg_row.shape), resident(seg_col.shape)]
        + [ANY_SPEC] * count
        + [resident((span, tokens))] * groups
        + [resident(exact.shape), resident(log_total.shape)],
        out_specs=[resident((groups, span, tokens)), resident(kv_shape)]
        + [resident(kv_shape)] * (members - 1),
        grid=(1,),
        scratch_shapes=[
            pltpu.VMEM((count, 3, span, tokens), BF16),
            pltpu.VMEM((groups, span, tokens), BF16),
            pltpu.VMEM((heads, 1, tokens), F32),
            pltpu.VMEM((span, tokens), F32),
            pltpu.VMEM((count, 2, span, tokens), F32),
            pltpu.SemaphoreType.DMA((count,)),
        ],
        compiler_params=params(),
        cost_estimate=pl.CostEstimate(
            flops=5 * span * groups * count * tokens * tokens,
            bytes_accessed=20 * span * tokens * count,
            transcendentals=heads * groups * count * tokens * tokens // 2,
        ),
        name="attend_back",
    )(active, seg_row, seg_col, *parts, *grads, exact, log_total)


OUT_BIAS, ATT_GAIN, ATT_SHIFT, DOWN_BIAS, FEED_GAIN, FEED_SHIFT = range(6)


def normalized(rows):
    centre = rows - jnp.mean(rows, axis=-1, keepdims=True)
    spread = jnp.mean(centre * centre, axis=-1, keepdims=True)
    inverse = lax.rsqrt(spread + EPSILON)
    return centre * inverse, inverse


def norm_back(grad, gain, normal, inverse):
    scaled = grad * gain
    mean_scaled = jnp.mean(scaled, axis=-1, keepdims=True)
    mean_both = jnp.mean(scaled * normal, axis=-1, keepdims=True)
    return inverse * (scaled - mean_scaled - normal * mean_both)


def feed_body(groups, span, blocks, order, x_ref, wo_ref, wu_ref, wd_ref, vec, ub_ref, *rest):
    contexts, rest = rest[:groups], rest[groups:]
    sum_first, hidden_low, sum_second, out, hidden, outward = rest
    j = pl.program_id(0)

    @pl.when(j == 0)
    def _():
        rows = x_ref[...] + vec[OUT_BIAS : OUT_BIAS + 1, :]
        for r in range(groups):
            start = pl.multiple_of(order[r] * span, span)
            rows += tn(contexts[r][...], wo_ref[pl.ds(start, span), :])
        sum_first[...] = rows
        normal, unused = normalized(rows)
        value = normal * vec[ATT_GAIN : ATT_GAIN + 1, :] + vec[ATT_SHIFT : ATT_SHIFT + 1, :]
        hidden[...] = value
        hidden_low[...] = value.astype(BF16)
        outward[...] = jnp.zeros_like(outward)

    inner = nn(hidden_low[...], wu_ref[...]) + ub_ref[0]
    activated = (0.5 * inner * (1.0 + lax.erf(inner * RSQRT2))).astype(BF16)
    outward[...] += nn(activated, wd_ref[...])

    @pl.when(j == blocks - 1)
    def _():
        rows = hidden[...] + outward[...] + vec[DOWN_BIAS : DOWN_BIAS + 1, :]
        sum_second[...] = rows
        normal, unused = normalized(rows)
        out[...] = normal * vec[FEED_GAIN : FEED_GAIN + 1, :] + vec[FEED_SHIFT : FEED_SHIFT + 1, :]


def feed(order, rows, w_output, w_up, w_down, vectors, up_bias, contexts):
    tokens, width = rows.shape
    groups, span = len(contexts), contexts[0].shape[0]
    blocks = w_up.shape[1] // width
    full = jax.ShapeDtypeStruct((tokens, width), F32)
    return pl.pallas_call(
        functools.partial(feed_body, groups, span, blocks),
        out_shape=[full, jax.ShapeDtypeStruct((tokens, width), BF16), full, full],
        grid=(blocks,),
        in_specs=[
            SMEM_SPEC,
            resident((tokens, width)),
            resident((width, width)),
            pl.BlockSpec((width, width), lambda j: (0, j)),
            pl.BlockSpec((width, width), lambda j: (j, 0)),
            resident(vectors.shape),
            pl.BlockSpec((1, 1, width), lambda j: (j, 0, 0)),
        ]
        + [resident((span, tokens))] * groups,
        out_specs=[resident((tokens, width))] * 4,
        scratch_shapes=[pltpu.VMEM((tokens, width), F32)] * 2,
        compiler_params=params(),
        cost_estimate=pl.CostEstimate(
            flops=(4 * blocks + 2) * tokens * width * width,
            bytes_accessed=(4 * blocks + 2) * width * width,
            transcendentals=0,
        ),
        name="feed",
    )(order, rows, w_output, w_up, w_down, vectors, up_bias, *contexts)


def feed_back_body(
    groups, span, blocks, devices, order, place, grad_ref, first_ref, second_ref, low_ref, *rest
):
    wo_ref, wu_ref, wd_ref, vec, ub_ref = rest[:5]
    contexts, rest = rest[5 : 5 + groups], rest[5 + groups :]
    own, send, grad_first, small = rest[:4]
    grad_contexts, rest = rest[4 : 4 + groups], rest[4 + groups :]
    grad_out, grad_hidden, tile = rest
    width = vec.shape[-1]
    me = place[0]
    j = pl.program_id(0)
    share = width // devices
    down_share = blocks * share
    per_block = width // down_share

    @pl.when(j == 0)
    def _():
        small[...] = jnp.zeros_like(small)
        grad = grad_ref[...]
        normal, inverse = normalized(second_ref[...])
        value = norm_back(grad, vec[FEED_GAIN : FEED_GAIN + 1, :], normal, inverse)
        grad_hidden[...] = value
        low = value.astype(BF16)
        grad_out[...] = low
        small[DOWN_BIAS : DOWN_BIAS + 1, :] = jnp.sum(low.astype(F32), axis=0, keepdims=True)
        small[FEED_GAIN : FEED_GAIN + 1, :] = jnp.sum(grad * normal, axis=0, keepdims=True)
        small[FEED_SHIFT : FEED_SHIFT + 1, :] = jnp.sum(grad, axis=0, keepdims=True)

    inner = nn(low_ref[...], wu_ref[...]) + ub_ref[0]
    below = 0.5 * (1.0 + lax.erf(inner * RSQRT2))
    activated = (inner * below).astype(BF16)
    slope = below + inner * (PDF_SCALE * jnp.exp(-0.5 * inner * inner))
    grad_inner = (nt(grad_out[...], wd_ref[...]) * slope).astype(BF16)
    small[pl.ds(8 + j, 1), :] = jnp.sum(grad_inner.astype(F32), axis=0, keepdims=True)
    grad_hidden[...] += nt(grad_inner, wu_ref[...])

    tile[...] = tn(activated, grad_out[...]).astype(BF16)
    for k in range(per_block):
        owner = (j * per_block + k) ^ me
        slot = lax.shift_right_logical(owner, 1)
        rows = pl.ds(k * down_share, down_share)

        @pl.when((owner & 1) == 0)
        def _():
            own[slot, pl.ds(0, down_share), :] = tile[rows, :]

        @pl.when((owner & 1) == 1)
        def _():
            send[slot, pl.ds(0, down_share), :] = tile[rows, :]

    tile[...] = tn(low_ref[...], grad_inner).astype(BF16)
    for i in range(devices // 2):
        for bit, target in ((0, own), (1, send)):
            start = pl.multiple_of((me ^ (2 * i + bit)) * share, share)
            base = pl.multiple_of(down_share + j * share, share)
            target[i, pl.ds(base, share), :] = tile[pl.ds(start, share), :]

    @pl.when(j == blocks - 1)
    def _():
        grad = grad_hidden[...]
        normal, inverse = normalized(first_ref[...])
        value = norm_back(grad, vec[ATT_GAIN : ATT_GAIN + 1, :], normal, inverse)
        grad_first[...] = value
        low = value.astype(BF16)
        small[OUT_BIAS : OUT_BIAS + 1, :] = jnp.sum(low.astype(F32), axis=0, keepdims=True)
        small[ATT_GAIN : ATT_GAIN + 1, :] = jnp.sum(grad * normal, axis=0, keepdims=True)
        small[ATT_SHIFT : ATT_SHIFT + 1, :] = jnp.sum(grad, axis=0, keepdims=True)
        for r in range(groups):
            start = pl.multiple_of(order[r] * span, span)
            tile[pl.ds(start, span), :] = nn(contexts[r][...], low).astype(BF16)
            grad_contexts[r][...] = nt(wo_ref[pl.ds(start, span), :], low).astype(BF16)
        for i in range(devices // 2):
            for bit, target in ((0, own), (1, send)):
                start = pl.multiple_of((me ^ (2 * i + bit)) * share, share)
                base = down_share + blocks * share
                target[i, base : base + share, :] = tile[pl.ds(start, share), :]


def feed_back(
    order, place, grad, first, second, low, w_output, w_up, w_down, vectors, up_bias, contexts, devices
):
    tokens, width = grad.shape
    groups, span = len(contexts), contexts[0].shape[0]
    blocks = w_up.shape[1] // width
    share = width // devices
    kept = (devices // 2, (2 * blocks + 1) * share, width)
    return pl.pallas_call(
        functools.partial(feed_back_body, groups, span, blocks, devices),
        out_shape=[
            jax.ShapeDtypeStruct(kept, BF16),
            jax.ShapeDtypeStruct(kept, BF16),
            jax.ShapeDtypeStruct((tokens, width), F32),
            jax.ShapeDtypeStruct((16, width), F32),
        ]
        + [jax.ShapeDtypeStruct((span, tokens), BF16)] * groups,
        grid=(blocks,),
        in_specs=[SMEM_SPEC, SMEM_SPEC]
        + [resident((tokens, width))] * 4
        + [
            resident((width, width)),
            pl.BlockSpec((width, width), lambda j: (0, j)),
            pl.BlockSpec((width, width), lambda j: (j, 0)),
            resident(vectors.shape),
            pl.BlockSpec((1, 1, width), lambda j: (j, 0, 0)),
        ]
        + [resident((span, tokens))] * groups,
        out_specs=[resident(kept), resident(kept), resident((tokens, width)), resident((16, width))]
        + [resident((span, tokens))] * groups,
        scratch_shapes=[
            pltpu.VMEM((tokens, width), BF16),
            pltpu.VMEM((tokens, width), F32),
            pltpu.VMEM((width, width), BF16),
        ],
        compiler_params=params(),
        cost_estimate=pl.CostEstimate(
            flops=(10 * blocks + 4) * tokens * width * width,
            bytes_accessed=(8 * blocks + 4) * width * width,
            transcendentals=0,
        ),
        name="feed_back",
    )(
        order,
        place,
        grad,
        first,
        second,
        low,
        w_output,
        w_up,
        w_down,
        vectors,
        up_bias,
        *contexts,
    )


def project_back_body(groups, span, devices, order, place, x_ref, grad_ref, w_ref, *rest):
    pieces, rest = rest[:groups], rest[groups:]
    own, send, out, small, joined, tile = rest
    width = w_ref.shape[0]
    me = place[0]
    j = pl.program_id(0)
    share = width // devices

    @pl.when(j == 0)
    def _():
        out[...] = grad_ref[...]
        small[...] = jnp.zeros_like(small)

    for r in range(groups):
        start = pl.multiple_of(order[r] * span, span)
        joined[pl.ds(start, span), :] = pieces[r][0]
    grad = joined[...].T
    small[pl.ds(j, 1), :] = jnp.sum(grad.astype(F32), axis=0, keepdims=True)
    out[...] += nt(grad, w_ref[...])
    tile[...] = tn(x_ref[...].astype(BF16), grad).astype(BF16)
    for i in range(devices // 2):
        for bit, target in ((0, own), (1, send)):
            start = pl.multiple_of((me ^ (2 * i + bit)) * share, share)
            base = pl.multiple_of(j * share, share)
            target[i, pl.ds(base, share), :] = tile[pl.ds(start, share), :]


def project_back(order, place, rows, grad, weight, pieces, devices):
    tokens, width = rows.shape
    groups, span = len(pieces), pieces[0].shape[1]
    kept = (devices // 2, 3 * (width // devices), width)
    return pl.pallas_call(
        functools.partial(project_back_body, groups, span, devices),
        out_shape=[
            jax.ShapeDtypeStruct(kept, BF16),
            jax.ShapeDtypeStruct(kept, BF16),
            jax.ShapeDtypeStruct((tokens, width), F32),
            jax.ShapeDtypeStruct((8, width), F32),
        ],
        grid=(3,),
        in_specs=[
            SMEM_SPEC,
            SMEM_SPEC,
            resident((tokens, width)),
            resident((tokens, width)),
            pl.BlockSpec((width, width), lambda j: (0, j)),
        ]
        + [pl.BlockSpec((1, span, tokens), lambda j: (j, 0, 0))] * groups,
        out_specs=[resident(kept), resident(kept), resident((tokens, width)), resident((8, width))],
        scratch_shapes=[pltpu.VMEM((width, tokens), BF16), pltpu.VMEM((width, width), BF16)],
        compiler_params=params(),
        cost_estimate=pl.CostEstimate(
            flops=12 * tokens * width * width, bytes_accessed=12 * width * width, transcendentals=0
        ),
        name="project_back",
    )(order, place, rows, grad, weight, *pieces)


class Stream:
    def __init__(self, steps):
        self.steps, self.result = steps, None
        self.flying = next(steps)

    def resume(self, arrived):
        try:
            self.flying = self.steps.send(arrived)
        except StopIteration as stop:
            self.flying, self.result = None, stop.value


def tick(streams, values=()):
    streams = [item for item in streams if item.flying is not None]
    values, flying = lax.optimization_barrier((values, [item.flying for item in streams]))
    for item, arrived in zip(streams, flying):
        item.resume(arrived)
    return values


def gather_steps(shard, devices, dp_size, masks):
    arrived = yield [exchange(shard, "dp", dp_size, m) for m in range(1, dp_size)]
    stack = jnp.stack([shard] + list(arrived))
    offsets = [(m, 0) for m in range(dp_size)]
    stacks = [stack]
    for mask in masks:
        (other,) = yield [exchange(stack, "seq", devices, mask)]
        offsets += [(d, q ^ mask) for d, q in offsets]
        stacks = [stack, other]
        stack = jnp.concatenate(stacks)
    arrived = yield [exchange(item, "seq", devices, 1) for item in stacks]
    offsets += [(d, q ^ 1) for d, q in offsets]
    return stacks + list(arrived), offsets


def sum_steps(own, send, devices, dp_size, dp_me):
    (arrived,) = yield [exchange(send, "seq", devices, 1)]
    rows, width = own.shape[1:]
    cut = rows // 2
    bits = int(math.log2(devices)) - 1
    masks = [2 << b for b in range(bits)]
    orders = (masks, masks[::-1])
    axes = [masks[::-1], masks[::-1]]
    kept = [
        add_low(own[:, part], arrived[:, part]).reshape((2,) * bits + (-1, width))
        for part in (slice(0, cut), slice(cut, rows))
    ]
    for step in range(bits):
        stay, leave = [], []
        for k in range(2):
            mask = orders[k][step]
            at = axes[k].index(mask)
            axes[k] = [m for m in axes[k] if m != mask]
            stay.append(lax.index_in_dim(kept[k], 0, at, keepdims=False))
            leave.append(
                exchange(lax.index_in_dim(kept[k], 1, at, keepdims=False), "seq", devices, mask)
            )
        leave = yield leave
        kept = [add_low(a, b) for a, b in zip(stay, leave)]
    total = jnp.concatenate(kept, axis=0)
    if dp_size != 4:
        return lax.psum(total, "dp")
    pieces = total.reshape(dp_size, rows // dp_size, width)

    def piece(m):
        return lax.dynamic_index_in_dim(pieces, dp_me ^ m, 0, keepdims=False)

    arrived = yield [exchange(piece(m), "dp", dp_size, m) for m in range(1, dp_size)]
    mine = sum((item.astype(F32) for item in arrived), piece(0).astype(F32)).astype(BF16)
    arrived = yield [exchange(mine, "dp", dp_size, m) for m in range(1, dp_size)]
    stack = [mine] + list(arrived)
    for bit in (1, 2):
        flip = (dp_me & bit) != 0
        stack = [jnp.where(flip, stack[i ^ bit], stack[i]) for i in range(dp_size)]
    return jnp.concatenate(stack, axis=0)


def vector_sum_steps(value, devices, dp_size):
    for axis, size in (("seq", devices), ("dp", dp_size)):
        for bit in range(int(math.log2(size))):
            (other,) = yield [exchange(value, axis, size, 1 << bit)]
            value = value + other
    return value


def add_low(a, b):
    return (a.astype(F32) + b.astype(F32)).astype(BF16)


def place_body(sources, layout, outs_count, table, *rest):
    parts, rest = rest[:sources], rest[sources:]
    outs, (buffer, in_sems, out_sems) = rest[:outs_count], rest[outs_count:]
    per = buffer.shape[0] // sources

    def into(a, k):
        i = a * per + k
        return pltpu.make_async_copy(parts[a].at[k], buffer.at[i], in_sems.at[i])

    def onward(a, k):
        i = a * per + k
        half = a * 2 // sources
        copies = []
        for at, (target, index, column, size, first) in enumerate(layout[half]):
            if index is None:
                goal = outs[target].at[table[i], :, pl.ds(first, size)]
            else:
                goal = outs[target].at[table[i], index]
            copies.append(
                pltpu.make_async_copy(
                    buffer.at[i, :, pl.ds(column, size)], goal, out_sems.at[i, at]
                )
            )
        return copies

    for a in range(sources):

        def begin(k, unused, a=a):
            into(a, k).start()
            return unused

        lax.fori_loop(0, per, begin, 0)
    for a in range(sources):

        def middle(k, unused, a=a):
            into(a, k).wait()
            for copy in onward(a, k):
                copy.start()
            return unused

        lax.fori_loop(0, per, middle, 0)
    for a in range(sources):

        def finish(k, unused, a=a):
            for copy in onward(a, k):
                copy.wait()
            return unused

        lax.fori_loop(0, per, finish, 0)


def put_in_place(first, second, layout, shapes, me, dp_me, devices):
    parts = first[0] + second[0]
    offsets = jnp.array(first[1] + second[1], jnp.int32)
    table = (dp_me ^ offsets[:, 0]) * devices + (me ^ offsets[:, 1])
    depth, columns = parts[0].shape[1:]
    count = len(first[1]) * 2
    most = max(len(item) for item in layout)
    size = 4 * count * depth * columns
    return pl.pallas_call(
        functools.partial(place_body, len(parts), layout, len(shapes)),
        out_shape=[jax.ShapeDtypeStruct(shape, BF16) for shape in shapes],
        in_specs=[SMEM_SPEC] + [ANY_SPEC] * len(parts),
        out_specs=[ANY_SPEC] * len(shapes),
        scratch_shapes=[
            pltpu.VMEM((count, depth, columns), BF16),
            pltpu.SemaphoreType.DMA((count,)),
            pltpu.SemaphoreType.DMA((count, most)),
        ],
        compiler_params=pltpu.CompilerParams(vmem_limit_bytes=VMEM_LIMIT),
        cost_estimate=pl.CostEstimate(flops=0, bytes_accessed=size, transcendentals=0),
        name="put_in_place",
    )(table, *parts)


def per_device(
    seq_size,
    dp_size,
    states,
    segment_ids,
    project_weight,
    query_bias,
    value_bias,
    output_weight,
    output_bias,
    attention_gain,
    attention_shift,
    up_weight,
    up_bias,
    down_weight,
    down_bias,
    feed_gain,
    feed_shift,
    cotangent,
):
    unused, tokens, width = states.shape
    groups = math.gcd(HEADS, seq_size)
    members = seq_size // groups
    share = width // seq_size
    inner_width = up_weight.shape[2]
    blocks = inner_width // width
    depth = width // (seq_size * dp_size)
    everyone = seq_size * dp_size
    me = lax.axis_index("seq")
    dp_me = lax.axis_index("dp")
    order = (me // members) ^ jnp.arange(groups, dtype=jnp.int32)
    place = me.reshape(1).astype(jnp.int32)
    both = ("dp", "seq")
    plain = depth % 8 != 0 or dp_size != 4

    vectors = jnp.stack(
        [
            output_bias,
            attention_gain,
            attention_shift,
            down_bias,
            feed_gain,
            feed_shift,
            query_bias,
            value_bias,
        ],
        axis=1,
    )
    flat = jnp.concatenate(
        [vectors.reshape(-1), up_bias.reshape(-1), segment_ids.astype(BF16).reshape(-1)]
    )
    used = flat.shape[0]
    flat = jnp.pad(flat, (0, -used % 1024)).reshape(-1, 128)

    def chunk_project(layer, half):
        cut = 3 * width // 2
        return project_weight[layer, :, half * cut : (half + 1) * cut]

    def chunk_rest(layer, half):
        cut = down_weight.shape[1] // 2
        down = down_weight[layer, half * cut : (half + 1) * cut]
        return jnp.concatenate(
            [
                output_weight[layer, :, half * (width // 2) : (half + 1) * (width // 2)],
                up_weight[layer, :, half * (inner_width // 2) : (half + 1) * (inner_width // 2)],
            ]
            + [down[t * depth : (t + 1) * depth] for t in range(blocks // 2)],
            axis=1,
        )

    masks = [2 << b for b in range(int(math.log2(seq_size)) - 1)]

    def gather(chunk, half=0):
        return Stream(gather_steps(chunk, seq_size, dp_size, masks[::-1] if half else masks))

    def project_streams(layer):
        return [gather(chunk_project(layer, half), half) for half in range(2)]

    def rest_streams(layer):
        return [gather(chunk_rest(layer, half), half) for half in range(2)]

    def placed_project(streams):
        cut = 3 * width // 2
        layout = [[(0, None, 0, cut, half * cut)] for half in range(2)]
        (made,) = put_in_place(
            streams[0].result,
            streams[1].result,
            layout,
            [(everyone, depth, 3 * width)],
            me,
            dp_me,
            seq_size,
        )
        return made.reshape(width, 3 * width)

    def placed_rest(streams):
        a, b = width // 2, inner_width // 2
        layout = [
            [(0, None, 0, a, half * a), (1, None, a, b, half * b)]
            + [
                (2, half * (blocks // 2) + t, a + b + t * width, width, 0)
                for t in range(blocks // 2)
            ]
            for half in range(2)
        ]
        w_output, w_up, w_down = put_in_place(
            streams[0].result,
            streams[1].result,
            layout,
            [
                (everyone, depth, width),
                (everyone, depth, inner_width),
                (everyone, blocks, depth, width),
            ],
            me,
            dp_me,
            seq_size,
        )
        return (
            w_output.reshape(width, width),
            w_up.reshape(width, inner_width),
            w_down.reshape(inner_width, width),
        )

    def swap_groups(items):
        return [items[0]] + [
            exchange(items[r], "seq", seq_size, r * members) for r in range(1, groups)
        ]

    def with_members(items):
        items = list(items)
        own = list(items)
        for j in range(1, members):
            items += [exchange(item, "seq", seq_size, j) for item in own]
        return items

    w_project, w_rest = [None] * LAYERS, [None] * LAYERS
    if plain:
        table = lax.all_gather(flat, both, axis=0, tiled=False)
        for layer in range(LAYERS):
            w_project[layer] = lax.all_gather(project_weight[layer], both, axis=0, tiled=True)
            w_rest[layer] = tuple(
                lax.all_gather(item[layer], both, axis=0, tiled=True)
                for item in (output_weight, up_weight, down_weight)
            )
        projects = rests = [[]] * LAYERS
    else:
        small = gather(flat)
        projects, rests = [project_streams(0), None], [None, None]
        first = projects[0] + [small]
        tick(first)
        rests[0] = rest_streams(0)
        tick(first)
        tick(first)
        tick(rests[0])
        tick(first)
        stacks, offsets = small.result
        offsets = jnp.array(offsets, jnp.int32)
        where = {pair: i for i, pair in enumerate(small.result[1])}
        lookup = jnp.array(
            [where[(d, q)] for d in range(dp_size) for q in range(seq_size)], jnp.int32
        )
        wanted = jnp.arange(everyone, dtype=jnp.int32) ^ (dp_me * seq_size + me)
        table = jnp.take(jnp.concatenate(stacks), jnp.take(lookup, wanted), axis=0)

    table = table.reshape(everyone, -1)
    small_rows = LAYERS * 8 * depth
    up_share = inner_width // everyone
    vectors = (
        table[:, :small_rows]
        .reshape(everyone, LAYERS, 8, depth)
        .transpose(1, 2, 0, 3)
        .reshape(LAYERS, 8, width)
        .astype(F32)
    )
    up_biases = (
        table[:, small_rows : small_rows + LAYERS * up_share]
        .reshape(everyone, LAYERS, up_share)
        .transpose(1, 0, 2)
        .reshape(LAYERS, blocks, 1, width)
        .astype(F32)
    )
    relative = jnp.array([r * members + j for j in range(members) for r in range(groups)], jnp.int32)
    segments = jnp.take(
        table[:, used - tokens : used], dp_me * seq_size + (me ^ relative), axis=0
    ).astype(jnp.int32)
    first_id, last_id = segments[:, 0], segments[:, -1]
    active = (
        (first_id[:groups, None] <= last_id[None, :])
        & (first_id[None, :] <= last_id[:groups, None])
    ).astype(jnp.int32)
    seg_row = segments[:groups, None, :]
    seg_col = segments[:, :, None]

    def projected(layer, current):
        vec = vectors[layer]
        bias = jnp.stack([vec[6], jnp.zeros_like(vec[6]), vec[7]])[:, None, :]
        return project(order, current, w_project[layer], bias, groups)

    current = states[0].astype(F32)
    saved = []
    for layer in range(LAYERS):
        last = layer == LAYERS - 1
        if not plain:
            w_project[layer] = placed_project(projects[layer])
        made = projected(layer, current)
        parts = with_members(swap_groups(made))
        parts = tick(rests[layer], tuple(parts))
        if not plain and not last:
            projects[layer + 1] = project_streams(layer + 1)
            rests[layer + 1] = rest_streams(layer + 1)
        *mixed, exact, log_total = attend(active, seg_row, seg_col, parts, groups, members)
        contexts = tuple(swap_groups(mixed))
        ahead = [] if plain or last else projects[layer + 1]
        contexts = tick(rests[layer] + ahead, contexts)
        contexts = tick(rests[layer] + ahead, contexts)
        if not plain:
            w_rest[layer] = placed_rest(rests[layer])
        w_output, w_up, w_down = w_rest[layer]
        sum_first, low, sum_second, following = feed(
            order,
            current,
            w_output,
            w_up,
            w_down,
            vectors[layer],
            up_biases[layer],
            contexts,
        )
        saved.append((current, parts, exact, log_total, contexts, sum_first, low, sum_second))
        current = following
        if not plain and not last:
            current = tick(ahead + rests[layer + 1], current)
            current = tick(ahead, current)
    output = current.astype(BF16)[None]

    grad = cotangent[0].astype(F32)
    smalls = [None] * LAYERS
    feeds, backs = [None] * LAYERS, [None] * LAYERS
    behind = []
    for layer in reversed(range(LAYERS)):
        w_output, w_up, w_down = w_rest[layer]
        entered, parts, exact, log_total, contexts, sum_first, low, sum_second = saved[layer]
        own, send, grad_first, small_feed, *grad_mixed = feed_back(
            order,
            place,
            grad,
            sum_first,
            sum_second,
            low,
            w_output,
            w_up,
            w_down,
            vectors[layer],
            up_biases[layer],
            contexts,
            seq_size,
        )
        grad_mixed = tick(behind, tuple(grad_mixed))
        feeds[layer] = Stream(sum_steps(own, send, seq_size, dp_size, dp_me))
        grads = tuple(swap_groups(grad_mixed))
        grads = tick(behind + [feeds[layer]], grads)
        grad_query, kept_kv, *sent_kv = attend_back(
            active, seg_row, seg_col, parts, grads, exact, log_total, groups, members
        )
        for j in range(1, members):
            kept_kv = kept_kv + exchange(sent_kv[j - 1], "seq", seq_size, j).astype(F32)
        messages = [
            jnp.concatenate([grad_query[r][None], kept_kv[r].astype(BF16)], axis=0)
            for r in range(groups)
        ]
        messages = tick(behind, tuple(messages))
        pieces = tuple(swap_groups(messages))
        pieces = tick(behind + [feeds[layer]], pieces)
        own, send, grad, small_project = project_back(
            order, place, entered, grad_first, w_project[layer], pieces, seq_size
        )
        backs[layer] = Stream(sum_steps(own, send, seq_size, dp_size, dp_me))
        behind = [feeds[layer], backs[layer]]
        smalls[layer] = jnp.concatenate(
            [small_feed[:6], small_feed[8 : 8 + blocks], small_project[0:1], small_project[2:3]],
            axis=0,
        )
    vector_sum = Stream(vector_sum_steps(jnp.stack(smalls), seq_size, dp_size))
    behind = feeds + backs + [vector_sum]
    while any(item.flying is not None for item in behind):
        tick(behind)
    small = vector_sum.result
    results = [(feeds[layer].result, backs[layer].result) for layer in range(LAYERS)]

    def mine(rows, size):
        return lax.dynamic_slice_in_dim(rows, me * size, size, axis=1)

    def columns(part, which):
        return jnp.concatenate([part[i * share : (i + 1) * share] for i in which], axis=1).astype(F32)

    down_rows = blocks * share
    g_project = jnp.stack([columns(item[1], range(3)) for item in results])
    g_up = jnp.stack([columns(item[0], range(blocks, 2 * blocks)) for item in results])
    g_down = jnp.stack([item[0][:down_rows].astype(F32) for item in results])
    g_output = jnp.stack([item[0][down_rows + blocks * share :].astype(F32) for item in results])
    wide = small[:, 6 : 6 + blocks].reshape(LAYERS, blocks * width)
    return (
        output,
        grad[None],
        g_project,
        mine(small[:, 6 + blocks], share),
        mine(small[:, 7 + blocks], share),
        g_output,
        mine(small[:, OUT_BIAS], share),
        mine(small[:, ATT_GAIN], share),
        mine(small[:, ATT_SHIFT], share),
        g_up,
        mine(wide, blocks * share),
        g_down,
        mine(small[:, DOWN_BIAS], share),
        mine(small[:, FEED_GAIN], share),
        mine(small[:, FEED_SHIFT], share),
    )


def solution(mesh):
    row, spread = P("dp", "seq", None), ("dp", "seq")
    matrix, vector = P(None, spread, None), P(None, spread)
    in_specs = (
        row,
        P("dp", "seq"),
        matrix,
        vector,
        vector,
        matrix,
        vector,
        vector,
        vector,
        matrix,
        vector,
        matrix,
        vector,
        vector,
        vector,
        row,
    )
    kept, line = P(None, "seq", None), P(None, "seq")
    out_specs = (row, row, kept, line, line, kept, line, line, line, kept, line, kept, line, line, line)
    return jax.shard_map(
        functools.partial(per_device, mesh.shape["seq"], mesh.shape["dp"]),
        mesh=mesh,
        in_specs=in_specs,
        out_specs=out_specs,
        check_vma=False,
    )
```

```python
import functools
import math

import jax
import jax.numpy as jnp
from jax import lax
from jax.experimental import pallas as pl
from jax.experimental.pallas import tpu as pltpu
from jax.sharding import PartitionSpec as P

HEADS = 12
HEAD_DIM = 64
LAYERS = 2
EPSILON = 1e-12
MASKED = -2.0e9
LOWEST = -1.0e9
SCALE = HEAD_DIM**-0.5
BF16 = jnp.bfloat16
F32 = jnp.float32
VMEM_LIMIT = 58 * 1024 * 1024
RSQRT2 = 0.7071067811865476
PDF_SCALE = 0.3989422804014327


def nn(a, b):
    return lax.dot_general(a, b, (((1,), (0,)), ((), ())), preferred_element_type=F32)


def nt(a, b):
    return lax.dot_general(a, b, (((1,), (1,)), ((), ())), preferred_element_type=F32)


def tn(a, b):
    return lax.dot_general(a, b, (((0,), (0,)), ((), ())), preferred_element_type=F32)


def exchange(value, axis, size, mask):
    return lax.ppermute(value, axis, [(i, i ^ mask) for i in range(size)])


def resident(shape):
    return pl.BlockSpec(shape, lambda *unused: (0,) * len(shape))


def column_spec(width, first, step=1):
    return pl.BlockSpec((width, width), lambda j: (0, first + step * j))


def down_spec(width, pieces):
    return pl.BlockSpec((width // pieces, pieces * width), lambda j: (j, 0))


def load_down(target, block, pieces, depth):
    if pieces == 1:
        target[...] = block[...]
        return
    width = target.shape[1]
    rows = block[...].astype(F32)
    parts = [
        rows[d * depth : (d + 1) * depth, t * width : (t + 1) * width]
        for d in range(rows.shape[0] // depth)
        for t in range(pieces)
    ]
    target[...] = jnp.concatenate(parts, axis=0).astype(BF16)


def params(count=1):
    return pltpu.CompilerParams(
        dimension_semantics=("arbitrary",) * count, vmem_limit_bytes=VMEM_LIMIT
    )


SMEM_SPEC = pl.BlockSpec(memory_space=pltpu.SMEM)
ANY_SPEC = pl.BlockSpec(memory_space=pl.ANY)


def project_body(groups, span, order, x_ref, w_ref, b_ref, *rest):
    outs, flipped = rest[:groups], rest[groups]
    rows = nn(x_ref[...].astype(BF16), w_ref[...]) + b_ref[0]
    flipped[...] = rows.T.astype(BF16)
    for r in range(groups):
        start = pl.multiple_of(order[r] * span, span)
        outs[r][0] = flipped[pl.ds(start, span), :]


def project(order, rows, weight, bias, groups):
    weight, first = weight
    tokens, width = rows.shape
    span = width // groups
    return pl.pallas_call(
        functools.partial(project_body, groups, span),
        out_shape=[jax.ShapeDtypeStruct((3, span, tokens), BF16)] * groups,
        grid=(3,),
        in_specs=[
            SMEM_SPEC,
            resident((tokens, width)),
            column_spec(width, first),
            pl.BlockSpec((1, 1, width), lambda j: (j, 0, 0)),
        ],
        out_specs=[pl.BlockSpec((1, span, tokens), lambda j: (j, 0, 0))] * groups,
        scratch_shapes=[pltpu.VMEM((width, tokens), BF16)],
        compiler_params=params(),
        cost_estimate=pl.CostEstimate(
            flops=6 * tokens * width * width, bytes_accessed=6 * width * width, transcendentals=0
        ),
        name="project",
    )(order, rows, weight, bias)


def load_stack(parts, stack, sems):
    copies = [pltpu.make_async_copy(part, stack.at[i], sems.at[i]) for i, part in enumerate(parts)]
    for copy in copies:
        copy.start()
    for copy in copies:
        copy.wait()


def attend_body(groups, members, heads, active, seg_row, seg_col, *rest):
    count = groups * members
    parts, rest = rest[:count], rest[count:]
    outs, rest = rest[:groups], rest[groups:]
    exact, log_total, stack, top, total, gathered, sems = rest
    load_stack(parts, stack, sems)
    tokens = stack.shape[-1]

    def one_block(r, unused):
        seg_query = seg_row[r]
        top[...] = jnp.full_like(top, LOWEST)
        total[...] = jnp.zeros_like(total)
        gathered[...] = jnp.zeros_like(gathered)

        def one_key(kb, unused):
            @pl.when(active[r, kb] != 0)
            def _():
                allowed = jnp.broadcast_to(seg_col[kb], (tokens, tokens)) == seg_query
                for h in range(heads):
                    part = pl.ds(h * HEAD_DIM, HEAD_DIM)
                    query = stack[r, 0, part, :] * SCALE
                    scores = tn(stack[kb, 1, part, :], query.astype(BF16))
                    scores = jnp.where(allowed, scores, MASKED)
                    old = top[h]
                    new = jnp.maximum(old, jnp.max(scores, axis=0, keepdims=True))
                    weights = jnp.exp(scores - new)
                    fade = jnp.exp(old - new)
                    total[h] = total[h] * fade + jnp.sum(weights, axis=0, keepdims=True)
                    top[h] = new
                    gathered[h] = gathered[h] * fade + nn(
                        stack[kb, 2, part, :], weights.astype(BF16)
                    )

            return unused

        lax.fori_loop(0, count, one_key, 0)
        for h in range(heads):
            exact[r, pl.ds(h * HEAD_DIM, HEAD_DIM), :] = gathered[h] / total[h]
            log_total[r, h] = top[h] + jnp.log(total[h])
        return unused

    lax.fori_loop(0, groups, one_block, 0)
    for r in range(groups):
        outs[r][...] = exact[r].astype(BF16)


def attend(active, seg_row, seg_col, parts, groups, members):
    unused, span, tokens = parts[0].shape
    heads = span // HEAD_DIM
    count = groups * members
    return pl.pallas_call(
        functools.partial(attend_body, groups, members, heads),
        out_shape=[jax.ShapeDtypeStruct((span, tokens), BF16)] * groups
        + [
            jax.ShapeDtypeStruct((groups, span, tokens), F32),
            jax.ShapeDtypeStruct((groups, heads, 1, tokens), F32),
        ],
        in_specs=[SMEM_SPEC, resident(seg_row.shape), resident(seg_col.shape)]
        + [ANY_SPEC] * count,
        out_specs=[resident((span, tokens))] * groups
        + [resident((groups, span, tokens)), resident((groups, heads, 1, tokens))],
        grid=(1,),
        scratch_shapes=[
            pltpu.VMEM((count, 3, span, tokens), BF16),
            pltpu.VMEM((heads, 1, tokens), F32),
            pltpu.VMEM((heads, 1, tokens), F32),
            pltpu.VMEM((heads, HEAD_DIM, tokens), F32),
            pltpu.SemaphoreType.DMA((count,)),
        ],
        compiler_params=params(),
        cost_estimate=pl.CostEstimate(
            flops=2 * span * groups * count * tokens * tokens,
            bytes_accessed=10 * span * tokens * count,
            transcendentals=heads * groups * count * tokens * tokens // 2,
        ),
        name="attend",
    )(active, seg_row, seg_col, *parts)


def attend_back_body(groups, members, heads, active, seg_row, seg_col, *rest):
    count = groups * members
    parts, rest = rest[:count], rest[count:]
    grads, rest = rest[:groups], rest[groups:]
    exact, log_total, rest = rest[0], rest[1], rest[2:]
    out_query, out_own, rest = rest[0], rest[1], rest[2:]
    out_send, rest = rest[: members - 1], rest[members - 1 :]
    stack, grad_stack, delta, grad_query, grad_kv, sems = rest
    load_stack(parts, stack, sems)
    tokens = stack.shape[-1]
    for r in range(groups):
        grad_stack[r] = grads[r][...]
    grad_kv[...] = jnp.zeros_like(grad_kv)

    def one_block(r, unused):
        seg_query = seg_row[r]
        grad_query[...] = jnp.zeros_like(grad_query)
        for h in range(heads):
            part = pl.ds(h * HEAD_DIM, HEAD_DIM)
            delta[h] = jnp.sum(
                grad_stack[r, part, :].astype(F32) * exact[r, part, :], axis=0, keepdims=True
            )

        def one_key(kb, unused):
            @pl.when(active[r, kb] != 0)
            def _():
                allowed = jnp.broadcast_to(seg_col[kb], (tokens, tokens)) == seg_query
                for h in range(heads):
                    part = pl.ds(h * HEAD_DIM, HEAD_DIM)
                    query = (stack[r, 0, part, :] * SCALE).astype(BF16)
                    grad = grad_stack[r, part, :]
                    keys = stack[kb, 1, part, :]
                    scores = jnp.where(allowed, tn(keys, query), MASKED)
                    weights = jnp.exp(scores - log_total[r, h])
                    grad_kv[kb, 1, part, :] += nt(grad, weights.astype(BF16))
                    grad_weights = tn(stack[kb, 2, part, :], grad)
                    grad_scores = (weights * (grad_weights - delta[h])).astype(BF16)
                    grad_kv[kb, 0, part, :] += nt(query, grad_scores)
                    grad_query[part, :] += nn(keys, grad_scores)

            return unused

        lax.fori_loop(0, count, one_key, 0)
        out_query[r] = (grad_query[...] * SCALE).astype(BF16)
        return unused

    lax.fori_loop(0, groups, one_block, 0)
    out_own[...] = grad_kv[:groups]
    for j in range(1, members):
        out_send[j - 1][...] = grad_kv[j * groups : (j + 1) * groups].astype(BF16)


def attend_back(active, seg_row, seg_col, parts, grads, exact, log_total, groups, members):
    unused, span, tokens = parts[0].shape
    heads = span // HEAD_DIM
    count = groups * members
    kv_shape = (groups, 2, span, tokens)
    return pl.pallas_call(
        functools.partial(attend_back_body, groups, members, heads),
        out_shape=[
            jax.ShapeDtypeStruct((groups, span, tokens), BF16),
            jax.ShapeDtypeStruct(kv_shape, F32),
        ]
        + [jax.ShapeDtypeStruct(kv_shape, BF16)] * (members - 1),
        in_specs=[SMEM_SPEC, resident(seg_row.shape), resident(seg_col.shape)]
        + [ANY_SPEC] * count
        + [resident((span, tokens))] * groups
        + [resident(exact.shape), resident(log_total.shape)],
        out_specs=[resident((groups, span, tokens)), resident(kv_shape)]
        + [resident(kv_shape)] * (members - 1),
        grid=(1,),
        scratch_shapes=[
            pltpu.VMEM((count, 3, span, tokens), BF16),
            pltpu.VMEM((groups, span, tokens), BF16),
            pltpu.VMEM((heads, 1, tokens), F32),
            pltpu.VMEM((span, tokens), F32),
            pltpu.VMEM((count, 2, span, tokens), F32),
            pltpu.SemaphoreType.DMA((count,)),
        ],
        compiler_params=params(),
        cost_estimate=pl.CostEstimate(
            flops=5 * span * groups * count * tokens * tokens,
            bytes_accessed=20 * span * tokens * count,
            transcendentals=heads * groups * count * tokens * tokens // 2,
        ),
        name="attend_back",
    )(active, seg_row, seg_col, *parts, *grads, exact, log_total)


OUT_BIAS, ATT_GAIN, ATT_SHIFT, DOWN_BIAS, FEED_GAIN, FEED_SHIFT = range(6)
SMALL_ROWS, SMALL_UP, SMALL_PROJECT = 16, 8, 12


def normalized(rows):
    centre = rows - jnp.mean(rows, axis=-1, keepdims=True)
    spread = jnp.mean(centre * centre, axis=-1, keepdims=True)
    inverse = lax.rsqrt(spread + EPSILON)
    return centre * inverse, inverse


def norm_back(grad, gain, normal, inverse):
    scaled = grad * gain
    mean_scaled = jnp.mean(scaled, axis=-1, keepdims=True)
    mean_both = jnp.mean(scaled * normal, axis=-1, keepdims=True)
    return inverse * (scaled - mean_scaled - normal * mean_both)


def feed_body(
    groups, span, blocks, pieces, depth, order, x_ref, wo_ref, wu_ref, wd_ref, vec, ub_ref, *rest
):
    contexts, rest = rest[:groups], rest[groups:]
    sum_first, hidden_low, sum_second, out, hidden, outward, down = rest
    j = pl.program_id(0)

    @pl.when(j == 0)
    def _():
        rows = x_ref[...] + vec[OUT_BIAS : OUT_BIAS + 1, :]
        for r in range(groups):
            start = pl.multiple_of(order[r] * span, span)
            rows += tn(contexts[r][...], wo_ref[pl.ds(start, span), :])
        sum_first[...] = rows
        normal, unused = normalized(rows)
        value = normal * vec[ATT_GAIN : ATT_GAIN + 1, :] + vec[ATT_SHIFT : ATT_SHIFT + 1, :]
        hidden[...] = value
        hidden_low[...] = value.astype(BF16)
        outward[...] = jnp.zeros_like(outward)

    inner = nn(hidden_low[...], wu_ref[...]) + ub_ref[0]
    activated = (0.5 * inner * (1.0 + lax.erf(inner * RSQRT2))).astype(BF16)
    load_down(down, wd_ref, pieces, depth)
    outward[...] += nn(activated, down[...])

    @pl.when(j == blocks - 1)
    def _():
        rows = hidden[...] + outward[...] + vec[DOWN_BIAS : DOWN_BIAS + 1, :]
        sum_second[...] = rows
        normal, unused = normalized(rows)
        out[...] = normal * vec[FEED_GAIN : FEED_GAIN + 1, :] + vec[FEED_SHIFT : FEED_SHIFT + 1, :]


def feed(order, rows, w_output, w_up, w_down, vectors, up_bias, contexts):
    (w_output, at_output), (w_up, at_up), (w_down, pieces, depth) = w_output, w_up, w_down
    tokens, width = rows.shape
    groups, span = len(contexts), contexts[0].shape[0]
    blocks = up_bias.shape[0]
    full = jax.ShapeDtypeStruct((tokens, width), F32)
    return pl.pallas_call(
        functools.partial(feed_body, groups, span, blocks, pieces, depth),
        out_shape=[full, jax.ShapeDtypeStruct((tokens, width), BF16), full, full],
        grid=(blocks,),
        in_specs=[
            SMEM_SPEC,
            resident((tokens, width)),
            column_spec(width, at_output, 0),
            column_spec(width, at_up),
            down_spec(width, pieces),
            resident(vectors.shape),
            pl.BlockSpec((1, 1, width), lambda j: (j, 0, 0)),
        ]
        + [resident((span, tokens))] * groups,
        out_specs=[resident((tokens, width))] * 4,
        scratch_shapes=[pltpu.VMEM((tokens, width), F32)] * 2 + [pltpu.VMEM((width, width), BF16)],
        compiler_params=params(),
        cost_estimate=pl.CostEstimate(
            flops=(4 * blocks + 2) * tokens * width * width,
            bytes_accessed=(4 * blocks + 2) * width * width,
            transcendentals=0,
        ),
        name="feed",
    )(order, rows, w_output, w_up, w_down, vectors, up_bias, *contexts)


def feed_back_body(
    groups,
    span,
    blocks,
    devices,
    pieces,
    depth,
    order,
    grad_ref,
    first_ref,
    second_ref,
    low_ref,
    *rest
):
    wo_ref, wu_ref, wd_ref, vec, ub_ref = rest[:5]
    contexts, rest = rest[5 : 5 + groups], rest[5 + groups :]
    shares, grad_first, small = rest[:3]
    grad_contexts, rest = rest[3 : 3 + groups], rest[3 + groups :]
    grad_out, grad_hidden, tile, down = rest
    width = vec.shape[-1]
    j = pl.program_id(0)
    share = width // devices
    down_share = blocks * share
    per_block = width // down_share

    @pl.when(j == 0)
    def _():
        small[...] = jnp.zeros_like(small)
        grad = grad_ref[...]
        normal, inverse = normalized(second_ref[...])
        value = norm_back(grad, vec[FEED_GAIN : FEED_GAIN + 1, :], normal, inverse)
        grad_hidden[...] = value
        low = value.astype(BF16)
        grad_out[...] = low
        small[DOWN_BIAS : DOWN_BIAS + 1, :] = jnp.sum(low.astype(F32), axis=0, keepdims=True)
        small[FEED_GAIN : FEED_GAIN + 1, :] = jnp.sum(grad * normal, axis=0, keepdims=True)
        small[FEED_SHIFT : FEED_SHIFT + 1, :] = jnp.sum(grad, axis=0, keepdims=True)

    inner = nn(low_ref[...], wu_ref[...]) + ub_ref[0]
    below = 0.5 * (1.0 + lax.erf(inner * RSQRT2))
    activated = (inner * below).astype(BF16)
    slope = below + inner * (PDF_SCALE * jnp.exp(-0.5 * inner * inner))
    load_down(down, wd_ref, pieces, depth)
    grad_inner = (nt(grad_out[...], down[...]) * slope).astype(BF16)
    small[pl.ds(SMALL_UP + j, 1), :] = jnp.sum(grad_inner.astype(F32), axis=0, keepdims=True)
    grad_hidden[...] += nt(grad_inner, wu_ref[...])

    product = tn(activated, grad_out[...]).astype(BF16)
    for k in range(per_block):
        shares[j * per_block + k, pl.ds(0, down_share), :] = product[
            k * down_share : (k + 1) * down_share, :
        ]
    product = tn(low_ref[...], grad_inner).astype(BF16)
    base = pl.multiple_of(down_share + j * share, share)
    for i in range(devices):
        shares[i, pl.ds(base, share), :] = product[i * share : (i + 1) * share, :]

    @pl.when(j == blocks - 1)
    def _():
        grad = grad_hidden[...]
        normal, inverse = normalized(first_ref[...])
        value = norm_back(grad, vec[ATT_GAIN : ATT_GAIN + 1, :], normal, inverse)
        grad_first[...] = value
        low = value.astype(BF16)
        small[OUT_BIAS : OUT_BIAS + 1, :] = jnp.sum(low.astype(F32), axis=0, keepdims=True)
        small[ATT_GAIN : ATT_GAIN + 1, :] = jnp.sum(grad * normal, axis=0, keepdims=True)
        small[ATT_SHIFT : ATT_SHIFT + 1, :] = jnp.sum(grad, axis=0, keepdims=True)
        for r in range(groups):
            start = pl.multiple_of(order[r] * span, span)
            tile[pl.ds(start, span), :] = nn(contexts[r][...], low).astype(BF16)
            grad_contexts[r][...] = nt(wo_ref[pl.ds(start, span), :], low).astype(BF16)
        last = down_share + blocks * share
        for i in range(devices):
            shares[i, last : last + share, :] = tile[i * share : (i + 1) * share, :]


def feed_back(
    order, grad, first, second, low, w_output, w_up, w_down, vectors, up_bias, contexts, devices
):
    (w_output, at_output), (w_up, at_up), (w_down, pieces, depth) = w_output, w_up, w_down
    tokens, width = grad.shape
    groups, span = len(contexts), contexts[0].shape[0]
    blocks = up_bias.shape[0]
    share = width // devices
    kept = (devices, (2 * blocks + 1) * share, width)
    return pl.pallas_call(
        functools.partial(feed_back_body, groups, span, blocks, devices, pieces, depth),
        out_shape=[
            jax.ShapeDtypeStruct(kept, BF16),
            jax.ShapeDtypeStruct((tokens, width), F32),
            jax.ShapeDtypeStruct((SMALL_ROWS, width), F32),
        ]
        + [jax.ShapeDtypeStruct((span, tokens), BF16)] * groups,
        grid=(blocks,),
        in_specs=[SMEM_SPEC]
        + [resident((tokens, width))] * 4
        + [
            column_spec(width, at_output, 0),
            column_spec(width, at_up),
            down_spec(width, pieces),
            resident(vectors.shape),
            pl.BlockSpec((1, 1, width), lambda j: (j, 0, 0)),
        ]
        + [resident((span, tokens))] * groups,
        out_specs=[resident(kept), resident((tokens, width)), resident((SMALL_ROWS, width))]
        + [resident((span, tokens))] * groups,
        scratch_shapes=[
            pltpu.VMEM((tokens, width), BF16),
            pltpu.VMEM((tokens, width), F32),
            pltpu.VMEM((width, width), BF16),
            pltpu.VMEM((width, width), BF16),
        ],
        compiler_params=params(),
        cost_estimate=pl.CostEstimate(
            flops=(10 * blocks + 4) * tokens * width * width,
            bytes_accessed=(8 * blocks + 4) * width * width,
            transcendentals=0,
        ),
        name="feed_back",
    )(
        order,
        grad,
        first,
        second,
        low,
        w_output,
        w_up,
        w_down,
        vectors,
        up_bias,
        *contexts,
    )


def project_back_body(groups, span, devices, order, place, x_ref, grad_ref, w_ref, small_ref, *rest):
    pieces, rest = rest[:groups], rest[groups:]
    own, send, out, small, joined, tile = rest
    width = out.shape[1]
    me = place[0]
    j = pl.program_id(0)
    share = width // devices

    @pl.when(j == 0)
    def _():
        out[...] = grad_ref[...]
        small[...] = small_ref[...]

    for r in range(groups):
        start = pl.multiple_of(order[r] * span, span)
        joined[pl.ds(start, span), :] = pieces[r][0]
    grad = joined[...].T
    small[pl.ds(SMALL_PROJECT + j, 1), :] = jnp.sum(grad.astype(F32), axis=0, keepdims=True)
    out[...] += nt(grad, w_ref[...])
    tile[...] = tn(x_ref[...].astype(BF16), grad).astype(BF16)
    for i in range(devices // 2):
        for bit, target in ((0, own), (1, send)):
            start = pl.multiple_of((me ^ (2 * i + bit)) * share, share)
            base = pl.multiple_of(j * share, share)
            target[i, pl.ds(base, share), :] = tile[pl.ds(start, share), :]

    @pl.when(j == 2)
    def _():
        rows = jnp.concatenate([small[...], jnp.zeros_like(small)], axis=0).astype(BF16)
        for i in range(devices // 2):
            for target in (own, send):
                target[i, 3 * share :, :] = rows


def project_back(order, place, rows, grad, weight, small, pieces, devices):
    weight, first = weight
    tokens, width = rows.shape
    groups, span = len(pieces), pieces[0].shape[1]
    kept = (devices // 2, 3 * (width // devices) + 2 * SMALL_ROWS, width)
    return pl.pallas_call(
        functools.partial(project_back_body, groups, span, devices),
        out_shape=[
            jax.ShapeDtypeStruct(kept, BF16),
            jax.ShapeDtypeStruct(kept, BF16),
            jax.ShapeDtypeStruct((tokens, width), F32),
        ],
        grid=(3,),
        in_specs=[
            SMEM_SPEC,
            SMEM_SPEC,
            resident((tokens, width)),
            resident((tokens, width)),
            column_spec(width, first),
            resident((SMALL_ROWS, width)),
        ]
        + [pl.BlockSpec((1, span, tokens), lambda j: (j, 0, 0))] * groups,
        out_specs=[resident(kept), resident(kept), resident((tokens, width))],
        scratch_shapes=[
            pltpu.VMEM((SMALL_ROWS, width), F32),
            pltpu.VMEM((width, tokens), BF16),
            pltpu.VMEM((width, width), BF16),
        ],
        compiler_params=params(),
        cost_estimate=pl.CostEstimate(
            flops=12 * tokens * width * width, bytes_accessed=12 * width * width, transcendentals=0
        ),
        name="project_back",
    )(order, place, rows, grad, weight, small, *pieces)


class Stream:
    def __init__(self, steps):
        self.steps, self.result, self.flying = steps, None, None
        self.resume(None)

    def resume(self, arrived):
        try:
            self.flying = self.steps.send(arrived)
        except StopIteration as stop:
            self.flying, self.result = None, stop.value


def tick(streams, values=()):
    streams = [item for item in streams if item.flying is not None]
    values, flying = lax.optimization_barrier((values, [item.flying for item in streams]))
    for item, arrived in zip(streams, flying):
        item.resume(arrived)
    return values


def sum_steps(own, send, devices, dp_size, dp_me):
    (arrived,) = yield [exchange(send, "seq", devices, 1)]
    rows, width = own.shape[1:]
    cut = rows // 2
    bits = int(math.log2(devices)) - 1
    masks = [2 << b for b in range(bits)]
    orders = (masks, masks[::-1])
    axes = [masks[::-1], masks[::-1]]
    kept = [
        add_low(own[:, part], arrived[:, part]).reshape((2,) * bits + (-1, width))
        for part in (slice(0, cut), slice(cut, rows))
    ]
    for step in range(bits):
        stay, leave = [], []
        for k in range(2):
            mask = orders[k][step]
            at = axes[k].index(mask)
            axes[k] = [m for m in axes[k] if m != mask]
            stay.append(lax.index_in_dim(kept[k], 0, at, keepdims=False))
            leave.append(
                exchange(lax.index_in_dim(kept[k], 1, at, keepdims=False), "seq", devices, mask)
            )
        leave = yield leave
        kept = [add_low(a, b) for a, b in zip(stay, leave)]
    total = jnp.concatenate(kept, axis=0)
    return (yield from dp_steps(total, dp_size, dp_me))


def dp_steps(total, dp_size, dp_me):
    rows, width = total.shape
    if dp_size != 4:
        return lax.psum(total, "dp")
    pieces = total.reshape(dp_size, rows // dp_size, width)

    def piece(m):
        return lax.dynamic_index_in_dim(pieces, dp_me ^ m, 0, keepdims=False)

    arrived = yield [exchange(piece(m), "dp", dp_size, m) for m in range(1, dp_size)]
    mine = sum((item.astype(F32) for item in arrived), piece(0).astype(F32)).astype(BF16)
    arrived = yield [exchange(mine, "dp", dp_size, m) for m in range(1, dp_size)]
    stack = [mine] + list(arrived)
    for bit in (1, 2):
        flip = (dp_me & bit) != 0
        stack = [jnp.where(flip, stack[i ^ bit], stack[i]) for i in range(dp_size)]
    return jnp.concatenate(stack, axis=0)


def add_low(a, b):
    return (a.astype(F32) + b.astype(F32)).astype(BF16)


def per_device(
    seq_size,
    dp_size,
    states,
    segment_ids,
    project_weight,
    query_bias,
    value_bias,
    output_weight,
    output_bias,
    attention_gain,
    attention_shift,
    up_weight,
    up_bias,
    down_weight,
    down_bias,
    feed_gain,
    feed_shift,
    cotangent,
):
    unused, tokens, width = states.shape
    groups = math.gcd(HEADS, seq_size)
    members = seq_size // groups
    share = width // seq_size
    inner_width = up_weight.shape[2]
    blocks = inner_width // width
    depth = width // (seq_size * dp_size)
    everyone = seq_size * dp_size
    me = lax.axis_index("seq")
    dp_me = lax.axis_index("dp")
    order = (me // members) ^ jnp.arange(groups, dtype=jnp.int32)
    place = me.reshape(1).astype(jnp.int32)
    both = ("dp", "seq")
    plain = depth % 8 != 0 or dp_size != 4

    vectors = jnp.stack(
        [
            output_bias,
            attention_gain,
            attention_shift,
            down_bias,
            feed_gain,
            feed_shift,
            query_bias,
            value_bias,
        ],
        axis=1,
    )
    flat = jnp.concatenate(
        [vectors.reshape(-1), up_bias.reshape(-1), segment_ids.astype(BF16).reshape(-1)]
    )
    used = flat.shape[0]
    flat = jnp.pad(flat, (0, -used % 1024)).reshape(-1, 128)

    def swap_groups(items):
        return [items[0]] + [
            exchange(items[r], "seq", seq_size, r * members) for r in range(1, groups)
        ]

    def with_members(items):
        items = list(items)
        own = list(items)
        for j in range(1, members):
            items += [exchange(item, "seq", seq_size, j) for item in own]
        return items

    def gathered(shard):
        return lax.all_gather(shard, both, axis=0, tiled=True)

    def rest_shard(layer):
        down = down_weight[layer].reshape(blocks, depth, width)
        return [down[t] for t in range(blocks)] + [up_weight[layer], output_weight[layer]]

    def rest_of(whole):
        return (whole, 2 * blocks), (whole, blocks), (whole, blocks, depth)

    if plain:
        table = lax.all_gather(flat, both, axis=0, tiled=False)
        w_project = [(gathered(project_weight[layer]), 0) for layer in range(LAYERS)]
        w_rest = [
            (
                (gathered(output_weight[layer]), 0),
                (gathered(up_weight[layer]), 0),
                (gathered(down_weight[layer]), 1, depth),
            )
            for layer in range(LAYERS)
        ]
    else:
        extra = jnp.pad(flat.reshape(-1), (0, depth * 128 - flat.size)).reshape(depth, 128)
        first = gathered(jnp.concatenate([project_weight[0], extra], axis=1))
        table = first[:, 3 * width :]
        w_project, w_rest = [(first, 0)], []
        for layer in range(LAYERS):
            parts = rest_shard(layer)
            if layer + 1 < LAYERS:
                parts.append(project_weight[layer + 1])
            whole = gathered(jnp.concatenate(parts, axis=1))
            w_rest.append(rest_of(whole))
            w_project.append((whole, 2 * blocks + 1))

    table = table.reshape(everyone, -1)
    small_rows = LAYERS * 8 * depth
    up_share = inner_width // everyone
    vectors = (
        table[:, :small_rows]
        .reshape(everyone, LAYERS, 8, depth)
        .transpose(1, 2, 0, 3)
        .reshape(LAYERS, 8, width)
        .astype(F32)
    )
    up_biases = (
        table[:, small_rows : small_rows + LAYERS * up_share]
        .reshape(everyone, LAYERS, up_share)
        .transpose(1, 0, 2)
        .reshape(LAYERS, blocks, 1, width)
        .astype(F32)
    )
    relative = jnp.array([r * members + j for j in range(members) for r in range(groups)], jnp.int32)
    segments = jnp.take(
        table[:, used - tokens : used], dp_me * seq_size + (me ^ relative), axis=0
    ).astype(jnp.int32)
    first_id, last_id = segments[:, 0], segments[:, -1]
    active = (
        (first_id[:groups, None] <= last_id[None, :])
        & (first_id[None, :] <= last_id[:groups, None])
    ).astype(jnp.int32)
    seg_row = segments[:groups, None, :]
    seg_col = segments[:, :, None]

    def projected(layer, current):
        vec = vectors[layer]
        bias = jnp.stack([vec[6], jnp.zeros_like(vec[6]), vec[7]])[:, None, :]
        return project(order, current, w_project[layer], bias, groups)

    current = states[0].astype(F32)
    saved = []
    for layer in range(LAYERS):
        made = projected(layer, current)
        parts = with_members(swap_groups(made))
        *mixed, exact, log_total = attend(active, seg_row, seg_col, parts, groups, members)
        contexts = swap_groups(mixed)
        w_output, w_up, w_down = w_rest[layer]
        sum_first, low, sum_second, following = feed(
            order,
            current,
            w_output,
            w_up,
            w_down,
            vectors[layer],
            up_biases[layer],
            contexts,
        )
        saved.append((current, parts, exact, log_total, contexts, sum_first, low, sum_second))
        current = following
    output = current.astype(BF16)[None]

    grad = cotangent[0].astype(F32)
    shares, feeds, backs = [None] * LAYERS, [None] * LAYERS, [None] * LAYERS
    behind = []
    for layer in reversed(range(LAYERS)):
        w_output, w_up, w_down = w_rest[layer]
        entered, parts, exact, log_total, contexts, sum_first, low, sum_second = saved[layer]
        terms, grad_first, small, *grad_mixed = feed_back(
            order,
            grad,
            sum_first,
            sum_second,
            low,
            w_output,
            w_up,
            w_down,
            vectors[layer],
            up_biases[layer],
            contexts,
            seq_size,
        )
        shares[layer] = lax.psum_scatter(
            terms.reshape(-1, width), "seq", scatter_dimension=0, tiled=True
        )
        grad_mixed = tick(behind, tuple(grad_mixed))
        grads = tuple(swap_groups(grad_mixed))
        grads = tick(behind, grads)
        grad_query, kept_kv, *sent_kv = attend_back(
            active, seg_row, seg_col, parts, grads, exact, log_total, groups, members
        )
        for j in range(1, members):
            kept_kv = kept_kv + exchange(sent_kv[j - 1], "seq", seq_size, j).astype(F32)
        messages = [
            jnp.concatenate([grad_query[r][None], kept_kv[r].astype(BF16)], axis=0)
            for r in range(groups)
        ]
        if layer + 1 < LAYERS:
            messages, later = lax.optimization_barrier((tuple(messages), shares[layer + 1]))
            feeds[layer + 1] = Stream(dp_steps(later, dp_size, dp_me))
        messages = tick(behind, tuple(messages))
        behind += [item for item in feeds if item is not None]
        pieces = tuple(swap_groups(messages))
        pieces = tick(behind, pieces)
        own, send, grad = project_back(
            order, place, entered, grad_first, w_project[layer], small, pieces, seq_size
        )
        backs[layer] = Stream(sum_steps(own, send, seq_size, dp_size, dp_me))
        behind = behind + [backs[layer]]
    tick(behind)
    tick(behind)
    feeds[0] = Stream(dp_steps(shares[0], dp_size, dp_me))
    behind = behind + [feeds[0]]
    while any(item.flying is not None for item in behind):
        tick(behind)
    small = jnp.stack(
        [backs[layer].result[3 * share : 3 * share + SMALL_ROWS] for layer in range(LAYERS)]
    ).astype(F32)
    results = [(feeds[layer].result, backs[layer].result) for layer in range(LAYERS)]

    def mine(rows, size):
        return lax.dynamic_slice_in_dim(rows, me * size, size, axis=1)

    def columns(part, which):
        return jnp.concatenate([part[i * share : (i + 1) * share] for i in which], axis=1).astype(F32)

    down_rows = blocks * share
    g_project = jnp.stack([columns(item[1], range(3)) for item in results])
    g_up = jnp.stack([columns(item[0], range(blocks, 2 * blocks)) for item in results])
    g_down = jnp.stack([item[0][:down_rows].astype(F32) for item in results])
    g_output = jnp.stack([item[0][down_rows + blocks * share :].astype(F32) for item in results])
    wide = small[:, SMALL_UP : SMALL_UP + blocks].reshape(LAYERS, blocks * width)
    return (
        output,
        grad[None],
        g_project,
        mine(small[:, SMALL_PROJECT], share),
        mine(small[:, SMALL_PROJECT + 2], share),
        g_output,
        mine(small[:, OUT_BIAS], share),
        mine(small[:, ATT_GAIN], share),
        mine(small[:, ATT_SHIFT], share),
        g_up,
        mine(wide, blocks * share),
        g_down,
        mine(small[:, DOWN_BIAS], share),
        mine(small[:, FEED_GAIN], share),
        mine(small[:, FEED_SHIFT], share),
    )


def solution(mesh):
    row, spread = P("dp", "seq", None), ("dp", "seq")
    matrix, vector = P(None, spread, None), P(None, spread)
    in_specs = (
        row,
        P("dp", "seq"),
        matrix,
        vector,
        vector,
        matrix,
        vector,
        vector,
        vector,
        matrix,
        vector,
        matrix,
        vector,
        vector,
        vector,
        row,
    )
    kept, line = P(None, "seq", None), P(None, "seq")
    out_specs = (row, row, kept, line, line, kept, line, line, line, kept, line, kept, line, line, line)
    return jax.shard_map(
        functools.partial(per_device, mesh.shape["seq"], mesh.shape["dp"]),
        mesh=mesh,
        in_specs=in_specs,
        out_specs=out_specs,
        check_vma=False,
    )
```

```python
import functools
import math

import jax
import jax.numpy as jnp
from jax import lax
from jax.experimental import pallas as pl
from jax.experimental.pallas import tpu as pltpu
from jax.sharding import PartitionSpec as P

HEADS = 12
HEAD_DIM = 64
LAYERS = 2
EPSILON = 1e-12
MASKED = -2.0e9
LOWEST = -1.0e9
SCALE = HEAD_DIM**-0.5
BF16 = jnp.bfloat16
F32 = jnp.float32
VMEM_LIMIT = 58 * 1024 * 1024
RSQRT2 = 0.7071067811865476
PDF_SCALE = 0.3989422804014327


def nn(a, b):
    return lax.dot_general(a, b, (((1,), (0,)), ((), ())), preferred_element_type=F32)


def nt(a, b):
    return lax.dot_general(a, b, (((1,), (1,)), ((), ())), preferred_element_type=F32)


def tn(a, b):
    return lax.dot_general(a, b, (((0,), (0,)), ((), ())), preferred_element_type=F32)


def exchange(value, axis, size, mask):
    return lax.ppermute(value, axis, [(i, i ^ mask) for i in range(size)])


def resident(shape):
    return pl.BlockSpec(shape, lambda *unused: (0,) * len(shape))


def column_spec(width, first, step=1):
    return pl.BlockSpec((width, width), lambda j: (0, first + step * j))


def down_spec(width, pieces):
    return pl.BlockSpec((width // pieces, pieces * width), lambda j: (j, 0))


def load_down(target, block, pieces, depth):
    if pieces == 1:
        target[...] = block[...]
        return
    width = target.shape[1]
    rows = block[...].astype(F32)
    parts = [
        rows[d * depth : (d + 1) * depth, t * width : (t + 1) * width]
        for d in range(rows.shape[0] // depth)
        for t in range(pieces)
    ]
    target[...] = jnp.concatenate(parts, axis=0).astype(BF16)


def params(count=1):
    return pltpu.CompilerParams(
        dimension_semantics=("arbitrary",) * count, vmem_limit_bytes=VMEM_LIMIT
    )


SMEM_SPEC = pl.BlockSpec(memory_space=pltpu.SMEM)
ANY_SPEC = pl.BlockSpec(memory_space=pl.ANY)


def pack_body(weight, *rest):
    items, (out, extra) = rest[:-2], rest[-2:]
    width = weight.shape[2]
    extra[...] = jnp.zeros_like(extra)
    at = 0
    for item in items:
        rows = item[...].astype(F32)
        for first in range(0, rows.shape[1], 128):
            part = rows[:, first : first + 128]
            extra[at : at + part.shape[0], : part.shape[1]] = part
            at += part.shape[0]
    out[:, :width] = weight[0]
    out[:, width:] = extra[...].astype(BF16)


def pack(weights, items):
    depth, width = weights.shape[1:]
    return pl.pallas_call(
        pack_body,
        out_shape=jax.ShapeDtypeStruct((depth, width + 128), BF16),
        grid=(1,),
        in_specs=[pl.BlockSpec((1, depth, width), lambda j: (0, 0, 0))]
        + [resident(item.shape) for item in items],
        out_specs=resident((depth, width + 128)),
        scratch_shapes=[pltpu.VMEM((depth, 128), F32)],
        compiler_params=params(),
        name="pack",
    )(weights, *items)


def project_body(groups, span, order, x_ref, w_ref, b_ref, *rest):
    outs, flipped = rest[:groups], rest[groups]
    rows = nn(x_ref[...].astype(BF16), w_ref[...]) + b_ref[0]
    flipped[...] = rows.T.astype(BF16)
    for r in range(groups):
        start = pl.multiple_of(order[r] * span, span)
        outs[r][0] = flipped[pl.ds(start, span), :]


def project(order, rows, weight, bias, groups):
    weight, first = weight
    tokens, width = rows.shape
    span = width // groups
    return pl.pallas_call(
        functools.partial(project_body, groups, span),
        out_shape=[jax.ShapeDtypeStruct((3, span, tokens), BF16)] * groups,
        grid=(3,),
        in_specs=[
            SMEM_SPEC,
            resident((tokens, width)),
            column_spec(width, first),
            pl.BlockSpec((1, 1, width), lambda j: (j, 0, 0)),
        ],
        out_specs=[pl.BlockSpec((1, span, tokens), lambda j: (j, 0, 0))] * groups,
        scratch_shapes=[pltpu.VMEM((width, tokens), BF16)],
        compiler_params=params(),
        cost_estimate=pl.CostEstimate(
            flops=6 * tokens * width * width, bytes_accessed=6 * width * width, transcendentals=0
        ),
        name="project",
    )(order, rows, weight, bias)


def load_stack(parts, stack, sems):
    copies = [pltpu.make_async_copy(part, stack.at[i], sems.at[i]) for i, part in enumerate(parts)]
    for copy in copies:
        copy.start()
    for copy in copies:
        copy.wait()


def attend_body(groups, members, heads, active, seg_row, seg_col, *rest):
    count = groups * members
    parts, rest = rest[:count], rest[count:]
    outs, rest = rest[:groups], rest[groups:]
    exact, log_total, stack, top, total, gathered, sems = rest
    load_stack(parts, stack, sems)
    tokens = stack.shape[-1]

    def one_block(r, unused):
        seg_query = seg_row[r]
        top[...] = jnp.full_like(top, LOWEST)
        total[...] = jnp.zeros_like(total)
        gathered[...] = jnp.zeros_like(gathered)

        def one_key(kb, unused):
            @pl.when(active[r, kb] != 0)
            def _():
                allowed = jnp.broadcast_to(seg_col[kb], (tokens, tokens)) == seg_query
                for h in range(heads):
                    part = pl.ds(h * HEAD_DIM, HEAD_DIM)
                    query = stack[r, 0, part, :] * SCALE
                    scores = tn(stack[kb, 1, part, :], query.astype(BF16))
                    scores = jnp.where(allowed, scores, MASKED)
                    old = top[h]
                    new = jnp.maximum(old, jnp.max(scores, axis=0, keepdims=True))
                    weights = jnp.exp(scores - new)
                    fade = jnp.exp(old - new)
                    total[h] = total[h] * fade + jnp.sum(weights, axis=0, keepdims=True)
                    top[h] = new
                    gathered[h] = gathered[h] * fade + nn(
                        stack[kb, 2, part, :], weights.astype(BF16)
                    )

            return unused

        lax.fori_loop(0, count, one_key, 0)
        for h in range(heads):
            exact[r, pl.ds(h * HEAD_DIM, HEAD_DIM), :] = gathered[h] / total[h]
            log_total[r, h] = top[h] + jnp.log(total[h])
        return unused

    lax.fori_loop(0, groups, one_block, 0)
    for r in range(groups):
        outs[r][...] = exact[r].astype(BF16)


def attend(active, seg_row, seg_col, parts, groups, members):
    unused, span, tokens = parts[0].shape
    heads = span // HEAD_DIM
    count = groups * members
    return pl.pallas_call(
        functools.partial(attend_body, groups, members, heads),
        out_shape=[jax.ShapeDtypeStruct((span, tokens), BF16)] * groups
        + [
            jax.ShapeDtypeStruct((groups, span, tokens), F32),
            jax.ShapeDtypeStruct((groups, heads, 1, tokens), F32),
        ],
        in_specs=[SMEM_SPEC, resident(seg_row.shape), resident(seg_col.shape)]
        + [ANY_SPEC] * count,
        out_specs=[resident((span, tokens))] * groups
        + [resident((groups, span, tokens)), resident((groups, heads, 1, tokens))],
        grid=(1,),
        scratch_shapes=[
            pltpu.VMEM((count, 3, span, tokens), BF16),
            pltpu.VMEM((heads, 1, tokens), F32),
            pltpu.VMEM((heads, 1, tokens), F32),
            pltpu.VMEM((heads, HEAD_DIM, tokens), F32),
            pltpu.SemaphoreType.DMA((count,)),
        ],
        compiler_params=params(),
        cost_estimate=pl.CostEstimate(
            flops=2 * span * groups * count * tokens * tokens,
            bytes_accessed=10 * span * tokens * count,
            transcendentals=heads * groups * count * tokens * tokens // 2,
        ),
        name="attend",
    )(active, seg_row, seg_col, *parts)


def attend_back_body(groups, members, heads, active, seg_row, seg_col, *rest):
    count = groups * members
    parts, rest = rest[:count], rest[count:]
    grads, rest = rest[:groups], rest[groups:]
    exact, log_total, rest = rest[0], rest[1], rest[2:]
    out_query, out_own, rest = rest[0], rest[1], rest[2:]
    out_send, rest = rest[: members - 1], rest[members - 1 :]
    stack, grad_stack, delta, grad_query, grad_kv, sems = rest
    load_stack(parts, stack, sems)
    tokens = stack.shape[-1]
    for r in range(groups):
        grad_stack[r] = grads[r][...]
    grad_kv[...] = jnp.zeros_like(grad_kv)

    def one_block(r, unused):
        seg_query = seg_row[r]
        grad_query[...] = jnp.zeros_like(grad_query)
        for h in range(heads):
            part = pl.ds(h * HEAD_DIM, HEAD_DIM)
            delta[h] = jnp.sum(
                grad_stack[r, part, :].astype(F32) * exact[r, part, :], axis=0, keepdims=True
            )

        def one_key(kb, unused):
            @pl.when(active[r, kb] != 0)
            def _():
                allowed = jnp.broadcast_to(seg_col[kb], (tokens, tokens)) == seg_query
                for h in range(heads):
                    part = pl.ds(h * HEAD_DIM, HEAD_DIM)
                    query = (stack[r, 0, part, :] * SCALE).astype(BF16)
                    grad = grad_stack[r, part, :]
                    keys = stack[kb, 1, part, :]
                    scores = jnp.where(allowed, tn(keys, query), MASKED)
                    weights = jnp.exp(scores - log_total[r, h])
                    grad_kv[kb, 1, part, :] += nt(grad, weights.astype(BF16))
                    grad_weights = tn(stack[kb, 2, part, :], grad)
                    grad_scores = (weights * (grad_weights - delta[h])).astype(BF16)
                    grad_kv[kb, 0, part, :] += nt(query, grad_scores)
                    grad_query[part, :] += nn(keys, grad_scores)

            return unused

        lax.fori_loop(0, count, one_key, 0)
        out_query[r] = (grad_query[...] * SCALE).astype(BF16)
        return unused

    lax.fori_loop(0, groups, one_block, 0)
    out_own[...] = grad_kv[:groups]
    for j in range(1, members):
        out_send[j - 1][...] = grad_kv[j * groups : (j + 1) * groups].astype(BF16)


def attend_back(active, seg_row, seg_col, parts, grads, exact, log_total, groups, members):
    unused, span, tokens = parts[0].shape
    heads = span // HEAD_DIM
    count = groups * members
    kv_shape = (groups, 2, span, tokens)
    return pl.pallas_call(
        functools.partial(attend_back_body, groups, members, heads),
        out_shape=[
            jax.ShapeDtypeStruct((groups, span, tokens), BF16),
            jax.ShapeDtypeStruct(kv_shape, F32),
        ]
        + [jax.ShapeDtypeStruct(kv_shape, BF16)] * (members - 1),
        in_specs=[SMEM_SPEC, resident(seg_row.shape), resident(seg_col.shape)]
        + [ANY_SPEC] * count
        + [resident((span, tokens))] * groups
        + [resident(exact.shape), resident(log_total.shape)],
        out_specs=[resident((groups, span, tokens)), resident(kv_shape)]
        + [resident(kv_shape)] * (members - 1),
        grid=(1,),
        scratch_shapes=[
            pltpu.VMEM((count, 3, span, tokens), BF16),
            pltpu.VMEM((groups, span, tokens), BF16),
            pltpu.VMEM((heads, 1, tokens), F32),
            pltpu.VMEM((span, tokens), F32),
            pltpu.VMEM((count, 2, span, tokens), F32),
            pltpu.SemaphoreType.DMA((count,)),
        ],
        compiler_params=params(),
        cost_estimate=pl.CostEstimate(
            flops=5 * span * groups * count * tokens * tokens,
            bytes_accessed=20 * span * tokens * count,
            transcendentals=heads * groups * count * tokens * tokens // 2,
        ),
        name="attend_back",
    )(active, seg_row, seg_col, *parts, *grads, exact, log_total)


OUT_BIAS, ATT_GAIN, ATT_SHIFT, DOWN_BIAS, FEED_GAIN, FEED_SHIFT = range(6)
SMALL_ROWS, SMALL_UP, SMALL_PROJECT = 16, 8, 12


def normalized(rows):
    centre = rows - jnp.mean(rows, axis=-1, keepdims=True)
    spread = jnp.mean(centre * centre, axis=-1, keepdims=True)
    inverse = lax.rsqrt(spread + EPSILON)
    return centre * inverse, inverse


def norm_back(grad, gain, normal, inverse):
    scaled = grad * gain
    mean_scaled = jnp.mean(scaled, axis=-1, keepdims=True)
    mean_both = jnp.mean(scaled * normal, axis=-1, keepdims=True)
    return inverse * (scaled - mean_scaled - normal * mean_both)


def feed_body(
    groups, span, blocks, pieces, depth, order, x_ref, wo_ref, wu_ref, wd_ref, vec, ub_ref, *rest
):
    contexts, rest = rest[:groups], rest[groups:]
    sum_first, hidden_low, sum_second, out, hidden, outward, down = rest
    j = pl.program_id(0)

    @pl.when(j == 0)
    def _():
        rows = x_ref[...] + vec[OUT_BIAS : OUT_BIAS + 1, :]
        for r in range(groups):
            start = pl.multiple_of(order[r] * span, span)
            rows += tn(contexts[r][...], wo_ref[pl.ds(start, span), :])
        sum_first[...] = rows
        normal, unused = normalized(rows)
        value = normal * vec[ATT_GAIN : ATT_GAIN + 1, :] + vec[ATT_SHIFT : ATT_SHIFT + 1, :]
        hidden[...] = value
        hidden_low[...] = value.astype(BF16)
        outward[...] = jnp.zeros_like(outward)

    inner = nn(hidden_low[...], wu_ref[...]) + ub_ref[0]
    activated = (0.5 * inner * (1.0 + lax.erf(inner * RSQRT2))).astype(BF16)
    load_down(down, wd_ref, pieces, depth)
    outward[...] += nn(activated, down[...])

    @pl.when(j == blocks - 1)
    def _():
        rows = hidden[...] + outward[...] + vec[DOWN_BIAS : DOWN_BIAS + 1, :]
        sum_second[...] = rows
        normal, unused = normalized(rows)
        out[...] = normal * vec[FEED_GAIN : FEED_GAIN + 1, :] + vec[FEED_SHIFT : FEED_SHIFT + 1, :]


def feed(order, rows, w_output, w_up, w_down, vectors, up_bias, contexts):
    (w_output, at_output), (w_up, at_up), (w_down, pieces, depth) = w_output, w_up, w_down
    tokens, width = rows.shape
    groups, span = len(contexts), contexts[0].shape[0]
    blocks = up_bias.shape[0]
    full = jax.ShapeDtypeStruct((tokens, width), F32)
    return pl.pallas_call(
        functools.partial(feed_body, groups, span, blocks, pieces, depth),
        out_shape=[full, jax.ShapeDtypeStruct((tokens, width), BF16), full, full],
        grid=(blocks,),
        in_specs=[
            SMEM_SPEC,
            resident((tokens, width)),
            column_spec(width, at_output, 0),
            column_spec(width, at_up),
            down_spec(width, pieces),
            resident(vectors.shape),
            pl.BlockSpec((1, 1, width), lambda j: (j, 0, 0)),
        ]
        + [resident((span, tokens))] * groups,
        out_specs=[resident((tokens, width))] * 4,
        scratch_shapes=[pltpu.VMEM((tokens, width), F32)] * 2 + [pltpu.VMEM((width, width), BF16)],
        compiler_params=params(),
        cost_estimate=pl.CostEstimate(
            flops=(4 * blocks + 2) * tokens * width * width,
            bytes_accessed=(4 * blocks + 2) * width * width,
            transcendentals=0,
        ),
        name="feed",
    )(order, rows, w_output, w_up, w_down, vectors, up_bias, *contexts)


def feed_back_body(
    groups,
    span,
    blocks,
    devices,
    pieces,
    depth,
    order,
    grad_ref,
    first_ref,
    second_ref,
    low_ref,
    *rest
):
    wo_ref, wu_ref, wd_ref, vec, ub_ref = rest[:5]
    contexts, rest = rest[5 : 5 + groups], rest[5 + groups :]
    shares, grad_first, small = rest[:3]
    grad_contexts, rest = rest[3 : 3 + groups], rest[3 + groups :]
    grad_out, grad_hidden, tile, down = rest
    width = vec.shape[-1]
    j = pl.program_id(0)
    share = width // devices
    down_share = blocks * share
    per_block = width // down_share

    @pl.when(j == 0)
    def _():
        small[...] = jnp.zeros_like(small)
        grad = grad_ref[...]
        normal, inverse = normalized(second_ref[...])
        value = norm_back(grad, vec[FEED_GAIN : FEED_GAIN + 1, :], normal, inverse)
        grad_hidden[...] = value
        low = value.astype(BF16)
        grad_out[...] = low
        small[DOWN_BIAS : DOWN_BIAS + 1, :] = jnp.sum(low.astype(F32), axis=0, keepdims=True)
        small[FEED_GAIN : FEED_GAIN + 1, :] = jnp.sum(grad * normal, axis=0, keepdims=True)
        small[FEED_SHIFT : FEED_SHIFT + 1, :] = jnp.sum(grad, axis=0, keepdims=True)

    inner = nn(low_ref[...], wu_ref[...]) + ub_ref[0]
    below = 0.5 * (1.0 + lax.erf(inner * RSQRT2))
    activated = (inner * below).astype(BF16)
    slope = below + inner * (PDF_SCALE * jnp.exp(-0.5 * inner * inner))
    load_down(down, wd_ref, pieces, depth)
    grad_inner = (nt(grad_out[...], down[...]) * slope).astype(BF16)
    small[pl.ds(SMALL_UP + j, 1), :] = jnp.sum(grad_inner.astype(F32), axis=0, keepdims=True)
    grad_hidden[...] += nt(grad_inner, wu_ref[...])

    product = tn(activated, grad_out[...]).astype(BF16)
    for k in range(per_block):
        shares[j * per_block + k, pl.ds(0, down_share), :] = product[
            k * down_share : (k + 1) * down_share, :
        ]
    product = tn(low_ref[...], grad_inner).astype(BF16)
    base = pl.multiple_of(down_share + j * share, share)
    for i in range(devices):
        shares[i, pl.ds(base, share), :] = product[i * share : (i + 1) * share, :]

    @pl.when(j == blocks - 1)
    def _():
        grad = grad_hidden[...]
        normal, inverse = normalized(first_ref[...])
        value = norm_back(grad, vec[ATT_GAIN : ATT_GAIN + 1, :], normal, inverse)
        grad_first[...] = value
        low = value.astype(BF16)
        small[OUT_BIAS : OUT_BIAS + 1, :] = jnp.sum(low.astype(F32), axis=0, keepdims=True)
        small[ATT_GAIN : ATT_GAIN + 1, :] = jnp.sum(grad * normal, axis=0, keepdims=True)
        small[ATT_SHIFT : ATT_SHIFT + 1, :] = jnp.sum(grad, axis=0, keepdims=True)
        for r in range(groups):
            start = pl.multiple_of(order[r] * span, span)
            tile[pl.ds(start, span), :] = nn(contexts[r][...], low).astype(BF16)
            grad_contexts[r][...] = nt(wo_ref[pl.ds(start, span), :], low).astype(BF16)
        last = down_share + blocks * share
        for i in range(devices):
            shares[i, last : last + share, :] = tile[i * share : (i + 1) * share, :]


def feed_back(
    order, grad, first, second, low, w_output, w_up, w_down, vectors, up_bias, contexts, devices
):
    (w_output, at_output), (w_up, at_up), (w_down, pieces, depth) = w_output, w_up, w_down
    tokens, width = grad.shape
    groups, span = len(contexts), contexts[0].shape[0]
    blocks = up_bias.shape[0]
    share = width // devices
    kept = (devices, (2 * blocks + 1) * share, width)
    return pl.pallas_call(
        functools.partial(feed_back_body, groups, span, blocks, devices, pieces, depth),
        out_shape=[
            jax.ShapeDtypeStruct(kept, BF16),
            jax.ShapeDtypeStruct((tokens, width), F32),
            jax.ShapeDtypeStruct((SMALL_ROWS, width), F32),
        ]
        + [jax.ShapeDtypeStruct((span, tokens), BF16)] * groups,
        grid=(blocks,),
        in_specs=[SMEM_SPEC]
        + [resident((tokens, width))] * 4
        + [
            column_spec(width, at_output, 0),
            column_spec(width, at_up),
            down_spec(width, pieces),
            resident(vectors.shape),
            pl.BlockSpec((1, 1, width), lambda j: (j, 0, 0)),
        ]
        + [resident((span, tokens))] * groups,
        out_specs=[resident(kept), resident((tokens, width)), resident((SMALL_ROWS, width))]
        + [resident((span, tokens))] * groups,
        scratch_shapes=[
            pltpu.VMEM((tokens, width), BF16),
            pltpu.VMEM((tokens, width), F32),
            pltpu.VMEM((width, width), BF16),
            pltpu.VMEM((width, width), BF16),
        ],
        compiler_params=params(),
        cost_estimate=pl.CostEstimate(
            flops=(10 * blocks + 4) * tokens * width * width,
            bytes_accessed=(8 * blocks + 4) * width * width,
            transcendentals=0,
        ),
        name="feed_back",
    )(
        order,
        grad,
        first,
        second,
        low,
        w_output,
        w_up,
        w_down,
        vectors,
        up_bias,
        *contexts,
    )


def project_back_body(groups, span, devices, order, place, x_ref, grad_ref, w_ref, small_ref, *rest):
    pieces, rest = rest[:groups], rest[groups:]
    own, send, out, small, joined, tile = rest
    width = out.shape[1]
    me = place[0]
    j = pl.program_id(0)
    share = width // devices

    @pl.when(j == 0)
    def _():
        out[...] = grad_ref[...]
        small[...] = small_ref[...]

    for r in range(groups):
        start = pl.multiple_of(order[r] * span, span)
        joined[pl.ds(start, span), :] = pieces[r][0]
    grad = joined[...].T
    small[pl.ds(SMALL_PROJECT + j, 1), :] = jnp.sum(grad.astype(F32), axis=0, keepdims=True)
    out[...] += nt(grad, w_ref[...])
    tile[...] = tn(x_ref[...].astype(BF16), grad).astype(BF16)
    for i in range(devices // 2):
        for bit, target in ((0, own), (1, send)):
            start = pl.multiple_of((me ^ (2 * i + bit)) * share, share)
            base = pl.multiple_of(j * share, share)
            target[i, pl.ds(base, share), :] = tile[pl.ds(start, share), :]

    @pl.when(j == 2)
    def _():
        rows = jnp.concatenate([small[...], jnp.zeros_like(small)], axis=0).astype(BF16)
        for i in range(devices // 2):
            for target in (own, send):
                target[i, 3 * share :, :] = rows


def project_back(order, place, rows, grad, weight, small, pieces, devices):
    weight, first = weight
    tokens, width = rows.shape
    groups, span = len(pieces), pieces[0].shape[1]
    kept = (devices // 2, 3 * (width // devices) + 2 * SMALL_ROWS, width)
    return pl.pallas_call(
        functools.partial(project_back_body, groups, span, devices),
        out_shape=[
            jax.ShapeDtypeStruct(kept, BF16),
            jax.ShapeDtypeStruct(kept, BF16),
            jax.ShapeDtypeStruct((tokens, width), F32),
        ],
        grid=(3,),
        in_specs=[
            SMEM_SPEC,
            SMEM_SPEC,
            resident((tokens, width)),
            resident((tokens, width)),
            column_spec(width, first),
            resident((SMALL_ROWS, width)),
        ]
        + [pl.BlockSpec((1, span, tokens), lambda j: (j, 0, 0))] * groups,
        out_specs=[resident(kept), resident(kept), resident((tokens, width))],
        scratch_shapes=[
            pltpu.VMEM((SMALL_ROWS, width), F32),
            pltpu.VMEM((width, tokens), BF16),
            pltpu.VMEM((width, width), BF16),
        ],
        compiler_params=params(),
        cost_estimate=pl.CostEstimate(
            flops=12 * tokens * width * width, bytes_accessed=12 * width * width, transcendentals=0
        ),
        name="project_back",
    )(order, place, rows, grad, weight, small, *pieces)


class Stream:
    def __init__(self, steps):
        self.steps, self.result, self.flying = steps, None, None
        self.resume(None)

    def resume(self, arrived):
        try:
            self.flying = self.steps.send(arrived)
        except StopIteration as stop:
            self.flying, self.result = None, stop.value


def tick(streams, values=()):
    streams = [item for item in streams if item.flying is not None]
    values, flying = lax.optimization_barrier((values, [item.flying for item in streams]))
    for item, arrived in zip(streams, flying):
        item.resume(arrived)
    return values


def sum_steps(own, send, devices, dp_size, dp_me):
    (arrived,) = yield [exchange(send, "seq", devices, 1)]
    rows, width = own.shape[1:]
    cut = rows // 2
    bits = int(math.log2(devices)) - 1
    masks = [2 << b for b in range(bits)]
    orders = (masks, masks[::-1])
    axes = [masks[::-1], masks[::-1]]
    kept = [
        add_low(own[:, part], arrived[:, part]).reshape((2,) * bits + (-1, width))
        for part in (slice(0, cut), slice(cut, rows))
    ]
    for step in range(bits):
        stay, leave = [], []
        for k in range(2):
            mask = orders[k][step]
            at = axes[k].index(mask)
            axes[k] = [m for m in axes[k] if m != mask]
            stay.append(lax.index_in_dim(kept[k], 0, at, keepdims=False))
            leave.append(
                exchange(lax.index_in_dim(kept[k], 1, at, keepdims=False), "seq", devices, mask)
            )
        leave = yield leave
        kept = [add_low(a, b) for a, b in zip(stay, leave)]
    total = jnp.concatenate(kept, axis=0)
    return (yield from dp_steps(total, dp_size, dp_me))


def dp_steps(total, dp_size, dp_me):
    rows, width = total.shape
    if dp_size != 4:
        return lax.psum(total, "dp")
    bits = [(dp_me >> b) & 1 for b in range(2)]
    for b in range(2):
        halves = total.reshape(2, -1, width)
        leave = lax.dynamic_index_in_dim(halves, 1 - bits[b], 0, keepdims=False)
        (arrived,) = yield [exchange(leave, "dp", dp_size, 1 << b)]
        total = add_low(lax.dynamic_index_in_dim(halves, bits[b], 0, keepdims=False), arrived)
    for b in (1, 0):
        (arrived,) = yield [exchange(total, "dp", dp_size, 1 << b)]
        flip = bits[b] != 0
        pair = [jnp.where(flip, arrived, total), jnp.where(flip, total, arrived)]
        total = jnp.concatenate(pair, axis=0)
    return total


def in_order(stack, place):
    for bit in (1, 2):
        flip = (place & bit) != 0
        stack = [jnp.where(flip, stack[i ^ bit], stack[i]) for i in range(4)]
    return stack


def add_low(a, b):
    return (a.astype(F32) + b.astype(F32)).astype(BF16)


def per_device(
    seq_size,
    dp_size,
    states,
    segment_ids,
    project_weight,
    query_bias,
    value_bias,
    output_weight,
    output_bias,
    attention_gain,
    attention_shift,
    up_weight,
    up_bias,
    down_weight,
    down_bias,
    feed_gain,
    feed_shift,
    cotangent,
):
    unused, tokens, width = states.shape
    groups = math.gcd(HEADS, seq_size)
    members = seq_size // groups
    share = width // seq_size
    inner_width = up_weight.shape[2]
    blocks = inner_width // width
    depth = width // (seq_size * dp_size)
    everyone = seq_size * dp_size
    me = lax.axis_index("seq")
    dp_me = lax.axis_index("dp")
    order = (me // members) ^ jnp.arange(groups, dtype=jnp.int32)
    place = me.reshape(1).astype(jnp.int32)
    both = ("dp", "seq")
    def lines(value):
        return jnp.pad(value, ((0, 0), (0, 128 - value.shape[1])))

    id_rows = -(-tokens // 128)
    shards = [
        output_bias,
        attention_gain,
        attention_shift,
        down_bias,
        feed_gain,
        feed_shift,
        query_bias,
        value_bias,
        up_bias,
    ]
    extra_rows = LAYERS * 9 + id_rows
    plain = depth % 8 != 0 or dp_size != 4 or extra_rows > depth

    def swap_groups(items):
        return [items[0]] + [
            exchange(items[r], "seq", seq_size, r * members) for r in range(1, groups)
        ]

    def with_members(items):
        items = list(items)
        own = list(items)
        for j in range(1, members):
            items += [exchange(item, "seq", seq_size, j) for item in own]
        return items

    def gathered(shard):
        return lax.all_gather(shard, both, axis=0, tiled=True)

    def over_dp(shard):
        return [exchange(shard, "dp", dp_size, m) for m in range(1, dp_size)]

    def over_seq(shard, arrived):
        stack = jnp.stack(in_order([shard] + list(arrived), dp_me))
        return lax.all_gather(stack, "seq", axis=1, tiled=True).reshape(width, -1)

    def rest_shard(layer):
        down = down_weight[layer].reshape(blocks, depth, width)
        return [down[t] for t in range(blocks)] + [up_weight[layer], output_weight[layer]]

    def rest_of(whole):
        return (whole, 2 * blocks), (whole, blocks), (whole, blocks, depth)

    if plain:
        ids = jnp.pad(segment_ids.astype(BF16), ((0, 0), (0, id_rows * 128 - tokens)))
        extra = [lines(item) for item in shards] + [ids.reshape(id_rows, 128)]
        extra = jnp.concatenate(extra, axis=0)
        table = lax.all_gather(extra, both, axis=0, tiled=False)
        w_project = [(gathered(project_weight[layer]), 0) for layer in range(LAYERS)]
        w_rest = [
            (
                (gathered(output_weight[layer]), 0),
                (gathered(up_weight[layer]), 0),
                (gathered(down_weight[layer]), 1, depth),
            )
            for layer in range(LAYERS)
        ]
    else:
        starting = pack(project_weight, shards + [segment_ids])
        shards = []
        for layer in range(LAYERS):
            parts = rest_shard(layer)
            if layer + 1 < LAYERS:
                parts.append(project_weight[layer + 1])
            shards.append(jnp.concatenate(parts, axis=1))
        arrived, shards[0] = lax.optimization_barrier((over_dp(starting), shards[0]))
        ahead = over_dp(shards[0])
        whole = over_seq(starting, arrived)
        table = whole[:, 3 * width :].reshape(everyone, depth, 128)
        w_project, w_rest = [(whole, 0)], []

    vectors = (
        table[:, : LAYERS * 8, :depth]
        .transpose(1, 0, 2)
        .reshape(8, LAYERS, width)
        .transpose(1, 0, 2)
        .astype(F32)
    )
    up_biases = (
        table[:, LAYERS * 8 : LAYERS * 9, : inner_width // everyone]
        .transpose(1, 0, 2)
        .reshape(LAYERS, blocks, 1, width)
        .astype(F32)
    )
    ids = table[:, LAYERS * 9 : LAYERS * 9 + id_rows].reshape(everyone, -1)[:, :tokens]
    relative = jnp.array([r * members + j for j in range(members) for r in range(groups)], jnp.int32)
    segments = jnp.take(ids, dp_me * seq_size + (me ^ relative), axis=0).astype(jnp.int32)
    first_id, last_id = segments[:, 0], segments[:, -1]
    active = (
        (first_id[:groups, None] <= last_id[None, :])
        & (first_id[None, :] <= last_id[:groups, None])
    ).astype(jnp.int32)
    seg_row = segments[:groups, None, :]
    seg_col = segments[:, :, None]

    def projected(layer, current):
        vec = vectors[layer]
        bias = jnp.stack([vec[6], jnp.zeros_like(vec[6]), vec[7]])[:, None, :]
        return project(order, current, w_project[layer], bias, groups)

    current = states[0].astype(F32)
    saved = []
    for layer in range(LAYERS):
        if not plain:
            whole = after if layer else over_seq(shards[0], ahead)
            w_rest.append(rest_of(whole))
            w_project.append((whole, 2 * blocks + 1))
        made = projected(layer, current)
        parts = tuple(with_members(swap_groups(made)))
        if not plain and layer + 1 < LAYERS:
            parts, shards[layer + 1] = lax.optimization_barrier((parts, shards[layer + 1]))
            ahead = over_dp(shards[layer + 1])
        *mixed, exact, log_total = attend(active, seg_row, seg_col, parts, groups, members)
        contexts = swap_groups(mixed)
        if not plain and layer + 1 < LAYERS:
            contexts, ahead = lax.optimization_barrier((contexts, ahead))
            after = over_seq(shards[layer + 1], ahead)
        w_output, w_up, w_down = w_rest[layer]
        sum_first, low, sum_second, following = feed(
            order,
            current,
            w_output,
            w_up,
            w_down,
            vectors[layer],
            up_biases[layer],
            contexts,
        )
        saved.append((current, parts, exact, log_total, contexts, sum_first, low, sum_second))
        current = following
    output = current.astype(BF16)[None]

    grad = cotangent[0].astype(F32)
    shares, feeds, backs = [None] * LAYERS, [None] * LAYERS, [None] * LAYERS
    behind = []
    for layer in reversed(range(LAYERS)):
        w_output, w_up, w_down = w_rest[layer]
        entered, parts, exact, log_total, contexts, sum_first, low, sum_second = saved[layer]
        terms, grad_first, small, *grad_mixed = feed_back(
            order,
            grad,
            sum_first,
            sum_second,
            low,
            w_output,
            w_up,
            w_down,
            vectors[layer],
            up_biases[layer],
            contexts,
            seq_size,
        )
        shares[layer] = lax.psum_scatter(
            terms.reshape(-1, width), "seq", scatter_dimension=0, tiled=True
        )
        grad_mixed = tick(behind, tuple(grad_mixed))
        grads = tuple(swap_groups(grad_mixed))
        grads = tick(behind, grads)
        if layer + 1 < LAYERS:
            grads, later = lax.optimization_barrier((grads, shares[layer + 1]))
            feeds[layer + 1] = Stream(dp_steps(later, dp_size, dp_me))
            behind = behind + [feeds[layer + 1]]
        grad_query, kept_kv, *sent_kv = attend_back(
            active, seg_row, seg_col, parts, grads, exact, log_total, groups, members
        )
        for j in range(1, members):
            kept_kv = kept_kv + exchange(sent_kv[j - 1], "seq", seq_size, j).astype(F32)
        messages = tuple(
            jnp.concatenate([grad_query[r][None], kept_kv[r].astype(BF16)], axis=0)
            for r in range(groups)
        )
        messages = tick(behind, messages)
        pieces = tuple(swap_groups(messages))
        pieces = tick(behind, pieces)
        own, send, grad = project_back(
            order, place, entered, grad_first, w_project[layer], small, pieces, seq_size
        )
        if layer + 1 < LAYERS:
            own, send = tick(behind, (own, send))
        backs[layer] = Stream(sum_steps(own, send, seq_size, dp_size, dp_me))
        behind = behind + [backs[layer]]
    tick(behind)
    tick(behind)
    feeds[0] = Stream(dp_steps(shares[0], dp_size, dp_me))
    behind = behind + [feeds[0]]
    while any(item.flying is not None for item in behind):
        tick(behind)
    small = jnp.stack(
        [backs[layer].result[3 * share : 3 * share + SMALL_ROWS] for layer in range(LAYERS)]
    ).astype(F32)
    results = [(feeds[layer].result, backs[layer].result) for layer in range(LAYERS)]

    def mine(rows, size):
        return lax.dynamic_slice_in_dim(rows, me * size, size, axis=1)

    def columns(part, which):
        return jnp.concatenate([part[i * share : (i + 1) * share] for i in which], axis=1).astype(F32)

    down_rows = blocks * share
    g_project = jnp.stack([columns(item[1], range(3)) for item in results])
    g_up = jnp.stack([columns(item[0], range(blocks, 2 * blocks)) for item in results])
    g_down = jnp.stack([item[0][:down_rows].astype(F32) for item in results])
    g_output = jnp.stack([item[0][down_rows + blocks * share :].astype(F32) for item in results])
    wide = small[:, SMALL_UP : SMALL_UP + blocks].reshape(LAYERS, blocks * width)
    return (
        output,
        grad[None],
        g_project,
        mine(small[:, SMALL_PROJECT], share),
        mine(small[:, SMALL_PROJECT + 2], share),
        g_output,
        mine(small[:, OUT_BIAS], share),
        mine(small[:, ATT_GAIN], share),
        mine(small[:, ATT_SHIFT], share),
        g_up,
        mine(wide, blocks * share),
        g_down,
        mine(small[:, DOWN_BIAS], share),
        mine(small[:, FEED_GAIN], share),
        mine(small[:, FEED_SHIFT], share),
    )


def solution(mesh):
    row, spread = P("dp", "seq", None), ("dp", "seq")
    matrix, vector = P(None, spread, None), P(None, spread)
    in_specs = (
        row,
        P("dp", "seq"),
        matrix,
        vector,
        vector,
        matrix,
        vector,
        vector,
        vector,
        matrix,
        vector,
        matrix,
        vector,
        vector,
        vector,
        row,
    )
    kept, line = P(None, "seq", None), P(None, "seq")
    out_specs = (row, row, kept, line, line, kept, line, line, line, kept, line, kept, line, line, line)
    return jax.shard_map(
        functools.partial(per_device, mesh.shape["seq"], mesh.shape["dp"]),
        mesh=mesh,
        in_specs=in_specs,
        out_specs=out_specs,
        check_vma=False,
    )
```

```python
import functools
import math

import jax
import jax.numpy as jnp
from jax import lax
from jax.experimental import pallas as pl
from jax.experimental.pallas import tpu as pltpu
from jax.sharding import PartitionSpec as P

HEADS = 12
HEAD_DIM = 64
LAYERS = 2
EPSILON = 1e-12
MASKED = -2.0e9
LOWEST = -1.0e9
SCALE = HEAD_DIM**-0.5
BF16 = jnp.bfloat16
F32 = jnp.float32
VMEM_LIMIT = 58 * 1024 * 1024
RSQRT2 = 0.7071067811865476
PDF_SCALE = 0.3989422804014327


def nn(a, b):
    return lax.dot_general(a, b, (((1,), (0,)), ((), ())), preferred_element_type=F32)


def nt(a, b):
    return lax.dot_general(a, b, (((1,), (1,)), ((), ())), preferred_element_type=F32)


def tn(a, b):
    return lax.dot_general(a, b, (((0,), (0,)), ((), ())), preferred_element_type=F32)


def exchange(value, axis, size, mask):
    return lax.ppermute(value, axis, [(i, i ^ mask) for i in range(size)])


def resident(shape):
    return pl.BlockSpec(shape, lambda *unused: (0,) * len(shape))


def column_spec(width, first, step=1):
    return pl.BlockSpec((width, width), lambda j: (0, first + step * j))


def down_spec(width, pieces):
    return pl.BlockSpec((width // pieces, pieces * width), lambda j: (j, 0))


def load_down(target, block, pieces, depth):
    if pieces == 1:
        target[...] = block[...]
        return
    width = target.shape[1]
    rows = block[...].astype(F32)
    parts = [
        rows[d * depth : (d + 1) * depth, t * width : (t + 1) * width]
        for d in range(rows.shape[0] // depth)
        for t in range(pieces)
    ]
    target[...] = jnp.concatenate(parts, axis=0).astype(BF16)


def params(count=1):
    return pltpu.CompilerParams(
        dimension_semantics=("arbitrary",) * count, vmem_limit_bytes=VMEM_LIMIT
    )


SMEM_SPEC = pl.BlockSpec(memory_space=pltpu.SMEM)
ANY_SPEC = pl.BlockSpec(memory_space=pl.ANY)


def pack_body(weight, *rest):
    items, (out, extra) = rest[:-2], rest[-2:]
    width = weight.shape[2]
    extra[...] = jnp.zeros_like(extra)
    at = 0
    for item in items:
        rows = item[...].astype(F32)
        for first in range(0, rows.shape[1], 128):
            part = rows[:, first : first + 128]
            extra[at : at + part.shape[0], : part.shape[1]] = part
            at += part.shape[0]
    out[:, :width] = weight[0]
    out[:, width:] = extra[...].astype(BF16)


def pack(weights, items):
    depth, width = weights.shape[1:]
    return pl.pallas_call(
        pack_body,
        out_shape=jax.ShapeDtypeStruct((depth, width + 128), BF16),
        grid=(1,),
        in_specs=[pl.BlockSpec((1, depth, width), lambda j: (0, 0, 0))]
        + [resident(item.shape) for item in items],
        out_specs=resident((depth, width + 128)),
        scratch_shapes=[pltpu.VMEM((depth, 128), F32)],
        compiler_params=params(),
        name="pack",
    )(weights, *items)


def project_body(groups, span, order, x_ref, w_ref, b_ref, *rest):
    outs, flipped = rest[:groups], rest[groups]
    rows = nn(x_ref[...].astype(BF16), w_ref[...]) + b_ref[0]
    flipped[...] = rows.T.astype(BF16)
    for r in range(groups):
        start = pl.multiple_of(order[r] * span, span)
        outs[r][0] = flipped[pl.ds(start, span), :]


def project(order, rows, weight, bias, groups):
    weight, first = weight
    tokens, width = rows.shape
    span = width // groups
    return pl.pallas_call(
        functools.partial(project_body, groups, span),
        out_shape=[jax.ShapeDtypeStruct((3, span, tokens), BF16)] * groups,
        grid=(3,),
        in_specs=[
            SMEM_SPEC,
            resident((tokens, width)),
            column_spec(width, first),
            pl.BlockSpec((1, 1, width), lambda j: (j, 0, 0)),
        ],
        out_specs=[pl.BlockSpec((1, span, tokens), lambda j: (j, 0, 0))] * groups,
        scratch_shapes=[pltpu.VMEM((width, tokens), BF16)],
        compiler_params=params(),
        cost_estimate=pl.CostEstimate(
            flops=6 * tokens * width * width, bytes_accessed=6 * width * width, transcendentals=0
        ),
        name="project",
    )(order, rows, weight, bias)


def load_stack(parts, stack, sems):
    copies = [pltpu.make_async_copy(part, stack.at[i], sems.at[i]) for i, part in enumerate(parts)]
    for copy in copies:
        copy.start()
    for copy in copies:
        copy.wait()


def attend_body(groups, members, heads, active, seg_row, seg_col, *rest):
    count = groups * members
    parts, rest = rest[:count], rest[count:]
    outs, rest = rest[:groups], rest[groups:]
    exact, log_total, stack, top, total, gathered, sems = rest
    load_stack(parts, stack, sems)
    tokens = stack.shape[-1]

    def one_block(r, unused):
        seg_query = seg_row[r]
        top[...] = jnp.full_like(top, LOWEST)
        total[...] = jnp.zeros_like(total)
        gathered[...] = jnp.zeros_like(gathered)

        def one_key(kb, unused):
            @pl.when(active[r, kb] != 0)
            def _():
                allowed = jnp.broadcast_to(seg_col[kb], (tokens, tokens)) == seg_query
                for h in range(heads):
                    part = pl.ds(h * HEAD_DIM, HEAD_DIM)
                    query = stack[r, 0, part, :] * SCALE
                    scores = tn(stack[kb, 1, part, :], query.astype(BF16))
                    scores = jnp.where(allowed, scores, MASKED)
                    old = top[h]
                    new = jnp.maximum(old, jnp.max(scores, axis=0, keepdims=True))
                    weights = jnp.exp(scores - new)
                    fade = jnp.exp(old - new)
                    total[h] = total[h] * fade + jnp.sum(weights, axis=0, keepdims=True)
                    top[h] = new
                    gathered[h] = gathered[h] * fade + nn(
                        stack[kb, 2, part, :], weights.astype(BF16)
                    )

            return unused

        lax.fori_loop(0, count, one_key, 0)
        for h in range(heads):
            exact[r, pl.ds(h * HEAD_DIM, HEAD_DIM), :] = gathered[h] / total[h]
            log_total[r, h] = top[h] + jnp.log(total[h])
        return unused

    lax.fori_loop(0, groups, one_block, 0)
    for r in range(groups):
        outs[r][...] = exact[r].astype(BF16)


def attend(active, seg_row, seg_col, parts, groups, members):
    unused, span, tokens = parts[0].shape
    heads = span // HEAD_DIM
    count = groups * members
    return pl.pallas_call(
        functools.partial(attend_body, groups, members, heads),
        out_shape=[jax.ShapeDtypeStruct((span, tokens), BF16)] * groups
        + [
            jax.ShapeDtypeStruct((groups, span, tokens), F32),
            jax.ShapeDtypeStruct((groups, heads, 1, tokens), F32),
        ],
        in_specs=[SMEM_SPEC, resident(seg_row.shape), resident(seg_col.shape)]
        + [ANY_SPEC] * count,
        out_specs=[resident((span, tokens))] * groups
        + [resident((groups, span, tokens)), resident((groups, heads, 1, tokens))],
        grid=(1,),
        scratch_shapes=[
            pltpu.VMEM((count, 3, span, tokens), BF16),
            pltpu.VMEM((heads, 1, tokens), F32),
            pltpu.VMEM((heads, 1, tokens), F32),
            pltpu.VMEM((heads, HEAD_DIM, tokens), F32),
            pltpu.SemaphoreType.DMA((count,)),
        ],
        compiler_params=params(),
        cost_estimate=pl.CostEstimate(
            flops=2 * span * groups * count * tokens * tokens,
            bytes_accessed=10 * span * tokens * count,
            transcendentals=heads * groups * count * tokens * tokens // 2,
        ),
        name="attend",
    )(active, seg_row, seg_col, *parts)


def attend_back_body(groups, members, heads, active, seg_row, seg_col, *rest):
    count = groups * members
    parts, rest = rest[:count], rest[count:]
    grads, rest = rest[:groups], rest[groups:]
    exact, log_total, rest = rest[0], rest[1], rest[2:]
    out_query, out_own, rest = rest[0], rest[1], rest[2:]
    out_send, rest = rest[: members - 1], rest[members - 1 :]
    stack, grad_stack, delta, grad_query, grad_kv, sems = rest
    load_stack(parts, stack, sems)
    tokens = stack.shape[-1]
    for r in range(groups):
        grad_stack[r] = grads[r][...]
    grad_kv[...] = jnp.zeros_like(grad_kv)

    def one_block(r, unused):
        seg_query = seg_row[r]
        grad_query[...] = jnp.zeros_like(grad_query)
        for h in range(heads):
            part = pl.ds(h * HEAD_DIM, HEAD_DIM)
            delta[h] = jnp.sum(
                grad_stack[r, part, :].astype(F32) * exact[r, part, :], axis=0, keepdims=True
            )

        def one_key(kb, unused):
            @pl.when(active[r, kb] != 0)
            def _():
                allowed = jnp.broadcast_to(seg_col[kb], (tokens, tokens)) == seg_query
                for h in range(heads):
                    part = pl.ds(h * HEAD_DIM, HEAD_DIM)
                    query = (stack[r, 0, part, :] * SCALE).astype(BF16)
                    grad = grad_stack[r, part, :]
                    keys = stack[kb, 1, part, :]
                    scores = jnp.where(allowed, tn(keys, query), MASKED)
                    weights = jnp.exp(scores - log_total[r, h])
                    grad_kv[kb, 1, part, :] += nt(grad, weights.astype(BF16))
                    grad_weights = tn(stack[kb, 2, part, :], grad)
                    grad_scores = (weights * (grad_weights - delta[h])).astype(BF16)
                    grad_kv[kb, 0, part, :] += nt(query, grad_scores)
                    grad_query[part, :] += nn(keys, grad_scores)

            return unused

        lax.fori_loop(0, count, one_key, 0)
        out_query[r] = (grad_query[...] * SCALE).astype(BF16)
        return unused

    lax.fori_loop(0, groups, one_block, 0)
    out_own[...] = grad_kv[:groups]
    for j in range(1, members):
        out_send[j - 1][...] = grad_kv[j * groups : (j + 1) * groups].astype(BF16)


def attend_back(active, seg_row, seg_col, parts, grads, exact, log_total, groups, members):
    unused, span, tokens = parts[0].shape
    heads = span // HEAD_DIM
    count = groups * members
    kv_shape = (groups, 2, span, tokens)
    return pl.pallas_call(
        functools.partial(attend_back_body, groups, members, heads),
        out_shape=[
            jax.ShapeDtypeStruct((groups, span, tokens), BF16),
            jax.ShapeDtypeStruct(kv_shape, F32),
        ]
        + [jax.ShapeDtypeStruct(kv_shape, BF16)] * (members - 1),
        in_specs=[SMEM_SPEC, resident(seg_row.shape), resident(seg_col.shape)]
        + [ANY_SPEC] * count
        + [resident((span, tokens))] * groups
        + [resident(exact.shape), resident(log_total.shape)],
        out_specs=[resident((groups, span, tokens)), resident(kv_shape)]
        + [resident(kv_shape)] * (members - 1),
        grid=(1,),
        scratch_shapes=[
            pltpu.VMEM((count, 3, span, tokens), BF16),
            pltpu.VMEM((groups, span, tokens), BF16),
            pltpu.VMEM((heads, 1, tokens), F32),
            pltpu.VMEM((span, tokens), F32),
            pltpu.VMEM((count, 2, span, tokens), F32),
            pltpu.SemaphoreType.DMA((count,)),
        ],
        compiler_params=params(),
        cost_estimate=pl.CostEstimate(
            flops=5 * span * groups * count * tokens * tokens,
            bytes_accessed=20 * span * tokens * count,
            transcendentals=heads * groups * count * tokens * tokens // 2,
        ),
        name="attend_back",
    )(active, seg_row, seg_col, *parts, *grads, exact, log_total)


OUT_BIAS, ATT_GAIN, ATT_SHIFT, DOWN_BIAS, FEED_GAIN, FEED_SHIFT = range(6)
SMALL_ROWS, SMALL_UP, SMALL_PROJECT = 16, 8, 12


def normalized(rows):
    centre = rows - jnp.mean(rows, axis=-1, keepdims=True)
    spread = jnp.mean(centre * centre, axis=-1, keepdims=True)
    inverse = lax.rsqrt(spread + EPSILON)
    return centre * inverse, inverse


def norm_back(grad, gain, normal, inverse):
    scaled = grad * gain
    mean_scaled = jnp.mean(scaled, axis=-1, keepdims=True)
    mean_both = jnp.mean(scaled * normal, axis=-1, keepdims=True)
    return inverse * (scaled - mean_scaled - normal * mean_both)


def feed_body(
    groups, span, blocks, pieces, depth, order, x_ref, wo_ref, wu_ref, wd_ref, vec, ub_ref, *rest
):
    contexts, rest = rest[:groups], rest[groups:]
    sum_first, hidden_low, sum_second, out, hidden, outward, down = rest
    j = pl.program_id(0)

    @pl.when(j == 0)
    def _():
        rows = x_ref[...] + vec[OUT_BIAS : OUT_BIAS + 1, :]
        for r in range(groups):
            start = pl.multiple_of(order[r] * span, span)
            rows += tn(contexts[r][...], wo_ref[pl.ds(start, span), :])
        sum_first[...] = rows
        normal, unused = normalized(rows)
        value = normal * vec[ATT_GAIN : ATT_GAIN + 1, :] + vec[ATT_SHIFT : ATT_SHIFT + 1, :]
        hidden[...] = value
        hidden_low[...] = value.astype(BF16)
        outward[...] = jnp.zeros_like(outward)

    inner = nn(hidden_low[...], wu_ref[...]) + ub_ref[0]
    activated = (0.5 * inner * (1.0 + lax.erf(inner * RSQRT2))).astype(BF16)
    load_down(down, wd_ref, pieces, depth)
    outward[...] += nn(activated, down[...])

    @pl.when(j == blocks - 1)
    def _():
        rows = hidden[...] + outward[...] + vec[DOWN_BIAS : DOWN_BIAS + 1, :]
        sum_second[...] = rows
        normal, unused = normalized(rows)
        out[...] = normal * vec[FEED_GAIN : FEED_GAIN + 1, :] + vec[FEED_SHIFT : FEED_SHIFT + 1, :]


def feed(order, rows, w_output, w_up, w_down, vectors, up_bias, contexts):
    (w_output, at_output), (w_up, at_up), (w_down, pieces, depth) = w_output, w_up, w_down
    tokens, width = rows.shape
    groups, span = len(contexts), contexts[0].shape[0]
    blocks = up_bias.shape[0]
    full = jax.ShapeDtypeStruct((tokens, width), F32)
    return pl.pallas_call(
        functools.partial(feed_body, groups, span, blocks, pieces, depth),
        out_shape=[full, jax.ShapeDtypeStruct((tokens, width), BF16), full, full],
        grid=(blocks,),
        in_specs=[
            SMEM_SPEC,
            resident((tokens, width)),
            column_spec(width, at_output, 0),
            column_spec(width, at_up),
            down_spec(width, pieces),
            resident(vectors.shape),
            pl.BlockSpec((1, 1, width), lambda j: (j, 0, 0)),
        ]
        + [resident((span, tokens))] * groups,
        out_specs=[resident((tokens, width))] * 4,
        scratch_shapes=[pltpu.VMEM((tokens, width), F32)] * 2 + [pltpu.VMEM((width, width), BF16)],
        compiler_params=params(),
        cost_estimate=pl.CostEstimate(
            flops=(4 * blocks + 2) * tokens * width * width,
            bytes_accessed=(4 * blocks + 2) * width * width,
            transcendentals=0,
        ),
        name="feed",
    )(order, rows, w_output, w_up, w_down, vectors, up_bias, *contexts)


def feed_back_body(
    groups,
    span,
    blocks,
    devices,
    pieces,
    depth,
    order,
    grad_ref,
    first_ref,
    second_ref,
    low_ref,
    *rest
):
    wo_ref, wu_ref, wd_ref, vec, ub_ref = rest[:5]
    contexts, rest = rest[5 : 5 + groups], rest[5 + groups :]
    shares, grad_first, small = rest[:3]
    grad_contexts, rest = rest[3 : 3 + groups], rest[3 + groups :]
    grad_out, grad_hidden, tile, down = rest
    width = vec.shape[-1]
    j = pl.program_id(0)
    share = width // devices
    down_share = blocks * share
    per_block = width // down_share

    @pl.when(j == 0)
    def _():
        small[...] = jnp.zeros_like(small)
        grad = grad_ref[...]
        normal, inverse = normalized(second_ref[...])
        value = norm_back(grad, vec[FEED_GAIN : FEED_GAIN + 1, :], normal, inverse)
        grad_hidden[...] = value
        low = value.astype(BF16)
        grad_out[...] = low
        small[DOWN_BIAS : DOWN_BIAS + 1, :] = jnp.sum(low.astype(F32), axis=0, keepdims=True)
        small[FEED_GAIN : FEED_GAIN + 1, :] = jnp.sum(grad * normal, axis=0, keepdims=True)
        small[FEED_SHIFT : FEED_SHIFT + 1, :] = jnp.sum(grad, axis=0, keepdims=True)

    inner = nn(low_ref[...], wu_ref[...]) + ub_ref[0]
    below = 0.5 * (1.0 + lax.erf(inner * RSQRT2))
    activated = (inner * below).astype(BF16)
    slope = below + inner * (PDF_SCALE * jnp.exp(-0.5 * inner * inner))
    load_down(down, wd_ref, pieces, depth)
    grad_inner = (nt(grad_out[...], down[...]) * slope).astype(BF16)
    small[pl.ds(SMALL_UP + j, 1), :] = jnp.sum(grad_inner.astype(F32), axis=0, keepdims=True)
    grad_hidden[...] += nt(grad_inner, wu_ref[...])

    product = tn(activated, grad_out[...]).astype(BF16)
    for k in range(per_block):
        shares[j * per_block + k, pl.ds(0, down_share), :] = product[
            k * down_share : (k + 1) * down_share, :
        ]
    product = tn(low_ref[...], grad_inner).astype(BF16)
    base = pl.multiple_of(down_share + j * share, share)
    for i in range(devices):
        shares[i, pl.ds(base, share), :] = product[i * share : (i + 1) * share, :]

    @pl.when(j == blocks - 1)
    def _():
        grad = grad_hidden[...]
        normal, inverse = normalized(first_ref[...])
        value = norm_back(grad, vec[ATT_GAIN : ATT_GAIN + 1, :], normal, inverse)
        grad_first[...] = value
        low = value.astype(BF16)
        small[OUT_BIAS : OUT_BIAS + 1, :] = jnp.sum(low.astype(F32), axis=0, keepdims=True)
        small[ATT_GAIN : ATT_GAIN + 1, :] = jnp.sum(grad * normal, axis=0, keepdims=True)
        small[ATT_SHIFT : ATT_SHIFT + 1, :] = jnp.sum(grad, axis=0, keepdims=True)
        for r in range(groups):
            start = pl.multiple_of(order[r] * span, span)
            tile[pl.ds(start, span), :] = nn(contexts[r][...], low).astype(BF16)
            grad_contexts[r][...] = nt(wo_ref[pl.ds(start, span), :], low).astype(BF16)
        last = down_share + blocks * share
        for i in range(devices):
            shares[i, last : last + share, :] = tile[i * share : (i + 1) * share, :]


def feed_back(
    order, grad, first, second, low, w_output, w_up, w_down, vectors, up_bias, contexts, devices
):
    (w_output, at_output), (w_up, at_up), (w_down, pieces, depth) = w_output, w_up, w_down
    tokens, width = grad.shape
    groups, span = len(contexts), contexts[0].shape[0]
    blocks = up_bias.shape[0]
    share = width // devices
    kept = (devices, (2 * blocks + 1) * share, width)
    return pl.pallas_call(
        functools.partial(feed_back_body, groups, span, blocks, devices, pieces, depth),
        out_shape=[
            jax.ShapeDtypeStruct(kept, BF16),
            jax.ShapeDtypeStruct((tokens, width), F32),
            jax.ShapeDtypeStruct((SMALL_ROWS, width), F32),
        ]
        + [jax.ShapeDtypeStruct((span, tokens), BF16)] * groups,
        grid=(blocks,),
        in_specs=[SMEM_SPEC]
        + [resident((tokens, width))] * 4
        + [
            column_spec(width, at_output, 0),
            column_spec(width, at_up),
            down_spec(width, pieces),
            resident(vectors.shape),
            pl.BlockSpec((1, 1, width), lambda j: (j, 0, 0)),
        ]
        + [resident((span, tokens))] * groups,
        out_specs=[resident(kept), resident((tokens, width)), resident((SMALL_ROWS, width))]
        + [resident((span, tokens))] * groups,
        scratch_shapes=[
            pltpu.VMEM((tokens, width), BF16),
            pltpu.VMEM((tokens, width), F32),
            pltpu.VMEM((width, width), BF16),
            pltpu.VMEM((width, width), BF16),
        ],
        compiler_params=params(),
        cost_estimate=pl.CostEstimate(
            flops=(10 * blocks + 4) * tokens * width * width,
            bytes_accessed=(8 * blocks + 4) * width * width,
            transcendentals=0,
        ),
        name="feed_back",
    )(
        order,
        grad,
        first,
        second,
        low,
        w_output,
        w_up,
        w_down,
        vectors,
        up_bias,
        *contexts,
    )


def project_back_body(groups, span, devices, order, place, x_ref, grad_ref, w_ref, small_ref, *rest):
    pieces, rest = rest[:groups], rest[groups:]
    own, send, out, small, joined, tile = rest
    width = out.shape[1]
    me = place[0]
    j = pl.program_id(0)
    share = width // devices

    @pl.when(j == 0)
    def _():
        out[...] = grad_ref[...]
        small[...] = small_ref[...]

    for r in range(groups):
        start = pl.multiple_of(order[r] * span, span)
        joined[pl.ds(start, span), :] = pieces[r][0]
    grad = joined[...].T
    small[pl.ds(SMALL_PROJECT + j, 1), :] = jnp.sum(grad.astype(F32), axis=0, keepdims=True)
    out[...] += nt(grad, w_ref[...])
    tile[...] = tn(x_ref[...].astype(BF16), grad).astype(BF16)
    for i in range(devices // 2):
        for bit, target in ((0, own), (1, send)):
            start = pl.multiple_of((me ^ (2 * i + bit)) * share, share)
            base = pl.multiple_of(j * share, share)
            target[i, pl.ds(base, share), :] = tile[pl.ds(start, share), :]

    @pl.when(j == 2)
    def _():
        rows = jnp.concatenate([small[...], jnp.zeros_like(small)], axis=0).astype(BF16)
        for i in range(devices // 2):
            for target in (own, send):
                target[i, 3 * share :, :] = rows


def project_back(order, place, rows, grad, weight, small, pieces, devices):
    weight, first = weight
    tokens, width = rows.shape
    groups, span = len(pieces), pieces[0].shape[1]
    kept = (devices // 2, 3 * (width // devices) + 2 * SMALL_ROWS, width)
    return pl.pallas_call(
        functools.partial(project_back_body, groups, span, devices),
        out_shape=[
            jax.ShapeDtypeStruct(kept, BF16),
            jax.ShapeDtypeStruct(kept, BF16),
            jax.ShapeDtypeStruct((tokens, width), F32),
        ],
        grid=(3,),
        in_specs=[
            SMEM_SPEC,
            SMEM_SPEC,
            resident((tokens, width)),
            resident((tokens, width)),
            column_spec(width, first),
            resident((SMALL_ROWS, width)),
        ]
        + [pl.BlockSpec((1, span, tokens), lambda j: (j, 0, 0))] * groups,
        out_specs=[resident(kept), resident(kept), resident((tokens, width))],
        scratch_shapes=[
            pltpu.VMEM((SMALL_ROWS, width), F32),
            pltpu.VMEM((width, tokens), BF16),
            pltpu.VMEM((width, width), BF16),
        ],
        compiler_params=params(),
        cost_estimate=pl.CostEstimate(
            flops=12 * tokens * width * width, bytes_accessed=12 * width * width, transcendentals=0
        ),
        name="project_back",
    )(order, place, rows, grad, weight, small, *pieces)


class Stream:
    def __init__(self, steps):
        self.steps, self.result, self.flying = steps, None, None
        self.resume(None)

    def resume(self, arrived):
        try:
            self.flying = self.steps.send(arrived)
        except StopIteration as stop:
            self.flying, self.result = None, stop.value


def tick(streams, values=()):
    streams = [item for item in streams if item.flying is not None]
    values, flying = lax.optimization_barrier((values, [item.flying for item in streams]))
    for item, arrived in zip(streams, flying):
        item.resume(arrived)
    return values


def sum_steps(own, send, devices, dp_size, dp_me):
    (arrived,) = yield [exchange(send, "seq", devices, 1)]
    rows, width = own.shape[1:]
    cut = rows // 2
    bits = int(math.log2(devices)) - 1
    masks = [2 << b for b in range(bits)]
    orders = (masks, masks[::-1])
    axes = [masks[::-1], masks[::-1]]
    kept = [
        add_low(own[:, part], arrived[:, part]).reshape((2,) * bits + (-1, width))
        for part in (slice(0, cut), slice(cut, rows))
    ]
    for step in range(bits):
        stay, leave = [], []
        for k in range(2):
            mask = orders[k][step]
            at = axes[k].index(mask)
            axes[k] = [m for m in axes[k] if m != mask]
            stay.append(lax.index_in_dim(kept[k], 0, at, keepdims=False))
            leave.append(
                exchange(lax.index_in_dim(kept[k], 1, at, keepdims=False), "seq", devices, mask)
            )
        leave = yield leave
        kept = [add_low(a, b) for a, b in zip(stay, leave)]
    total = jnp.concatenate(kept, axis=0)
    return (yield from dp_steps(total, dp_size, dp_me))


def dp_direct_steps(total, dp_size, dp_me):
    rows, width = total.shape
    if dp_size != 4:
        return lax.psum(total, "dp")
    pieces = total.reshape(dp_size, rows // dp_size, width)

    def piece(m):
        return lax.dynamic_index_in_dim(pieces, dp_me ^ m, 0, keepdims=False)

    own, *leave = yield [piece(m) for m in range(dp_size)]
    arrived = yield [exchange(leave[m - 1], "dp", dp_size, m) for m in range(1, dp_size)]
    mine = sum((item.astype(F32) for item in arrived), own.astype(F32)).astype(BF16)
    arrived = yield [exchange(mine, "dp", dp_size, m) for m in range(1, dp_size)]
    return jnp.concatenate(in_order([mine] + list(arrived), dp_me), axis=0)


def dp_steps(total, dp_size, dp_me):
    rows, width = total.shape
    if dp_size != 4:
        return lax.psum(total, "dp")
    pieces = total.reshape(dp_size, rows // dp_size, width)

    def piece(m):
        return lax.dynamic_index_in_dim(pieces, dp_me ^ m, 0, keepdims=False)

    (passing,) = yield [exchange(piece(3), "dp", dp_size, 1)]
    across = add_low(piece(2), passing)
    arrived = yield [exchange(piece(1), "dp", dp_size, 1), exchange(across, "dp", dp_size, 2)]
    mine = sum((item.astype(F32) for item in arrived), piece(0).astype(F32)).astype(BF16)
    near, far = yield [exchange(mine, "dp", dp_size, 1), exchange(mine, "dp", dp_size, 2)]
    (last,) = yield [exchange(far, "dp", dp_size, 1)]
    return jnp.concatenate(in_order([mine, near, far, last], dp_me), axis=0)


def in_order(stack, place):
    for bit in (1, 2):
        flip = (place & bit) != 0
        stack = [jnp.where(flip, stack[i ^ bit], stack[i]) for i in range(4)]
    return stack


def add_low(a, b):
    return (a.astype(F32) + b.astype(F32)).astype(BF16)


def per_device(
    seq_size,
    dp_size,
    states,
    segment_ids,
    project_weight,
    query_bias,
    value_bias,
    output_weight,
    output_bias,
    attention_gain,
    attention_shift,
    up_weight,
    up_bias,
    down_weight,
    down_bias,
    feed_gain,
    feed_shift,
    cotangent,
):
    unused, tokens, width = states.shape
    groups = math.gcd(HEADS, seq_size)
    members = seq_size // groups
    share = width // seq_size
    inner_width = up_weight.shape[2]
    blocks = inner_width // width
    depth = width // (seq_size * dp_size)
    everyone = seq_size * dp_size
    me = lax.axis_index("seq")
    dp_me = lax.axis_index("dp")
    order = (me // members) ^ jnp.arange(groups, dtype=jnp.int32)
    place = me.reshape(1).astype(jnp.int32)
    both = ("dp", "seq")
    def lines(value):
        return jnp.pad(value, ((0, 0), (0, 128 - value.shape[1])))

    id_rows = -(-tokens // 128)
    shards = [
        output_bias,
        attention_gain,
        attention_shift,
        down_bias,
        feed_gain,
        feed_shift,
        query_bias,
        value_bias,
        up_bias,
    ]
    extra_rows = LAYERS * 9 + id_rows
    plain = depth % 8 != 0 or dp_size != 4 or extra_rows > depth

    def swap_groups(items):
        return [items[0]] + [
            exchange(items[r], "seq", seq_size, r * members) for r in range(1, groups)
        ]

    def with_members(items):
        items = list(items)
        own = list(items)
        for j in range(1, members):
            items += [exchange(item, "seq", seq_size, j) for item in own]
        return items

    def gathered(shard):
        return lax.all_gather(shard, both, axis=0, tiled=True)

    def over_dp(shard, relay=True):
        near, far = (exchange(shard, "dp", dp_size, m) for m in (1, 2))
        last = exchange(far, "dp", dp_size, 1) if relay else exchange(shard, "dp", dp_size, 3)
        return [near, far, last]

    def over_seq(shard, arrived):
        stack = jnp.stack(in_order([shard] + list(arrived), dp_me))
        return lax.all_gather(stack, "seq", axis=1, tiled=True).reshape(width, -1)

    def rest_shard(layer):
        down = down_weight[layer].reshape(blocks, depth, width)
        return [down[t] for t in range(blocks)] + [up_weight[layer], output_weight[layer]]

    def rest_of(whole):
        return (whole, 2 * blocks), (whole, blocks), (whole, blocks, depth)

    if plain:
        ids = jnp.pad(segment_ids.astype(BF16), ((0, 0), (0, id_rows * 128 - tokens)))
        extra = [lines(item) for item in shards] + [ids.reshape(id_rows, 128)]
        extra = jnp.concatenate(extra, axis=0)
        table = lax.all_gather(extra, both, axis=0, tiled=False)
        w_project = [(gathered(project_weight[layer]), 0) for layer in range(LAYERS)]
        w_rest = [
            (
                (gathered(output_weight[layer]), 0),
                (gathered(up_weight[layer]), 0),
                (gathered(down_weight[layer]), 1, depth),
            )
            for layer in range(LAYERS)
        ]
    else:
        starting = pack(project_weight, shards + [segment_ids])
        shards = []
        for layer in range(LAYERS):
            parts = rest_shard(layer)
            if layer + 1 < LAYERS:
                parts.append(project_weight[layer + 1])
            shards.append(jnp.concatenate(parts, axis=1))
        arrived = over_dp(starting, relay=False)
        ahead = over_dp(shards[0])
        whole = over_seq(starting, arrived)
        table = whole[:, 3 * width :].reshape(everyone, depth, 128)
        w_project, w_rest = [(whole, 0)], []

    vectors = (
        table[:, : LAYERS * 8, :depth]
        .transpose(1, 0, 2)
        .reshape(8, LAYERS, width)
        .transpose(1, 0, 2)
        .astype(F32)
    )
    up_biases = (
        table[:, LAYERS * 8 : LAYERS * 9, : inner_width // everyone]
        .transpose(1, 0, 2)
        .reshape(LAYERS, blocks, 1, width)
        .astype(F32)
    )
    ids = table[:, LAYERS * 9 : LAYERS * 9 + id_rows].reshape(everyone, -1)[:, :tokens]
    relative = jnp.array([r * members + j for j in range(members) for r in range(groups)], jnp.int32)
    segments = jnp.take(ids, dp_me * seq_size + (me ^ relative), axis=0).astype(jnp.int32)
    first_id, last_id = segments[:, 0], segments[:, -1]
    active = (
        (first_id[:groups, None] <= last_id[None, :])
        & (first_id[None, :] <= last_id[:groups, None])
    ).astype(jnp.int32)
    seg_row = segments[:groups, None, :]
    seg_col = segments[:, :, None]

    def projected(layer, current):
        vec = vectors[layer]
        bias = jnp.stack([vec[6], jnp.zeros_like(vec[6]), vec[7]])[:, None, :]
        return project(order, current, w_project[layer], bias, groups)

    current = states[0].astype(F32)
    saved = []
    for layer in range(LAYERS):
        if not plain:
            whole = after if layer else over_seq(shards[0], ahead)
            w_rest.append(rest_of(whole))
            w_project.append((whole, 2 * blocks + 1))
        made = projected(layer, current)
        parts = tuple(with_members(swap_groups(made)))
        if not plain and layer + 1 < LAYERS:
            parts, shards[layer + 1] = lax.optimization_barrier((parts, shards[layer + 1]))
            ahead = over_dp(shards[layer + 1])
        *mixed, exact, log_total = attend(active, seg_row, seg_col, parts, groups, members)
        contexts = swap_groups(mixed)
        if not plain and layer + 1 < LAYERS:
            contexts, ahead = lax.optimization_barrier((contexts, ahead))
            after = over_seq(shards[layer + 1], ahead)
        w_output, w_up, w_down = w_rest[layer]
        sum_first, low, sum_second, following = feed(
            order,
            current,
            w_output,
            w_up,
            w_down,
            vectors[layer],
            up_biases[layer],
            contexts,
        )
        saved.append((current, parts, exact, log_total, contexts, sum_first, low, sum_second))
        current = following
    output = current.astype(BF16)[None]

    grad = cotangent[0].astype(F32)
    shares, feeds, backs = [None] * LAYERS, [None] * LAYERS, [None] * LAYERS
    behind = []
    for layer in reversed(range(LAYERS)):
        w_output, w_up, w_down = w_rest[layer]
        entered, parts, exact, log_total, contexts, sum_first, low, sum_second = saved[layer]
        terms, grad_first, small, *grad_mixed = feed_back(
            order,
            grad,
            sum_first,
            sum_second,
            low,
            w_output,
            w_up,
            w_down,
            vectors[layer],
            up_biases[layer],
            contexts,
            seq_size,
        )
        shares[layer] = lax.psum_scatter(
            terms.reshape(-1, width), "seq", scatter_dimension=0, tiled=True
        )
        grad_mixed = tick(behind, tuple(grad_mixed))
        if layer + 1 < LAYERS:
            grad_mixed, later = lax.optimization_barrier((grad_mixed, shares[layer + 1]))
            feeds[layer + 1] = Stream(dp_direct_steps(later, dp_size, dp_me))
            grad_mixed = tick([feeds[layer + 1]], grad_mixed)
            behind = behind + [feeds[layer + 1]]
        grads = tuple(swap_groups(grad_mixed))
        if layer + 1 < LAYERS:
            grads = tick([backs[layer + 1]], grads)
        made = attend_back(
            active, seg_row, seg_col, parts, grads, exact, log_total, groups, members
        )
        grad_query, kept_kv, *sent_kv = tick(behind, tuple(made))
        for j in range(1, members):
            kept_kv = kept_kv + exchange(sent_kv[j - 1], "seq", seq_size, j).astype(F32)
        messages = tuple(
            jnp.concatenate([grad_query[r][None], kept_kv[r].astype(BF16)], axis=0)
            for r in range(groups)
        )
        pieces = tuple(swap_groups(messages))
        made = project_back(
            order, place, entered, grad_first, w_project[layer], small, pieces, seq_size
        )
        own, send, grad = tick(behind, tuple(made))
        backs[layer] = Stream(sum_steps(own, send, seq_size, dp_size, dp_me))
        behind = [backs[layer]]
    last = tick(backs, shares[0])
    feeds[0] = Stream(dp_steps(last, dp_size, dp_me))
    behind = backs + feeds
    for unused in range(2):
        tick(behind)
        tick(backs)
    while any(item.flying is not None for item in behind):
        tick(behind)
    small = jnp.stack(
        [backs[layer].result[3 * share : 3 * share + SMALL_ROWS] for layer in range(LAYERS)]
    ).astype(F32)
    results = [(feeds[layer].result, backs[layer].result) for layer in range(LAYERS)]

    def mine(rows, size):
        return lax.dynamic_slice_in_dim(rows, me * size, size, axis=1)

    def columns(part, which):
        return jnp.concatenate([part[i * share : (i + 1) * share] for i in which], axis=1).astype(F32)

    down_rows = blocks * share
    g_project = jnp.stack([columns(item[1], range(3)) for item in results])
    g_up = jnp.stack([columns(item[0], range(blocks, 2 * blocks)) for item in results])
    g_down = jnp.stack([item[0][:down_rows].astype(F32) for item in results])
    g_output = jnp.stack([item[0][down_rows + blocks * share :].astype(F32) for item in results])
    wide = small[:, SMALL_UP : SMALL_UP + blocks].reshape(LAYERS, blocks * width)
    return (
        output,
        grad[None],
        g_project,
        mine(small[:, SMALL_PROJECT], share),
        mine(small[:, SMALL_PROJECT + 2], share),
        g_output,
        mine(small[:, OUT_BIAS], share),
        mine(small[:, ATT_GAIN], share),
        mine(small[:, ATT_SHIFT], share),
        g_up,
        mine(wide, blocks * share),
        g_down,
        mine(small[:, DOWN_BIAS], share),
        mine(small[:, FEED_GAIN], share),
        mine(small[:, FEED_SHIFT], share),
    )


def solution(mesh):
    row, spread = P("dp", "seq", None), ("dp", "seq")
    matrix, vector = P(None, spread, None), P(None, spread)
    in_specs = (
        row,
        P("dp", "seq"),
        matrix,
        vector,
        vector,
        matrix,
        vector,
        vector,
        vector,
        matrix,
        vector,
        matrix,
        vector,
        vector,
        vector,
        row,
    )
    kept, line = P(None, "seq", None), P(None, "seq")
    out_specs = (row, row, kept, line, line, kept, line, line, line, kept, line, kept, line, line, line)
    return jax.shard_map(
        functools.partial(per_device, mesh.shape["seq"], mesh.shape["dp"]),
        mesh=mesh,
        in_specs=in_specs,
        out_specs=out_specs,
        check_vma=False,
    )
```

```python
import functools
import math

import jax
import jax.numpy as jnp
from jax import lax
from jax.experimental import pallas as pl
from jax.experimental.pallas import tpu as pltpu
from jax.sharding import PartitionSpec as P

HEADS = 12
HEAD_DIM = 64
LAYERS = 2
EPSILON = 1e-12
MASKED = -2.0e9
LOWEST = -1.0e9
SCALE = HEAD_DIM**-0.5
BF16 = jnp.bfloat16
F32 = jnp.float32
VMEM_LIMIT = 58 * 1024 * 1024
RSQRT2 = 0.7071067811865476
PDF_SCALE = 0.3989422804014327


def nn(a, b):
    return lax.dot_general(a, b, (((1,), (0,)), ((), ())), preferred_element_type=F32)


def nt(a, b):
    return lax.dot_general(a, b, (((1,), (1,)), ((), ())), preferred_element_type=F32)


def tn(a, b):
    return lax.dot_general(a, b, (((0,), (0,)), ((), ())), preferred_element_type=F32)


def exchange(value, axis, size, mask):
    return lax.ppermute(value, axis, [(i, i ^ mask) for i in range(size)])


def resident(shape):
    return pl.BlockSpec(shape, lambda *unused: (0,) * len(shape))


def column_spec(width, first, step=1):
    return pl.BlockSpec((width, width), lambda j: (0, first + step * j))


def down_spec(width, pieces):
    return pl.BlockSpec((width // pieces, pieces * width), lambda j: (j, 0))


def load_down(target, block, pieces, depth):
    if pieces == 1:
        target[...] = block[...]
        return
    width = target.shape[1]
    rows = block[...].astype(F32)
    parts = [
        rows[d * depth : (d + 1) * depth, t * width : (t + 1) * width]
        for d in range(rows.shape[0] // depth)
        for t in range(pieces)
    ]
    target[...] = jnp.concatenate(parts, axis=0).astype(BF16)


def params(count=1):
    return pltpu.CompilerParams(
        dimension_semantics=("arbitrary",) * count, vmem_limit_bytes=VMEM_LIMIT
    )


SMEM_SPEC = pl.BlockSpec(memory_space=pltpu.SMEM)
ANY_SPEC = pl.BlockSpec(memory_space=pl.ANY)


def pack_body(weight, *rest):
    items, (out, extra) = rest[:-2], rest[-2:]
    width = weight.shape[2]
    extra[...] = jnp.zeros_like(extra)
    at = 0
    for item in items:
        rows = item[...].astype(F32)
        for first in range(0, rows.shape[1], 128):
            part = rows[:, first : first + 128]
            extra[at : at + part.shape[0], : part.shape[1]] = part
            at += part.shape[0]
    out[:, :width] = weight[0]
    out[:, width:] = extra[...].astype(BF16)


def pack(weights, items):
    depth, width = weights.shape[1:]
    return pl.pallas_call(
        pack_body,
        out_shape=jax.ShapeDtypeStruct((depth, width + 128), BF16),
        grid=(1,),
        in_specs=[pl.BlockSpec((1, depth, width), lambda j: (0, 0, 0))]
        + [resident(item.shape) for item in items],
        out_specs=resident((depth, width + 128)),
        scratch_shapes=[pltpu.VMEM((depth, 128), F32)],
        compiler_params=params(),
        name="pack",
    )(weights, *items)


def project_body(groups, span, order, x_ref, w_ref, b_ref, *rest):
    outs, flipped = rest[:groups], rest[groups]
    rows = nn(x_ref[...].astype(BF16), w_ref[...]) + b_ref[0]
    flipped[...] = rows.T.astype(BF16)
    for r in range(groups):
        start = pl.multiple_of(order[r] * span, span)
        outs[r][0] = flipped[pl.ds(start, span), :]


def project(order, rows, weight, bias, groups):
    weight, first = weight
    tokens, width = rows.shape
    span = width // groups
    return pl.pallas_call(
        functools.partial(project_body, groups, span),
        out_shape=[jax.ShapeDtypeStruct((3, span, tokens), BF16)] * groups,
        grid=(3,),
        in_specs=[
            SMEM_SPEC,
            resident((tokens, width)),
            column_spec(width, first),
            pl.BlockSpec((1, 1, width), lambda j: (j, 0, 0)),
        ],
        out_specs=[pl.BlockSpec((1, span, tokens), lambda j: (j, 0, 0))] * groups,
        scratch_shapes=[pltpu.VMEM((width, tokens), BF16)],
        compiler_params=params(),
        cost_estimate=pl.CostEstimate(
            flops=6 * tokens * width * width, bytes_accessed=6 * width * width, transcendentals=0
        ),
        name="project",
    )(order, rows, weight, bias)


def load_stack(parts, stack, sems):
    copies = [pltpu.make_async_copy(part, stack.at[i], sems.at[i]) for i, part in enumerate(parts)]
    for copy in copies:
        copy.start()
    for copy in copies:
        copy.wait()


def attend_body(groups, members, heads, active, seg_row, seg_col, *rest):
    count = groups * members
    parts, rest = rest[:count], rest[count:]
    outs, rest = rest[:groups], rest[groups:]
    exact, log_total, stack, top, total, gathered, sems = rest
    load_stack(parts, stack, sems)
    tokens = stack.shape[-1]

    def one_block(r, unused):
        seg_query = seg_row[r]
        top[...] = jnp.full_like(top, LOWEST)
        total[...] = jnp.zeros_like(total)
        gathered[...] = jnp.zeros_like(gathered)

        def one_key(kb, unused):
            @pl.when(active[r, kb] != 0)
            def _():
                allowed = jnp.broadcast_to(seg_col[kb], (tokens, tokens)) == seg_query
                for h in range(heads):
                    part = pl.ds(h * HEAD_DIM, HEAD_DIM)
                    query = stack[r, 0, part, :] * SCALE
                    scores = tn(stack[kb, 1, part, :], query.astype(BF16))
                    scores = jnp.where(allowed, scores, MASKED)
                    old = top[h]
                    new = jnp.maximum(old, jnp.max(scores, axis=0, keepdims=True))
                    weights = jnp.exp(scores - new)
                    fade = jnp.exp(old - new)
                    total[h] = total[h] * fade + jnp.sum(weights, axis=0, keepdims=True)
                    top[h] = new
                    gathered[h] = gathered[h] * fade + nn(
                        stack[kb, 2, part, :], weights.astype(BF16)
                    )

            return unused

        lax.fori_loop(0, count, one_key, 0)
        for h in range(heads):
            exact[r, pl.ds(h * HEAD_DIM, HEAD_DIM), :] = gathered[h] / total[h]
            log_total[r, h] = top[h] + jnp.log(total[h])
        return unused

    lax.fori_loop(0, groups, one_block, 0)
    for r in range(groups):
        outs[r][...] = exact[r].astype(BF16)


def attend(active, seg_row, seg_col, parts, groups, members):
    unused, span, tokens = parts[0].shape
    heads = span // HEAD_DIM
    count = groups * members
    return pl.pallas_call(
        functools.partial(attend_body, groups, members, heads),
        out_shape=[jax.ShapeDtypeStruct((span, tokens), BF16)] * groups
        + [
            jax.ShapeDtypeStruct((groups, span, tokens), F32),
            jax.ShapeDtypeStruct((groups, heads, 1, tokens), F32),
        ],
        in_specs=[SMEM_SPEC, resident(seg_row.shape), resident(seg_col.shape)]
        + [ANY_SPEC] * count,
        out_specs=[resident((span, tokens))] * groups
        + [resident((groups, span, tokens)), resident((groups, heads, 1, tokens))],
        grid=(1,),
        scratch_shapes=[
            pltpu.VMEM((count, 3, span, tokens), BF16),
            pltpu.VMEM((heads, 1, tokens), F32),
            pltpu.VMEM((heads, 1, tokens), F32),
            pltpu.VMEM((heads, HEAD_DIM, tokens), F32),
            pltpu.SemaphoreType.DMA((count,)),
        ],
        compiler_params=params(),
        cost_estimate=pl.CostEstimate(
            flops=2 * span * groups * count * tokens * tokens,
            bytes_accessed=10 * span * tokens * count,
            transcendentals=heads * groups * count * tokens * tokens // 2,
        ),
        name="attend",
    )(active, seg_row, seg_col, *parts)


def attend_back_body(groups, members, heads, active, seg_row, seg_col, *rest):
    count = groups * members
    parts, rest = rest[:count], rest[count:]
    grads, rest = rest[:groups], rest[groups:]
    exact, log_total, rest = rest[0], rest[1], rest[2:]
    out_query, out_own, rest = rest[0], rest[1], rest[2:]
    out_send, rest = rest[: members - 1], rest[members - 1 :]
    stack, grad_stack, delta, grad_query, grad_kv, sems = rest
    load_stack(parts, stack, sems)
    tokens = stack.shape[-1]
    for r in range(groups):
        grad_stack[r] = grads[r][...]
    grad_kv[...] = jnp.zeros_like(grad_kv)

    def one_block(r, unused):
        seg_query = seg_row[r]
        grad_query[...] = jnp.zeros_like(grad_query)
        for h in range(heads):
            part = pl.ds(h * HEAD_DIM, HEAD_DIM)
            delta[h] = jnp.sum(
                grad_stack[r, part, :].astype(F32) * exact[r, part, :], axis=0, keepdims=True
            )

        def one_key(kb, unused):
            @pl.when(active[r, kb] != 0)
            def _():
                allowed = jnp.broadcast_to(seg_col[kb], (tokens, tokens)) == seg_query
                for h in range(heads):
                    part = pl.ds(h * HEAD_DIM, HEAD_DIM)
                    query = (stack[r, 0, part, :] * SCALE).astype(BF16)
                    grad = grad_stack[r, part, :]
                    keys = stack[kb, 1, part, :]
                    scores = jnp.where(allowed, tn(keys, query), MASKED)
                    weights = jnp.exp(scores - log_total[r, h])
                    grad_kv[kb, 1, part, :] += nt(grad, weights.astype(BF16))
                    grad_weights = tn(stack[kb, 2, part, :], grad)
                    grad_scores = (weights * (grad_weights - delta[h])).astype(BF16)
                    grad_kv[kb, 0, part, :] += nt(query, grad_scores)
                    grad_query[part, :] += nn(keys, grad_scores)

            return unused

        lax.fori_loop(0, count, one_key, 0)
        out_query[r] = (grad_query[...] * SCALE).astype(BF16)
        return unused

    lax.fori_loop(0, groups, one_block, 0)
    out_own[...] = grad_kv[:groups]
    for j in range(1, members):
        out_send[j - 1][...] = grad_kv[j * groups : (j + 1) * groups].astype(BF16)


def attend_back(active, seg_row, seg_col, parts, grads, exact, log_total, groups, members):
    unused, span, tokens = parts[0].shape
    heads = span // HEAD_DIM
    count = groups * members
    kv_shape = (groups, 2, span, tokens)
    return pl.pallas_call(
        functools.partial(attend_back_body, groups, members, heads),
        out_shape=[
            jax.ShapeDtypeStruct((groups, span, tokens), BF16),
            jax.ShapeDtypeStruct(kv_shape, F32),
        ]
        + [jax.ShapeDtypeStruct(kv_shape, BF16)] * (members - 1),
        in_specs=[SMEM_SPEC, resident(seg_row.shape), resident(seg_col.shape)]
        + [ANY_SPEC] * count
        + [resident((span, tokens))] * groups
        + [resident(exact.shape), resident(log_total.shape)],
        out_specs=[resident((groups, span, tokens)), resident(kv_shape)]
        + [resident(kv_shape)] * (members - 1),
        grid=(1,),
        scratch_shapes=[
            pltpu.VMEM((count, 3, span, tokens), BF16),
            pltpu.VMEM((groups, span, tokens), BF16),
            pltpu.VMEM((heads, 1, tokens), F32),
            pltpu.VMEM((span, tokens), F32),
            pltpu.VMEM((count, 2, span, tokens), F32),
            pltpu.SemaphoreType.DMA((count,)),
        ],
        compiler_params=params(),
        cost_estimate=pl.CostEstimate(
            flops=5 * span * groups * count * tokens * tokens,
            bytes_accessed=20 * span * tokens * count,
            transcendentals=heads * groups * count * tokens * tokens // 2,
        ),
        name="attend_back",
    )(active, seg_row, seg_col, *parts, *grads, exact, log_total)


OUT_BIAS, ATT_GAIN, ATT_SHIFT, DOWN_BIAS, FEED_GAIN, FEED_SHIFT = range(6)
SMALL_ROWS, SMALL_UP, SMALL_PROJECT = 16, 8, 12


def normalized(rows):
    centre = rows - jnp.mean(rows, axis=-1, keepdims=True)
    spread = jnp.mean(centre * centre, axis=-1, keepdims=True)
    inverse = lax.rsqrt(spread + EPSILON)
    return centre * inverse, inverse


def norm_back(grad, gain, normal, inverse):
    scaled = grad * gain
    mean_scaled = jnp.mean(scaled, axis=-1, keepdims=True)
    mean_both = jnp.mean(scaled * normal, axis=-1, keepdims=True)
    return inverse * (scaled - mean_scaled - normal * mean_both)


def feed_body(
    groups, span, blocks, pieces, depth, order, x_ref, wo_ref, wu_ref, wd_ref, vec, ub_ref, *rest
):
    contexts, rest = rest[:groups], rest[groups:]
    sum_first, hidden_low, sum_second, out, hidden, outward, down = rest
    j = pl.program_id(0)

    @pl.when(j == 0)
    def _():
        rows = x_ref[...] + vec[OUT_BIAS : OUT_BIAS + 1, :]
        for r in range(groups):
            start = pl.multiple_of(order[r] * span, span)
            rows += tn(contexts[r][...], wo_ref[pl.ds(start, span), :])
        sum_first[...] = rows
        normal, unused = normalized(rows)
        value = normal * vec[ATT_GAIN : ATT_GAIN + 1, :] + vec[ATT_SHIFT : ATT_SHIFT + 1, :]
        hidden[...] = value
        hidden_low[...] = value.astype(BF16)
        outward[...] = jnp.zeros_like(outward)

    inner = nn(hidden_low[...], wu_ref[...]) + ub_ref[0]
    activated = (0.5 * inner * (1.0 + lax.erf(inner * RSQRT2))).astype(BF16)
    load_down(down, wd_ref, pieces, depth)
    outward[...] += nn(activated, down[...])

    @pl.when(j == blocks - 1)
    def _():
        rows = hidden[...] + outward[...] + vec[DOWN_BIAS : DOWN_BIAS + 1, :]
        sum_second[...] = rows
        normal, unused = normalized(rows)
        out[...] = normal * vec[FEED_GAIN : FEED_GAIN + 1, :] + vec[FEED_SHIFT : FEED_SHIFT + 1, :]


def feed(order, rows, w_output, w_up, w_down, vectors, up_bias, contexts):
    (w_output, at_output), (w_up, at_up), (w_down, pieces, depth) = w_output, w_up, w_down
    tokens, width = rows.shape
    groups, span = len(contexts), contexts[0].shape[0]
    blocks = up_bias.shape[0]
    full = jax.ShapeDtypeStruct((tokens, width), F32)
    return pl.pallas_call(
        functools.partial(feed_body, groups, span, blocks, pieces, depth),
        out_shape=[full, jax.ShapeDtypeStruct((tokens, width), BF16), full, full],
        grid=(blocks,),
        in_specs=[
            SMEM_SPEC,
            resident((tokens, width)),
            column_spec(width, at_output, 0),
            column_spec(width, at_up),
            down_spec(width, pieces),
            resident(vectors.shape),
            pl.BlockSpec((1, 1, width), lambda j: (j, 0, 0)),
        ]
        + [resident((span, tokens))] * groups,
        out_specs=[resident((tokens, width))] * 4,
        scratch_shapes=[pltpu.VMEM((tokens, width), F32)] * 2 + [pltpu.VMEM((width, width), BF16)],
        compiler_params=params(),
        cost_estimate=pl.CostEstimate(
            flops=(4 * blocks + 2) * tokens * width * width,
            bytes_accessed=(4 * blocks + 2) * width * width,
            transcendentals=0,
        ),
        name="feed",
    )(order, rows, w_output, w_up, w_down, vectors, up_bias, *contexts)


def feed_back_body(
    groups,
    span,
    blocks,
    devices,
    pieces,
    depth,
    apart,
    order,
    grad_ref,
    first_ref,
    second_ref,
    low_ref,
    *rest
):
    wo_ref, wu_ref, wd_ref, vec, ub_ref = rest[:5]
    contexts, rest = rest[5 : 5 + groups], rest[5 + groups :]
    shares, rest = rest[0], rest[1:]
    if apart:
        out_shares, rest = rest[0], rest[1:]
    grad_first, small = rest[:2]
    grad_contexts, rest = rest[2 : 2 + groups], rest[2 + groups :]
    grad_out, grad_hidden, tile, down = rest
    width = vec.shape[-1]
    j = pl.program_id(0)
    share = width // devices
    down_share = blocks * share
    per_block = width // down_share

    @pl.when(j == 0)
    def _():
        small[...] = jnp.zeros_like(small)
        grad = grad_ref[...]
        normal, inverse = normalized(second_ref[...])
        value = norm_back(grad, vec[FEED_GAIN : FEED_GAIN + 1, :], normal, inverse)
        grad_hidden[...] = value
        low = value.astype(BF16)
        grad_out[...] = low
        small[DOWN_BIAS : DOWN_BIAS + 1, :] = jnp.sum(low.astype(F32), axis=0, keepdims=True)
        small[FEED_GAIN : FEED_GAIN + 1, :] = jnp.sum(grad * normal, axis=0, keepdims=True)
        small[FEED_SHIFT : FEED_SHIFT + 1, :] = jnp.sum(grad, axis=0, keepdims=True)

    inner = nn(low_ref[...], wu_ref[...]) + ub_ref[0]
    below = 0.5 * (1.0 + lax.erf(inner * RSQRT2))
    activated = (inner * below).astype(BF16)
    slope = below + inner * (PDF_SCALE * jnp.exp(-0.5 * inner * inner))
    load_down(down, wd_ref, pieces, depth)
    grad_inner = (nt(grad_out[...], down[...]) * slope).astype(BF16)
    small[pl.ds(SMALL_UP + j, 1), :] = jnp.sum(grad_inner.astype(F32), axis=0, keepdims=True)
    grad_hidden[...] += nt(grad_inner, wu_ref[...])

    product = tn(activated, grad_out[...]).astype(BF16)
    for k in range(per_block):
        shares[j * per_block + k, pl.ds(0, down_share), :] = product[
            k * down_share : (k + 1) * down_share, :
        ]
    product = tn(low_ref[...], grad_inner).astype(BF16)
    base = pl.multiple_of(down_share + j * share, share)
    for i in range(devices):
        shares[i, pl.ds(base, share), :] = product[i * share : (i + 1) * share, :]

    @pl.when(j == blocks - 1)
    def _():
        grad = grad_hidden[...]
        normal, inverse = normalized(first_ref[...])
        value = norm_back(grad, vec[ATT_GAIN : ATT_GAIN + 1, :], normal, inverse)
        grad_first[...] = value
        low = value.astype(BF16)
        small[OUT_BIAS : OUT_BIAS + 1, :] = jnp.sum(low.astype(F32), axis=0, keepdims=True)
        small[ATT_GAIN : ATT_GAIN + 1, :] = jnp.sum(grad * normal, axis=0, keepdims=True)
        small[ATT_SHIFT : ATT_SHIFT + 1, :] = jnp.sum(grad, axis=0, keepdims=True)
        for r in range(groups):
            start = pl.multiple_of(order[r] * span, span)
            tile[pl.ds(start, span), :] = nn(contexts[r][...], low).astype(BF16)
            grad_contexts[r][...] = nt(wo_ref[pl.ds(start, span), :], low).astype(BF16)
        last = down_share + blocks * share
        for i in range(devices):
            rows = tile[i * share : (i + 1) * share, :]
            if apart:
                out_shares[i] = rows
            else:
                shares[i, last : last + share, :] = rows


def feed_back(
    order,
    grad,
    first,
    second,
    low,
    w_output,
    w_up,
    w_down,
    vectors,
    up_bias,
    contexts,
    devices,
    apart,
):
    (w_output, at_output), (w_up, at_up), (w_down, pieces, depth) = w_output, w_up, w_down
    tokens, width = grad.shape
    groups, span = len(contexts), contexts[0].shape[0]
    blocks = up_bias.shape[0]
    share = width // devices
    kept = [(devices, (2 * blocks + 1) * share, width)]
    if apart:
        kept = [(devices, 2 * blocks * share, width), (devices, share, width)]
    return pl.pallas_call(
        functools.partial(feed_back_body, groups, span, blocks, devices, pieces, depth, apart),
        out_shape=[jax.ShapeDtypeStruct(item, BF16) for item in kept]
        + [
            jax.ShapeDtypeStruct((tokens, width), F32),
            jax.ShapeDtypeStruct((SMALL_ROWS, width), F32),
        ]
        + [jax.ShapeDtypeStruct((span, tokens), BF16)] * groups,
        grid=(blocks,),
        in_specs=[SMEM_SPEC]
        + [resident((tokens, width))] * 4
        + [
            column_spec(width, at_output, 0),
            column_spec(width, at_up),
            down_spec(width, pieces),
            resident(vectors.shape),
            pl.BlockSpec((1, 1, width), lambda j: (j, 0, 0)),
        ]
        + [resident((span, tokens))] * groups,
        out_specs=[resident(item) for item in kept]
        + [resident((tokens, width)), resident((SMALL_ROWS, width))]
        + [resident((span, tokens))] * groups,
        scratch_shapes=[
            pltpu.VMEM((tokens, width), BF16),
            pltpu.VMEM((tokens, width), F32),
            pltpu.VMEM((width, width), BF16),
            pltpu.VMEM((width, width), BF16),
        ],
        compiler_params=params(),
        cost_estimate=pl.CostEstimate(
            flops=(10 * blocks + 4) * tokens * width * width,
            bytes_accessed=(8 * blocks + 4) * width * width,
            transcendentals=0,
        ),
        name="feed_back",
    )(
        order,
        grad,
        first,
        second,
        low,
        w_output,
        w_up,
        w_down,
        vectors,
        up_bias,
        *contexts,
    )


def project_back_body(groups, span, devices, order, place, x_ref, grad_ref, w_ref, small_ref, *rest):
    pieces, rest = rest[:groups], rest[groups:]
    own, send, out, small, joined, tile = rest
    width = out.shape[1]
    me = place[0]
    j = pl.program_id(0)
    share = width // devices

    @pl.when(j == 0)
    def _():
        out[...] = grad_ref[...]
        small[...] = small_ref[...]

    for r in range(groups):
        start = pl.multiple_of(order[r] * span, span)
        joined[pl.ds(start, span), :] = pieces[r][0]
    grad = joined[...].T
    small[pl.ds(SMALL_PROJECT + j, 1), :] = jnp.sum(grad.astype(F32), axis=0, keepdims=True)
    out[...] += nt(grad, w_ref[...])
    tile[...] = tn(x_ref[...].astype(BF16), grad).astype(BF16)
    for i in range(devices // 2):
        for bit, target in ((0, own), (1, send)):
            start = pl.multiple_of((me ^ (2 * i + bit)) * share, share)
            base = pl.multiple_of(j * share, share)
            target[i, pl.ds(base, share), :] = tile[pl.ds(start, share), :]

    @pl.when(j == 2)
    def _():
        rows = jnp.concatenate([small[...], jnp.zeros_like(small)], axis=0).astype(BF16)
        for i in range(devices // 2):
            for target in (own, send):
                target[i, 3 * share :, :] = rows


def project_back(order, place, rows, grad, weight, small, pieces, devices):
    weight, first = weight
    tokens, width = rows.shape
    groups, span = len(pieces), pieces[0].shape[1]
    kept = (devices // 2, 3 * (width // devices) + 2 * SMALL_ROWS, width)
    return pl.pallas_call(
        functools.partial(project_back_body, groups, span, devices),
        out_shape=[
            jax.ShapeDtypeStruct(kept, BF16),
            jax.ShapeDtypeStruct(kept, BF16),
            jax.ShapeDtypeStruct((tokens, width), F32),
        ],
        grid=(3,),
        in_specs=[
            SMEM_SPEC,
            SMEM_SPEC,
            resident((tokens, width)),
            resident((tokens, width)),
            column_spec(width, first),
            resident((SMALL_ROWS, width)),
        ]
        + [pl.BlockSpec((1, span, tokens), lambda j: (j, 0, 0))] * groups,
        out_specs=[resident(kept), resident(kept), resident((tokens, width))],
        scratch_shapes=[
            pltpu.VMEM((SMALL_ROWS, width), F32),
            pltpu.VMEM((width, tokens), BF16),
            pltpu.VMEM((width, width), BF16),
        ],
        compiler_params=params(),
        cost_estimate=pl.CostEstimate(
            flops=12 * tokens * width * width, bytes_accessed=12 * width * width, transcendentals=0
        ),
        name="project_back",
    )(order, place, rows, grad, weight, small, *pieces)


class Stream:
    def __init__(self, steps):
        self.steps, self.result, self.flying = steps, None, None
        self.resume(None)

    def resume(self, arrived):
        try:
            self.flying = self.steps.send(arrived)
        except StopIteration as stop:
            self.flying, self.result = None, stop.value


def tick(streams, values=()):
    streams = [item for item in streams if item.flying is not None]
    values, flying = lax.optimization_barrier((values, [item.flying for item in streams]))
    for item, arrived in zip(streams, flying):
        item.resume(arrived)
    return values


def sum_steps(own, send, devices, dp_size, dp_me):
    (arrived,) = yield [exchange(send, "seq", devices, 1)]
    rows, width = own.shape[1:]
    cut = rows // 2
    bits = int(math.log2(devices)) - 1
    masks = [2 << b for b in range(bits)]
    orders = (masks, masks[::-1])
    axes = [masks[::-1], masks[::-1]]
    kept = [
        add_low(own[:, part], arrived[:, part]).reshape((2,) * bits + (-1, width))
        for part in (slice(0, cut), slice(cut, rows))
    ]
    for step in range(bits):
        stay, leave = [], []
        for k in range(2):
            mask = orders[k][step]
            at = axes[k].index(mask)
            axes[k] = [m for m in axes[k] if m != mask]
            stay.append(lax.index_in_dim(kept[k], 0, at, keepdims=False))
            leave.append(
                exchange(lax.index_in_dim(kept[k], 1, at, keepdims=False), "seq", devices, mask)
            )
        leave = yield leave
        kept = [add_low(a, b) for a, b in zip(stay, leave)]
    total = jnp.concatenate(kept, axis=0)
    return (yield from dp_steps(total, dp_size, dp_me))


def dp_direct_steps(total, dp_size, dp_me):
    rows, width = total.shape
    if dp_size != 4:
        return lax.psum(total, "dp")
    pieces = total.reshape(dp_size, rows // dp_size, width)

    def piece(m):
        return lax.dynamic_index_in_dim(pieces, dp_me ^ m, 0, keepdims=False)

    own, *leave = yield [piece(m) for m in range(dp_size)]
    arrived = yield [exchange(leave[m - 1], "dp", dp_size, m) for m in range(1, dp_size)]
    mine = sum((item.astype(F32) for item in arrived), own.astype(F32)).astype(BF16)
    arrived = yield [exchange(mine, "dp", dp_size, m) for m in range(1, dp_size)]
    return jnp.concatenate(in_order([mine] + list(arrived), dp_me), axis=0)


def dp_steps(total, dp_size, dp_me):
    rows, width = total.shape
    if dp_size != 4:
        return lax.psum(total, "dp")
    pieces = total.reshape(dp_size, rows // dp_size, width)

    def piece(m):
        return lax.dynamic_index_in_dim(pieces, dp_me ^ m, 0, keepdims=False)

    (passing,) = yield [exchange(piece(3), "dp", dp_size, 1)]
    across = add_low(piece(2), passing)
    arrived = yield [exchange(piece(1), "dp", dp_size, 1), exchange(across, "dp", dp_size, 2)]
    mine = sum((item.astype(F32) for item in arrived), piece(0).astype(F32)).astype(BF16)
    near, far = yield [exchange(mine, "dp", dp_size, 1), exchange(mine, "dp", dp_size, 2)]
    (last,) = yield [exchange(far, "dp", dp_size, 1)]
    return jnp.concatenate(in_order([mine, near, far, last], dp_me), axis=0)


def in_order(stack, place):
    for bit in (1, 2):
        flip = (place & bit) != 0
        stack = [jnp.where(flip, stack[i ^ bit], stack[i]) for i in range(4)]
    return stack


def add_low(a, b):
    return (a.astype(F32) + b.astype(F32)).astype(BF16)


def per_device(
    seq_size,
    dp_size,
    states,
    segment_ids,
    project_weight,
    query_bias,
    value_bias,
    output_weight,
    output_bias,
    attention_gain,
    attention_shift,
    up_weight,
    up_bias,
    down_weight,
    down_bias,
    feed_gain,
    feed_shift,
    cotangent,
):
    unused, tokens, width = states.shape
    groups = math.gcd(HEADS, seq_size)
    members = seq_size // groups
    share = width // seq_size
    inner_width = up_weight.shape[2]
    blocks = inner_width // width
    depth = width // (seq_size * dp_size)
    everyone = seq_size * dp_size
    me = lax.axis_index("seq")
    dp_me = lax.axis_index("dp")
    order = (me // members) ^ jnp.arange(groups, dtype=jnp.int32)
    place = me.reshape(1).astype(jnp.int32)
    both = ("dp", "seq")
    def lines(value):
        return jnp.pad(value, ((0, 0), (0, 128 - value.shape[1])))

    id_rows = -(-tokens // 128)
    shards = [
        output_bias,
        attention_gain,
        attention_shift,
        down_bias,
        feed_gain,
        feed_shift,
        query_bias,
        value_bias,
        up_bias,
    ]
    extra_rows = LAYERS * 9 + id_rows
    plain = depth % 8 != 0 or dp_size != 4 or extra_rows > depth

    def swap_groups(items):
        return [items[0]] + [
            exchange(items[r], "seq", seq_size, r * members) for r in range(1, groups)
        ]

    def over_devices(terms):
        rows = terms.reshape(-1, width)
        return lax.psum_scatter(rows, "seq", scatter_dimension=0, tiled=True)

    def with_members(items):
        items = list(items)
        own = list(items)
        for j in range(1, members):
            items += [exchange(item, "seq", seq_size, j) for item in own]
        return items

    def gathered(shard):
        return lax.all_gather(shard, both, axis=0, tiled=True)

    def over_dp(shard, relay=True):
        near, far = (exchange(shard, "dp", dp_size, m) for m in (1, 2))
        last = exchange(far, "dp", dp_size, 1) if relay else exchange(shard, "dp", dp_size, 3)
        return [near, far, last]

    def over_seq(shard, arrived):
        stack = jnp.stack(in_order([shard] + list(arrived), dp_me))
        return lax.all_gather(stack, "seq", axis=1, tiled=True).reshape(width, -1)

    def rest_shard(layer):
        down = down_weight[layer].reshape(blocks, depth, width)
        return [down[t] for t in range(blocks)] + [up_weight[layer], output_weight[layer]]

    def rest_of(whole):
        return (whole, 2 * blocks), (whole, blocks), (whole, blocks, depth)

    if plain:
        ids = jnp.pad(segment_ids.astype(BF16), ((0, 0), (0, id_rows * 128 - tokens)))
        extra = [lines(item) for item in shards] + [ids.reshape(id_rows, 128)]
        extra = jnp.concatenate(extra, axis=0)
        table = lax.all_gather(extra, both, axis=0, tiled=False)
        w_project = [(gathered(project_weight[layer]), 0) for layer in range(LAYERS)]
        w_rest = [
            (
                (gathered(output_weight[layer]), 0),
                (gathered(up_weight[layer]), 0),
                (gathered(down_weight[layer]), 1, depth),
            )
            for layer in range(LAYERS)
        ]
    else:
        starting = pack(project_weight, shards + [segment_ids])
        shards = []
        for layer in range(LAYERS):
            parts = rest_shard(layer)
            if layer + 1 < LAYERS:
                parts.append(project_weight[layer + 1])
            shards.append(jnp.concatenate(parts, axis=1))
        arrived = over_dp(starting, relay=False)
        ahead = over_dp(shards[0])
        whole = over_seq(starting, arrived)
        table = whole[:, 3 * width :].reshape(everyone, depth, 128)
        w_project, w_rest = [(whole, 0)], []

    vectors = (
        table[:, : LAYERS * 8, :depth]
        .transpose(1, 0, 2)
        .reshape(8, LAYERS, width)
        .transpose(1, 0, 2)
        .astype(F32)
    )
    up_biases = (
        table[:, LAYERS * 8 : LAYERS * 9, : inner_width // everyone]
        .transpose(1, 0, 2)
        .reshape(LAYERS, blocks, 1, width)
        .astype(F32)
    )
    ids = table[:, LAYERS * 9 : LAYERS * 9 + id_rows].reshape(everyone, -1)[:, :tokens]
    relative = jnp.array([r * members + j for j in range(members) for r in range(groups)], jnp.int32)
    segments = jnp.take(ids, dp_me * seq_size + (me ^ relative), axis=0).astype(jnp.int32)
    first_id, last_id = segments[:, 0], segments[:, -1]
    active = (
        (first_id[:groups, None] <= last_id[None, :])
        & (first_id[None, :] <= last_id[:groups, None])
    ).astype(jnp.int32)
    seg_row = segments[:groups, None, :]
    seg_col = segments[:, :, None]

    def projected(layer, current):
        vec = vectors[layer]
        bias = jnp.stack([vec[6], jnp.zeros_like(vec[6]), vec[7]])[:, None, :]
        return project(order, current, w_project[layer], bias, groups)

    current = states[0].astype(F32)
    saved = []
    for layer in range(LAYERS):
        if not plain:
            whole = after if layer else over_seq(shards[0], ahead)
            w_rest.append(rest_of(whole))
            w_project.append((whole, 2 * blocks + 1))
        made = projected(layer, current)
        parts = tuple(with_members(swap_groups(made)))
        if not plain and layer + 1 < LAYERS:
            parts, shards[layer + 1] = lax.optimization_barrier((parts, shards[layer + 1]))
            ahead = over_dp(shards[layer + 1])
        *mixed, exact, log_total = attend(active, seg_row, seg_col, parts, groups, members)
        contexts = swap_groups(mixed)
        if not plain and layer + 1 < LAYERS:
            contexts, ahead = lax.optimization_barrier((contexts, ahead))
            after = over_seq(shards[layer + 1], ahead)
        w_output, w_up, w_down = w_rest[layer]
        sum_first, low, sum_second, following = feed(
            order,
            current,
            w_output,
            w_up,
            w_down,
            vectors[layer],
            up_biases[layer],
            contexts,
        )
        saved.append((current, parts, exact, log_total, contexts, sum_first, low, sum_second))
        current = following
    output = current.astype(BF16)[None]

    grad = cotangent[0].astype(F32)
    shares, feeds, backs = [None] * LAYERS, [None] * LAYERS, [None] * LAYERS
    behind = []
    for layer in reversed(range(LAYERS)):
        w_output, w_up, w_down = w_rest[layer]
        entered, parts, exact, log_total, contexts, sum_first, low, sum_second = saved[layer]
        terms, *made = feed_back(
            order,
            grad,
            sum_first,
            sum_second,
            low,
            w_output,
            w_up,
            w_down,
            vectors[layer],
            up_biases[layer],
            contexts,
            seq_size,
            layer == 0,
        )
        if layer == 0:
            out_terms, *made = made
        grad_first, small, *grad_mixed = made
        shares[layer] = over_devices(terms)
        grad_mixed = tick(behind, tuple(grad_mixed))
        if layer + 1 < LAYERS:
            grad_mixed, later = lax.optimization_barrier((grad_mixed, shares[layer + 1]))
            feeds[layer + 1] = Stream(dp_direct_steps(later, dp_size, dp_me))
            grad_mixed = tick([feeds[layer + 1]], grad_mixed)
            behind = behind + [feeds[layer + 1]]
        grads = tuple(swap_groups(grad_mixed))
        if layer + 1 < LAYERS:
            grads = tick([backs[layer + 1]], grads)
        if layer == 0:
            grads, out_terms = lax.optimization_barrier((grads, out_terms))
            out_share = over_devices(out_terms)
        made = attend_back(
            active, seg_row, seg_col, parts, grads, exact, log_total, groups, members
        )
        grad_query, kept_kv, *sent_kv = tick(behind, tuple(made))
        for j in range(1, members):
            kept_kv = kept_kv + exchange(sent_kv[j - 1], "seq", seq_size, j).astype(F32)
        messages = tuple(
            jnp.concatenate([grad_query[r][None], kept_kv[r].astype(BF16)], axis=0)
            for r in range(groups)
        )
        pieces = tuple(swap_groups(messages))
        if layer + 1 < LAYERS:
            pieces = tick([backs[layer + 1]], pieces)
        made = project_back(
            order, place, entered, grad_first, w_project[layer], small, pieces, seq_size
        )
        own, send, grad = tick([item for item in feeds if item is not None], tuple(made))
        backs[layer] = Stream(sum_steps(own, send, seq_size, dp_size, dp_me))
        behind = [backs[layer]]
    last = tick(backs[:1], shares[0])
    feeds[0] = Stream(dp_steps(last, dp_size, dp_me))
    behind = backs + feeds
    tick(behind)
    tick(backs)
    last = tick(behind, out_share)
    out_stream = Stream(dp_direct_steps(last, dp_size, dp_me))
    tick(backs + [out_stream])
    behind = behind + [out_stream]
    while any(item.flying is not None for item in behind):
        tick(behind)
    small = jnp.stack(
        [backs[layer].result[3 * share : 3 * share + SMALL_ROWS] for layer in range(LAYERS)]
    ).astype(F32)
    results = [(feeds[layer].result, backs[layer].result) for layer in range(LAYERS)]

    def mine(rows, size):
        return lax.dynamic_slice_in_dim(rows, me * size, size, axis=1)

    def columns(part, which):
        return jnp.concatenate([part[i * share : (i + 1) * share] for i in which], axis=1).astype(F32)

    down_rows = blocks * share
    g_project = jnp.stack([columns(item[1], range(3)) for item in results])
    g_up = jnp.stack([columns(item[0], range(blocks, 2 * blocks)) for item in results])
    g_down = jnp.stack([item[0][:down_rows].astype(F32) for item in results])
    outs = [out_stream.result] + [item[0][down_rows + blocks * share :] for item in results[1:]]
    g_output = jnp.stack(outs).astype(F32)
    wide = small[:, SMALL_UP : SMALL_UP + blocks].reshape(LAYERS, blocks * width)
    return (
        output,
        grad[None],
        g_project,
        mine(small[:, SMALL_PROJECT], share),
        mine(small[:, SMALL_PROJECT + 2], share),
        g_output,
        mine(small[:, OUT_BIAS], share),
        mine(small[:, ATT_GAIN], share),
        mine(small[:, ATT_SHIFT], share),
        g_up,
        mine(wide, blocks * share),
        g_down,
        mine(small[:, DOWN_BIAS], share),
        mine(small[:, FEED_GAIN], share),
        mine(small[:, FEED_SHIFT], share),
    )


def solution(mesh):
    row, spread = P("dp", "seq", None), ("dp", "seq")
    matrix, vector = P(None, spread, None), P(None, spread)
    in_specs = (
        row,
        P("dp", "seq"),
        matrix,
        vector,
        vector,
        matrix,
        vector,
        vector,
        vector,
        matrix,
        vector,
        matrix,
        vector,
        vector,
        vector,
        row,
    )
    kept, line = P(None, "seq", None), P(None, "seq")
    out_specs = (row, row, kept, line, line, kept, line, line, line, kept, line, kept, line, line, line)
    return jax.shard_map(
        functools.partial(per_device, mesh.shape["seq"], mesh.shape["dp"]),
        mesh=mesh,
        in_specs=in_specs,
        out_specs=out_specs,
        check_vma=False,
    )
```

```python
import functools
import math

import jax
import jax.numpy as jnp
from jax import lax
from jax.experimental import pallas as pl
from jax.experimental.pallas import tpu as pltpu
from jax.sharding import PartitionSpec as P

HEADS = 12
HEAD_DIM = 64
LAYERS = 2
EPSILON = 1e-12
MASKED = -2.0e9
LOWEST = -1.0e9
SCALE = HEAD_DIM**-0.5
BF16 = jnp.bfloat16
F32 = jnp.float32
VMEM_LIMIT = 58 * 1024 * 1024
RSQRT2 = 0.7071067811865476
PDF_SCALE = 0.3989422804014327


def nn(a, b):
    return lax.dot_general(a, b, (((1,), (0,)), ((), ())), preferred_element_type=F32)


def nt(a, b):
    return lax.dot_general(a, b, (((1,), (1,)), ((), ())), preferred_element_type=F32)


def tn(a, b):
    return lax.dot_general(a, b, (((0,), (0,)), ((), ())), preferred_element_type=F32)


def exchange(value, axis, size, mask):
    return lax.ppermute(value, axis, [(i, i ^ mask) for i in range(size)])


def resident(shape):
    return pl.BlockSpec(shape, lambda *unused: (0,) * len(shape))


def column_spec(width, first, step=1):
    return pl.BlockSpec((width, width), lambda j: (0, first + step * j))


def down_spec(width, pieces):
    return pl.BlockSpec((width // pieces, pieces * width), lambda j: (j, 0))


def load_down(target, block, pieces, depth):
    if pieces == 1:
        target[...] = block[...]
        return
    width = target.shape[1]
    rows = block[...].astype(F32)
    parts = [
        rows[d * depth : (d + 1) * depth, t * width : (t + 1) * width]
        for d in range(rows.shape[0] // depth)
        for t in range(pieces)
    ]
    target[...] = jnp.concatenate(parts, axis=0).astype(BF16)


def params(count=1):
    return pltpu.CompilerParams(
        dimension_semantics=("arbitrary",) * count, vmem_limit_bytes=VMEM_LIMIT
    )


SMEM_SPEC = pl.BlockSpec(memory_space=pltpu.SMEM)
ANY_SPEC = pl.BlockSpec(memory_space=pl.ANY)


def pack_body(weight, *rest):
    items, (out, extra) = rest[:-2], rest[-2:]
    width = weight.shape[2]
    extra[...] = jnp.zeros_like(extra)
    at = 0
    for item in items:
        rows = item[...].astype(F32)
        for first in range(0, rows.shape[1], 128):
            part = rows[:, first : first + 128]
            extra[at : at + part.shape[0], : part.shape[1]] = part
            at += part.shape[0]
    out[:, :width] = weight[0]
    out[:, width:] = extra[...].astype(BF16)


def pack(weights, items):
    depth, width = weights.shape[1:]
    return pl.pallas_call(
        pack_body,
        out_shape=jax.ShapeDtypeStruct((depth, width + 128), BF16),
        grid=(1,),
        in_specs=[pl.BlockSpec((1, depth, width), lambda j: (0, 0, 0))]
        + [resident(item.shape) for item in items],
        out_specs=resident((depth, width + 128)),
        scratch_shapes=[pltpu.VMEM((depth, 128), F32)],
        compiler_params=params(),
        name="pack",
    )(weights, *items)


def project_body(groups, span, order, x_ref, w_ref, b_ref, *rest):
    outs, flipped = rest[:groups], rest[groups]
    rows = nn(x_ref[...].astype(BF16), w_ref[...]) + b_ref[0]
    flipped[...] = rows.T.astype(BF16)
    for r in range(groups):
        start = pl.multiple_of(order[r] * span, span)
        outs[r][0] = flipped[pl.ds(start, span), :]


def project(order, rows, weight, bias, groups):
    weight, first = weight
    tokens, width = rows.shape
    span = width // groups
    return pl.pallas_call(
        functools.partial(project_body, groups, span),
        out_shape=[jax.ShapeDtypeStruct((3, span, tokens), BF16)] * groups,
        grid=(3,),
        in_specs=[
            SMEM_SPEC,
            resident((tokens, width)),
            column_spec(width, first),
            pl.BlockSpec((1, 1, width), lambda j: (j, 0, 0)),
        ],
        out_specs=[pl.BlockSpec((1, span, tokens), lambda j: (j, 0, 0))] * groups,
        scratch_shapes=[pltpu.VMEM((width, tokens), BF16)],
        compiler_params=params(),
        cost_estimate=pl.CostEstimate(
            flops=6 * tokens * width * width, bytes_accessed=6 * width * width, transcendentals=0
        ),
        name="project",
    )(order, rows, weight, bias)


def load_stack(parts, stack, sems):
    copies = [pltpu.make_async_copy(part, stack.at[i], sems.at[i]) for i, part in enumerate(parts)]
    for copy in copies:
        copy.start()
    for copy in copies:
        copy.wait()


def attend_body(groups, members, heads, active, seg_row, seg_col, *rest):
    count = groups * members
    parts, rest = rest[:count], rest[count:]
    outs, rest = rest[:groups], rest[groups:]
    exact, log_total, stack, top, total, gathered, sems = rest
    load_stack(parts, stack, sems)
    tokens = stack.shape[-1]

    def one_block(r, unused):
        seg_query = seg_row[r]
        top[...] = jnp.full_like(top, LOWEST)
        total[...] = jnp.zeros_like(total)
        gathered[...] = jnp.zeros_like(gathered)

        def one_key(kb, unused):
            @pl.when(active[r, kb] != 0)
            def _():
                allowed = jnp.broadcast_to(seg_col[kb], (tokens, tokens)) == seg_query
                for h in range(heads):
                    part = pl.ds(h * HEAD_DIM, HEAD_DIM)
                    query = stack[r, 0, part, :] * SCALE
                    scores = tn(stack[kb, 1, part, :], query.astype(BF16))
                    scores = jnp.where(allowed, scores, MASKED)
                    old = top[h]
                    new = jnp.maximum(old, jnp.max(scores, axis=0, keepdims=True))
                    weights = jnp.exp(scores - new)
                    fade = jnp.exp(old - new)
                    total[h] = total[h] * fade + jnp.sum(weights, axis=0, keepdims=True)
                    top[h] = new
                    gathered[h] = gathered[h] * fade + nn(
                        stack[kb, 2, part, :], weights.astype(BF16)
                    )

            return unused

        lax.fori_loop(0, count, one_key, 0)
        for h in range(heads):
            exact[r, pl.ds(h * HEAD_DIM, HEAD_DIM), :] = gathered[h] / total[h]
            log_total[r, h] = top[h] + jnp.log(total[h])
        return unused

    lax.fori_loop(0, groups, one_block, 0)
    for r in range(groups):
        outs[r][...] = exact[r].astype(BF16)


def attend(active, seg_row, seg_col, parts, groups, members):
    unused, span, tokens = parts[0].shape
    heads = span // HEAD_DIM
    count = groups * members
    return pl.pallas_call(
        functools.partial(attend_body, groups, members, heads),
        out_shape=[jax.ShapeDtypeStruct((span, tokens), BF16)] * groups
        + [
            jax.ShapeDtypeStruct((groups, span, tokens), F32),
            jax.ShapeDtypeStruct((groups, heads, 1, tokens), F32),
        ],
        in_specs=[SMEM_SPEC, resident(seg_row.shape), resident(seg_col.shape)]
        + [ANY_SPEC] * count,
        out_specs=[resident((span, tokens))] * groups
        + [resident((groups, span, tokens)), resident((groups, heads, 1, tokens))],
        grid=(1,),
        scratch_shapes=[
            pltpu.VMEM((count, 3, span, tokens), BF16),
            pltpu.VMEM((heads, 1, tokens), F32),
            pltpu.VMEM((heads, 1, tokens), F32),
            pltpu.VMEM((heads, HEAD_DIM, tokens), F32),
            pltpu.SemaphoreType.DMA((count,)),
        ],
        compiler_params=params(),
        cost_estimate=pl.CostEstimate(
            flops=2 * span * groups * count * tokens * tokens,
            bytes_accessed=10 * span * tokens * count,
            transcendentals=heads * groups * count * tokens * tokens // 2,
        ),
        name="attend",
    )(active, seg_row, seg_col, *parts)


def attend_back_body(groups, members, heads, active, seg_row, seg_col, *rest):
    count = groups * members
    parts, rest = rest[:count], rest[count:]
    grads, rest = rest[:groups], rest[groups:]
    exact, log_total, rest = rest[0], rest[1], rest[2:]
    out_query, out_own, rest = rest[0], rest[1], rest[2:]
    out_send, rest = rest[: members - 1], rest[members - 1 :]
    stack, grad_stack, delta, grad_query, grad_kv, sems = rest
    load_stack(parts, stack, sems)
    tokens = stack.shape[-1]
    for r in range(groups):
        grad_stack[r] = grads[r][...]
    grad_kv[...] = jnp.zeros_like(grad_kv)

    def one_block(r, unused):
        seg_query = seg_row[r]
        grad_query[...] = jnp.zeros_like(grad_query)
        for h in range(heads):
            part = pl.ds(h * HEAD_DIM, HEAD_DIM)
            delta[h] = jnp.sum(
                grad_stack[r, part, :].astype(F32) * exact[r, part, :], axis=0, keepdims=True
            )

        def one_key(kb, unused):
            @pl.when(active[r, kb] != 0)
            def _():
                allowed = jnp.broadcast_to(seg_col[kb], (tokens, tokens)) == seg_query
                for h in range(heads):
                    part = pl.ds(h * HEAD_DIM, HEAD_DIM)
                    query = (stack[r, 0, part, :] * SCALE).astype(BF16)
                    grad = grad_stack[r, part, :]
                    keys = stack[kb, 1, part, :]
                    scores = jnp.where(allowed, tn(keys, query), MASKED)
                    weights = jnp.exp(scores - log_total[r, h])
                    grad_kv[kb, 1, part, :] += nt(grad, weights.astype(BF16))
                    grad_weights = tn(stack[kb, 2, part, :], grad)
                    grad_scores = (weights * (grad_weights - delta[h])).astype(BF16)
                    grad_kv[kb, 0, part, :] += nt(query, grad_scores)
                    grad_query[part, :] += nn(keys, grad_scores)

            return unused

        lax.fori_loop(0, count, one_key, 0)
        out_query[r] = (grad_query[...] * SCALE).astype(BF16)
        return unused

    lax.fori_loop(0, groups, one_block, 0)
    out_own[...] = grad_kv[:groups]
    for j in range(1, members):
        out_send[j - 1][...] = grad_kv[j * groups : (j + 1) * groups].astype(BF16)


def attend_back(active, seg_row, seg_col, parts, grads, exact, log_total, groups, members):
    unused, span, tokens = parts[0].shape
    heads = span // HEAD_DIM
    count = groups * members
    kv_shape = (groups, 2, span, tokens)
    return pl.pallas_call(
        functools.partial(attend_back_body, groups, members, heads),
        out_shape=[
            jax.ShapeDtypeStruct((groups, span, tokens), BF16),
            jax.ShapeDtypeStruct(kv_shape, F32),
        ]
        + [jax.ShapeDtypeStruct(kv_shape, BF16)] * (members - 1),
        in_specs=[SMEM_SPEC, resident(seg_row.shape), resident(seg_col.shape)]
        + [ANY_SPEC] * count
        + [resident((span, tokens))] * groups
        + [resident(exact.shape), resident(log_total.shape)],
        out_specs=[resident((groups, span, tokens)), resident(kv_shape)]
        + [resident(kv_shape)] * (members - 1),
        grid=(1,),
        scratch_shapes=[
            pltpu.VMEM((count, 3, span, tokens), BF16),
            pltpu.VMEM((groups, span, tokens), BF16),
            pltpu.VMEM((heads, 1, tokens), F32),
            pltpu.VMEM((span, tokens), F32),
            pltpu.VMEM((count, 2, span, tokens), F32),
            pltpu.SemaphoreType.DMA((count,)),
        ],
        compiler_params=params(),
        cost_estimate=pl.CostEstimate(
            flops=5 * span * groups * count * tokens * tokens,
            bytes_accessed=20 * span * tokens * count,
            transcendentals=heads * groups * count * tokens * tokens // 2,
        ),
        name="attend_back",
    )(active, seg_row, seg_col, *parts, *grads, exact, log_total)


OUT_BIAS, ATT_GAIN, ATT_SHIFT, DOWN_BIAS, FEED_GAIN, FEED_SHIFT = range(6)
SMALL_ROWS, SMALL_UP, SMALL_PROJECT = 16, 8, 12


def normalized(rows):
    centre = rows - jnp.mean(rows, axis=-1, keepdims=True)
    spread = jnp.mean(centre * centre, axis=-1, keepdims=True)
    inverse = lax.rsqrt(spread + EPSILON)
    return centre * inverse, inverse


def norm_back(grad, gain, normal, inverse):
    scaled = grad * gain
    mean_scaled = jnp.mean(scaled, axis=-1, keepdims=True)
    mean_both = jnp.mean(scaled * normal, axis=-1, keepdims=True)
    return inverse * (scaled - mean_scaled - normal * mean_both)


def feed_body(
    groups, span, blocks, pieces, depth, order, x_ref, wo_ref, wu_ref, wd_ref, vec, ub_ref, *rest
):
    contexts, rest = rest[:groups], rest[groups:]
    sum_first, hidden_low, sum_second, out, hidden, outward, down = rest
    j = pl.program_id(0)

    @pl.when(j == 0)
    def _():
        rows = x_ref[...] + vec[OUT_BIAS : OUT_BIAS + 1, :]
        for r in range(groups):
            start = pl.multiple_of(order[r] * span, span)
            rows += tn(contexts[r][...], wo_ref[pl.ds(start, span), :])
        sum_first[...] = rows
        normal, unused = normalized(rows)
        value = normal * vec[ATT_GAIN : ATT_GAIN + 1, :] + vec[ATT_SHIFT : ATT_SHIFT + 1, :]
        hidden[...] = value
        hidden_low[...] = value.astype(BF16)
        outward[...] = jnp.zeros_like(outward)

    inner = nn(hidden_low[...], wu_ref[...]) + ub_ref[0]
    activated = (0.5 * inner * (1.0 + lax.erf(inner * RSQRT2))).astype(BF16)
    load_down(down, wd_ref, pieces, depth)
    outward[...] += nn(activated, down[...])

    @pl.when(j == blocks - 1)
    def _():
        rows = hidden[...] + outward[...] + vec[DOWN_BIAS : DOWN_BIAS + 1, :]
        sum_second[...] = rows
        normal, unused = normalized(rows)
        out[...] = normal * vec[FEED_GAIN : FEED_GAIN + 1, :] + vec[FEED_SHIFT : FEED_SHIFT + 1, :]


def feed(order, rows, w_output, w_up, w_down, vectors, up_bias, contexts):
    (w_output, at_output), (w_up, at_up), (w_down, pieces, depth) = w_output, w_up, w_down
    tokens, width = rows.shape
    groups, span = len(contexts), contexts[0].shape[0]
    blocks = up_bias.shape[0]
    full = jax.ShapeDtypeStruct((tokens, width), F32)
    return pl.pallas_call(
        functools.partial(feed_body, groups, span, blocks, pieces, depth),
        out_shape=[full, jax.ShapeDtypeStruct((tokens, width), BF16), full, full],
        grid=(blocks,),
        in_specs=[
            SMEM_SPEC,
            resident((tokens, width)),
            column_spec(width, at_output, 0),
            column_spec(width, at_up),
            down_spec(width, pieces),
            resident(vectors.shape),
            pl.BlockSpec((1, 1, width), lambda j: (j, 0, 0)),
        ]
        + [resident((span, tokens))] * groups,
        out_specs=[resident((tokens, width))] * 4,
        scratch_shapes=[pltpu.VMEM((tokens, width), F32)] * 2 + [pltpu.VMEM((width, width), BF16)],
        compiler_params=params(),
        cost_estimate=pl.CostEstimate(
            flops=(4 * blocks + 2) * tokens * width * width,
            bytes_accessed=(4 * blocks + 2) * width * width,
            transcendentals=0,
        ),
        name="feed",
    )(order, rows, w_output, w_up, w_down, vectors, up_bias, *contexts)


def feed_back_body(
    groups,
    span,
    blocks,
    devices,
    pieces,
    depth,
    order,
    grad_ref,
    first_ref,
    second_ref,
    low_ref,
    *rest
):
    wo_ref, wu_ref, wd_ref, vec, ub_ref = rest[:5]
    contexts, rest = rest[5 : 5 + groups], rest[5 + groups :]
    shares, grad_first, small = rest[:3]
    grad_contexts, rest = rest[3 : 3 + groups], rest[3 + groups :]
    grad_out, grad_hidden, tile, down = rest
    width = vec.shape[-1]
    j = pl.program_id(0)
    share = width // devices
    down_share = blocks * share
    per_block = width // down_share

    @pl.when(j == 0)
    def _():
        small[...] = jnp.zeros_like(small)
        grad = grad_ref[...]
        normal, inverse = normalized(second_ref[...])
        value = norm_back(grad, vec[FEED_GAIN : FEED_GAIN + 1, :], normal, inverse)
        grad_hidden[...] = value
        low = value.astype(BF16)
        grad_out[...] = low
        small[DOWN_BIAS : DOWN_BIAS + 1, :] = jnp.sum(low.astype(F32), axis=0, keepdims=True)
        small[FEED_GAIN : FEED_GAIN + 1, :] = jnp.sum(grad * normal, axis=0, keepdims=True)
        small[FEED_SHIFT : FEED_SHIFT + 1, :] = jnp.sum(grad, axis=0, keepdims=True)

    inner = nn(low_ref[...], wu_ref[...]) + ub_ref[0]
    below = 0.5 * (1.0 + lax.erf(inner * RSQRT2))
    activated = (inner * below).astype(BF16)
    slope = below + inner * (PDF_SCALE * jnp.exp(-0.5 * inner * inner))
    load_down(down, wd_ref, pieces, depth)
    grad_inner = (nt(grad_out[...], down[...]) * slope).astype(BF16)
    small[pl.ds(SMALL_UP + j, 1), :] = jnp.sum(grad_inner.astype(F32), axis=0, keepdims=True)
    grad_hidden[...] += nt(grad_inner, wu_ref[...])

    product = tn(activated, grad_out[...]).astype(BF16)
    for k in range(per_block):
        shares[j * per_block + k, pl.ds(0, down_share), :] = product[
            k * down_share : (k + 1) * down_share, :
        ]
    product = tn(low_ref[...], grad_inner).astype(BF16)
    base = pl.multiple_of(down_share + j * share, share)
    for i in range(devices):
        shares[i, pl.ds(base, share), :] = product[i * share : (i + 1) * share, :]

    @pl.when(j == blocks - 1)
    def _():
        grad = grad_hidden[...]
        normal, inverse = normalized(first_ref[...])
        value = norm_back(grad, vec[ATT_GAIN : ATT_GAIN + 1, :], normal, inverse)
        grad_first[...] = value
        low = value.astype(BF16)
        small[OUT_BIAS : OUT_BIAS + 1, :] = jnp.sum(low.astype(F32), axis=0, keepdims=True)
        small[ATT_GAIN : ATT_GAIN + 1, :] = jnp.sum(grad * normal, axis=0, keepdims=True)
        small[ATT_SHIFT : ATT_SHIFT + 1, :] = jnp.sum(grad, axis=0, keepdims=True)
        for r in range(groups):
            start = pl.multiple_of(order[r] * span, span)
            tile[pl.ds(start, span), :] = nn(contexts[r][...], low).astype(BF16)
            grad_contexts[r][...] = nt(wo_ref[pl.ds(start, span), :], low).astype(BF16)
        last = down_share + blocks * share
        for i in range(devices):
            shares[i, last : last + share, :] = tile[i * share : (i + 1) * share, :]


def feed_back(
    order, grad, first, second, low, w_output, w_up, w_down, vectors, up_bias, contexts, devices
):
    (w_output, at_output), (w_up, at_up), (w_down, pieces, depth) = w_output, w_up, w_down
    tokens, width = grad.shape
    groups, span = len(contexts), contexts[0].shape[0]
    blocks = up_bias.shape[0]
    share = width // devices
    kept = (devices, (2 * blocks + 1) * share, width)
    return pl.pallas_call(
        functools.partial(feed_back_body, groups, span, blocks, devices, pieces, depth),
        out_shape=[
            jax.ShapeDtypeStruct(kept, BF16),
            jax.ShapeDtypeStruct((tokens, width), F32),
            jax.ShapeDtypeStruct((SMALL_ROWS, width), F32),
        ]
        + [jax.ShapeDtypeStruct((span, tokens), BF16)] * groups,
        grid=(blocks,),
        in_specs=[SMEM_SPEC]
        + [resident((tokens, width))] * 4
        + [
            column_spec(width, at_output, 0),
            column_spec(width, at_up),
            down_spec(width, pieces),
            resident(vectors.shape),
            pl.BlockSpec((1, 1, width), lambda j: (j, 0, 0)),
        ]
        + [resident((span, tokens))] * groups,
        out_specs=[resident(kept), resident((tokens, width)), resident((SMALL_ROWS, width))]
        + [resident((span, tokens))] * groups,
        scratch_shapes=[
            pltpu.VMEM((tokens, width), BF16),
            pltpu.VMEM((tokens, width), F32),
            pltpu.VMEM((width, width), BF16),
            pltpu.VMEM((width, width), BF16),
        ],
        compiler_params=params(),
        cost_estimate=pl.CostEstimate(
            flops=(10 * blocks + 4) * tokens * width * width,
            bytes_accessed=(8 * blocks + 4) * width * width,
            transcendentals=0,
        ),
        name="feed_back",
    )(
        order,
        grad,
        first,
        second,
        low,
        w_output,
        w_up,
        w_down,
        vectors,
        up_bias,
        *contexts,
    )


def project_back_body(groups, span, devices, order, place, x_ref, grad_ref, w_ref, small_ref, *rest):
    pieces, rest = rest[:groups], rest[groups:]
    own, send, out, small, joined, tile = rest
    width = out.shape[1]
    me = place[0]
    j = pl.program_id(0)
    share = width // devices

    @pl.when(j == 0)
    def _():
        out[...] = grad_ref[...]
        small[...] = small_ref[...]

    for r in range(groups):
        start = pl.multiple_of(order[r] * span, span)
        joined[pl.ds(start, span), :] = pieces[r][0]
    grad = joined[...].T
    small[pl.ds(SMALL_PROJECT + j, 1), :] = jnp.sum(grad.astype(F32), axis=0, keepdims=True)
    out[...] += nt(grad, w_ref[...])
    tile[...] = tn(x_ref[...].astype(BF16), grad).astype(BF16)
    for i in range(devices // 2):
        for bit, target in ((0, own), (1, send)):
            start = pl.multiple_of((me ^ (2 * i + bit)) * share, share)
            base = pl.multiple_of(j * share, share)
            target[i, pl.ds(base, share), :] = tile[pl.ds(start, share), :]

    @pl.when(j == 2)
    def _():
        rows = jnp.concatenate([small[...], jnp.zeros_like(small)], axis=0).astype(BF16)
        for i in range(devices // 2):
            for target in (own, send):
                target[i, 3 * share :, :] = rows


def project_back(order, place, rows, grad, weight, small, pieces, devices):
    weight, first = weight
    tokens, width = rows.shape
    groups, span = len(pieces), pieces[0].shape[1]
    kept = (devices // 2, 3 * (width // devices) + 2 * SMALL_ROWS, width)
    return pl.pallas_call(
        functools.partial(project_back_body, groups, span, devices),
        out_shape=[
            jax.ShapeDtypeStruct(kept, BF16),
            jax.ShapeDtypeStruct(kept, BF16),
            jax.ShapeDtypeStruct((tokens, width), F32),
        ],
        grid=(3,),
        in_specs=[
            SMEM_SPEC,
            SMEM_SPEC,
            resident((tokens, width)),
            resident((tokens, width)),
            column_spec(width, first),
            resident((SMALL_ROWS, width)),
        ]
        + [pl.BlockSpec((1, span, tokens), lambda j: (j, 0, 0))] * groups,
        out_specs=[resident(kept), resident(kept), resident((tokens, width))],
        scratch_shapes=[
            pltpu.VMEM((SMALL_ROWS, width), F32),
            pltpu.VMEM((width, tokens), BF16),
            pltpu.VMEM((width, width), BF16),
        ],
        compiler_params=params(),
        cost_estimate=pl.CostEstimate(
            flops=12 * tokens * width * width, bytes_accessed=12 * width * width, transcendentals=0
        ),
        name="project_back",
    )(order, place, rows, grad, weight, small, *pieces)


class Stream:
    def __init__(self, steps):
        self.steps, self.result, self.flying = steps, None, None
        self.resume(None)

    def resume(self, arrived):
        try:
            self.flying = self.steps.send(arrived)
        except StopIteration as stop:
            self.flying, self.result = None, stop.value


def tick(streams, values=()):
    streams = [item for item in streams if item.flying is not None]
    values, flying = lax.optimization_barrier((values, [item.flying for item in streams]))
    for item, arrived in zip(streams, flying):
        item.resume(arrived)
    return values


def sum_steps(own, send, devices, dp_size, dp_me):
    (arrived,) = yield [exchange(send, "seq", devices, 1)]
    rows, width = own.shape[1:]
    cut = rows // 2
    bits = int(math.log2(devices)) - 1
    masks = [2 << b for b in range(bits)]
    orders = (masks, masks[::-1])
    axes = [masks[::-1], masks[::-1]]
    kept = [
        add_low(own[:, part], arrived[:, part]).reshape((2,) * bits + (-1, width))
        for part in (slice(0, cut), slice(cut, rows))
    ]
    for step in range(bits):
        stay, leave = [], []
        for k in range(2):
            mask = orders[k][step]
            at = axes[k].index(mask)
            axes[k] = [m for m in axes[k] if m != mask]
            stay.append(lax.index_in_dim(kept[k], 0, at, keepdims=False))
            leave.append(
                exchange(lax.index_in_dim(kept[k], 1, at, keepdims=False), "seq", devices, mask)
            )
        leave = yield leave
        kept = [add_low(a, b) for a, b in zip(stay, leave)]
    total = jnp.concatenate(kept, axis=0)
    return (yield from dp_steps(total, dp_size, dp_me))


def dp_direct_steps(total, dp_size, dp_me):
    rows, width = total.shape
    if dp_size != 4:
        return lax.psum(total, "dp")
    pieces = total.reshape(dp_size, rows // dp_size, width)

    def piece(m):
        return lax.dynamic_index_in_dim(pieces, dp_me ^ m, 0, keepdims=False)

    own, *leave = yield [piece(m) for m in range(dp_size)]
    arrived = yield [exchange(leave[m - 1], "dp", dp_size, m) for m in range(1, dp_size)]
    mine = sum((item.astype(F32) for item in arrived), own.astype(F32)).astype(BF16)
    arrived = yield [exchange(mine, "dp", dp_size, m) for m in range(1, dp_size)]
    return jnp.concatenate(in_order([mine] + list(arrived), dp_me), axis=0)


def dp_steps(total, dp_size, dp_me):
    rows, width = total.shape
    if dp_size != 4:
        return lax.psum(total, "dp")
    pieces = total.reshape(dp_size, rows // dp_size, width)

    def piece(m):
        return lax.dynamic_index_in_dim(pieces, dp_me ^ m, 0, keepdims=False)

    (passing,) = yield [exchange(piece(3), "dp", dp_size, 1)]
    across = add_low(piece(2), passing)
    arrived = yield [exchange(piece(1), "dp", dp_size, 1), exchange(across, "dp", dp_size, 2)]
    mine = sum((item.astype(F32) for item in arrived), piece(0).astype(F32)).astype(BF16)
    near, far = yield [exchange(mine, "dp", dp_size, 1), exchange(mine, "dp", dp_size, 2)]
    (last,) = yield [exchange(far, "dp", dp_size, 1)]
    return jnp.concatenate(in_order([mine, near, far, last], dp_me), axis=0)


def in_order(stack, place):
    for bit in (1, 2):
        flip = (place & bit) != 0
        stack = [jnp.where(flip, stack[i ^ bit], stack[i]) for i in range(4)]
    return stack


def add_low(a, b):
    return (a.astype(F32) + b.astype(F32)).astype(BF16)


def per_device(
    seq_size,
    dp_size,
    states,
    segment_ids,
    project_weight,
    query_bias,
    value_bias,
    output_weight,
    output_bias,
    attention_gain,
    attention_shift,
    up_weight,
    up_bias,
    down_weight,
    down_bias,
    feed_gain,
    feed_shift,
    cotangent,
):
    unused, tokens, width = states.shape
    groups = math.gcd(HEADS, seq_size)
    members = seq_size // groups
    share = width // seq_size
    inner_width = up_weight.shape[2]
    blocks = inner_width // width
    depth = width // (seq_size * dp_size)
    everyone = seq_size * dp_size
    me = lax.axis_index("seq")
    dp_me = lax.axis_index("dp")
    order = (me // members) ^ jnp.arange(groups, dtype=jnp.int32)
    place = me.reshape(1).astype(jnp.int32)
    both = ("dp", "seq")
    def lines(value):
        return jnp.pad(value, ((0, 0), (0, 128 - value.shape[1])))

    id_rows = -(-tokens // 128)
    shards = [
        output_bias,
        attention_gain,
        attention_shift,
        down_bias,
        feed_gain,
        feed_shift,
        query_bias,
        value_bias,
        up_bias,
    ]
    extra_rows = LAYERS * 9 + id_rows
    plain = depth % 8 != 0 or dp_size != 4 or extra_rows > depth

    def swap_groups(items):
        return [items[0]] + [
            exchange(items[r], "seq", seq_size, r * members) for r in range(1, groups)
        ]

    def with_members(items):
        items = list(items)
        own = list(items)
        for j in range(1, members):
            items += [exchange(item, "seq", seq_size, j) for item in own]
        return items

    def gathered(shard):
        return lax.all_gather(shard, both, axis=0, tiled=True)

    def over_dp(shard, relay=True):
        near, far = (exchange(shard, "dp", dp_size, m) for m in (1, 2))
        last = exchange(far, "dp", dp_size, 1) if relay else exchange(shard, "dp", dp_size, 3)
        return [near, far, last]

    def over_seq(shard, arrived):
        stack = jnp.stack(in_order([shard] + list(arrived), dp_me))
        return lax.all_gather(stack, "seq", axis=1, tiled=True).reshape(width, -1)

    def rest_shard(layer):
        down = down_weight[layer].reshape(blocks, depth, width)
        return [down[t] for t in range(blocks)] + [up_weight[layer], output_weight[layer]]

    def rest_of(whole):
        return (whole, 2 * blocks), (whole, blocks), (whole, blocks, depth)

    if plain:
        ids = jnp.pad(segment_ids.astype(BF16), ((0, 0), (0, id_rows * 128 - tokens)))
        extra = [lines(item) for item in shards] + [ids.reshape(id_rows, 128)]
        extra = jnp.concatenate(extra, axis=0)
        table = lax.all_gather(extra, both, axis=0, tiled=False)
        w_project = [(gathered(project_weight[layer]), 0) for layer in range(LAYERS)]
        w_rest = [
            (
                (gathered(output_weight[layer]), 0),
                (gathered(up_weight[layer]), 0),
                (gathered(down_weight[layer]), 1, depth),
            )
            for layer in range(LAYERS)
        ]
    else:
        starting = pack(project_weight, shards + [segment_ids])
        shards = []
        for layer in range(LAYERS):
            parts = rest_shard(layer)
            if layer + 1 < LAYERS:
                parts.append(project_weight[layer + 1])
            shards.append(jnp.concatenate(parts, axis=1))
        arrived = over_dp(starting, relay=False)
        ahead = over_dp(shards[0])
        whole = over_seq(starting, arrived)
        table = whole[:, 3 * width :].reshape(everyone, depth, 128)
        w_project, w_rest = [(whole, 0)], []

    vectors = (
        table[:, : LAYERS * 8, :depth]
        .transpose(1, 0, 2)
        .reshape(8, LAYERS, width)
        .transpose(1, 0, 2)
        .astype(F32)
    )
    up_biases = (
        table[:, LAYERS * 8 : LAYERS * 9, : inner_width // everyone]
        .transpose(1, 0, 2)
        .reshape(LAYERS, blocks, 1, width)
        .astype(F32)
    )
    ids = table[:, LAYERS * 9 : LAYERS * 9 + id_rows].reshape(everyone, -1)[:, :tokens]
    relative = jnp.array([r * members + j for j in range(members) for r in range(groups)], jnp.int32)
    segments = jnp.take(ids, dp_me * seq_size + (me ^ relative), axis=0).astype(jnp.int32)
    first_id, last_id = segments[:, 0], segments[:, -1]
    active = (
        (first_id[:groups, None] <= last_id[None, :])
        & (first_id[None, :] <= last_id[:groups, None])
    ).astype(jnp.int32)
    seg_row = segments[:groups, None, :]
    seg_col = segments[:, :, None]

    def projected(layer, current):
        vec = vectors[layer]
        bias = jnp.stack([vec[6], jnp.zeros_like(vec[6]), vec[7]])[:, None, :]
        return project(order, current, w_project[layer], bias, groups)

    current = states[0].astype(F32)
    saved = []
    for layer in range(LAYERS):
        if not plain:
            whole = after if layer else over_seq(shards[0], ahead)
            w_rest.append(rest_of(whole))
            w_project.append((whole, 2 * blocks + 1))
        made = projected(layer, current)
        parts = tuple(with_members(swap_groups(made)))
        if not plain and layer + 1 < LAYERS:
            parts, shards[layer + 1] = lax.optimization_barrier((parts, shards[layer + 1]))
            ahead = over_dp(shards[layer + 1])
        *mixed, exact, log_total = attend(active, seg_row, seg_col, parts, groups, members)
        contexts = swap_groups(mixed)
        if not plain and layer + 1 < LAYERS:
            contexts, ahead = lax.optimization_barrier((contexts, ahead))
            after = over_seq(shards[layer + 1], ahead)
        w_output, w_up, w_down = w_rest[layer]
        sum_first, low, sum_second, following = feed(
            order,
            current,
            w_output,
            w_up,
            w_down,
            vectors[layer],
            up_biases[layer],
            contexts,
        )
        saved.append((current, parts, exact, log_total, contexts, sum_first, low, sum_second))
        current = following
    output = current.astype(BF16)[None]

    grad = cotangent[0].astype(F32)
    shares, feeds, backs = [None] * LAYERS, [None] * LAYERS, [None] * LAYERS
    behind = []
    for layer in reversed(range(LAYERS)):
        w_output, w_up, w_down = w_rest[layer]
        entered, parts, exact, log_total, contexts, sum_first, low, sum_second = saved[layer]
        terms, grad_first, small, *grad_mixed = feed_back(
            order,
            grad,
            sum_first,
            sum_second,
            low,
            w_output,
            w_up,
            w_down,
            vectors[layer],
            up_biases[layer],
            contexts,
            seq_size,
        )
        shares[layer] = lax.psum_scatter(
            terms.reshape(-1, width), "seq", scatter_dimension=0, tiled=True
        )
        grad_mixed = tick(behind, tuple(grad_mixed))
        if layer + 1 < LAYERS:
            grad_mixed, later = lax.optimization_barrier((grad_mixed, shares[layer + 1]))
            feeds[layer + 1] = Stream(dp_direct_steps(later, dp_size, dp_me))
            grad_mixed = tick([feeds[layer + 1]], grad_mixed)
            behind = behind + [feeds[layer + 1]]
        grads = tuple(swap_groups(grad_mixed))
        if layer + 1 < LAYERS:
            grads = tick([backs[layer + 1]], grads)
        made = attend_back(
            active, seg_row, seg_col, parts, grads, exact, log_total, groups, members
        )
        grad_query, kept_kv, *sent_kv = tick(behind, tuple(made))
        for j in range(1, members):
            kept_kv = kept_kv + exchange(sent_kv[j - 1], "seq", seq_size, j).astype(F32)
        messages = tuple(
            jnp.concatenate([grad_query[r][None], kept_kv[r].astype(BF16)], axis=0)
            for r in range(groups)
        )
        pieces = tuple(swap_groups(messages))
        if layer + 1 < LAYERS:
            pieces = tick([backs[layer + 1]], pieces)
        made = project_back(
            order, place, entered, grad_first, w_project[layer], small, pieces, seq_size
        )
        own, send, grad = tick(behind, tuple(made))
        backs[layer] = Stream(sum_steps(own, send, seq_size, dp_size, dp_me))
        behind = [backs[layer]]
    last = tick(backs, shares[0])
    feeds[0] = Stream(dp_steps(last, dp_size, dp_me))
    behind = backs + feeds
    for unused in range(2):
        tick(behind)
        tick(backs)
    tick(behind)
    for items in (feeds, backs):
        while any(item.flying is not None for item in items):
            tick(items)
    small = jnp.stack(
        [backs[layer].result[3 * share : 3 * share + SMALL_ROWS] for layer in range(LAYERS)]
    ).astype(F32)
    results = [(feeds[layer].result, backs[layer].result) for layer in range(LAYERS)]

    def mine(rows, size):
        return lax.dynamic_slice_in_dim(rows, me * size, size, axis=1)

    def columns(part, which):
        return jnp.concatenate([part[i * share : (i + 1) * share] for i in which], axis=1).astype(F32)

    down_rows = blocks * share
    g_project = jnp.stack([columns(item[1], range(3)) for item in results])
    g_up = jnp.stack([columns(item[0], range(blocks, 2 * blocks)) for item in results])
    g_down = jnp.stack([item[0][:down_rows].astype(F32) for item in results])
    g_output = jnp.stack([item[0][down_rows + blocks * share :].astype(F32) for item in results])
    wide = small[:, SMALL_UP : SMALL_UP + blocks].reshape(LAYERS, blocks * width)
    return (
        output,
        grad[None],
        g_project,
        mine(small[:, SMALL_PROJECT], share),
        mine(small[:, SMALL_PROJECT + 2], share),
        g_output,
        mine(small[:, OUT_BIAS], share),
        mine(small[:, ATT_GAIN], share),
        mine(small[:, ATT_SHIFT], share),
        g_up,
        mine(wide, blocks * share),
        g_down,
        mine(small[:, DOWN_BIAS], share),
        mine(small[:, FEED_GAIN], share),
        mine(small[:, FEED_SHIFT], share),
    )


def solution(mesh):
    row, spread = P("dp", "seq", None), ("dp", "seq")
    matrix, vector = P(None, spread, None), P(None, spread)
    in_specs = (
        row,
        P("dp", "seq"),
        matrix,
        vector,
        vector,
        matrix,
        vector,
        vector,
        vector,
        matrix,
        vector,
        matrix,
        vector,
        vector,
        vector,
        row,
    )
    kept, line = P(None, "seq", None), P(None, "seq")
    out_specs = (row, row, kept, line, line, kept, line, line, line, kept, line, kept, line, line, line)
    return jax.shard_map(
        functools.partial(per_device, mesh.shape["seq"], mesh.shape["dp"]),
        mesh=mesh,
        in_specs=in_specs,
        out_specs=out_specs,
        check_vma=False,
    )
```
